32 devices in a mesh: row: 4 (over y, x), col: 8 (over z, core).
Axes of the slice: x: 2, y: 2, z: 4, core: 2. Of those that a mesh axis runs over, the one named last changes fastest.
Arguments:
- increment: float32 [4, 60, 32, 1024], P(None, None, 'row', 'col'), may hold values from -6 to 6
- residual: float32 [4, 60, 32, 1024], P(None, None, 'row', 'col'), may hold values from -6 to 6
- direction: float32 [4, 60, 32, 1024], P(None, None, 'row', 'col'), may hold values from -6 to 6
- lanczos: bfloat16 [10, 4, 60, 32, 1024], P(None, None, None, 'row', 'col'), may hold values from -10 to 10
- vertical_modes: float32 [4, 60, 60], replicated, may hold values from -0.75 to 0.75
- amplitude: float32 [4, 60], replicated, may hold values from 0.5 to 2
- length_east: float32 [4, 8], replicated, may hold values from 0.25 to 4
- length_north: float32 [4, 8], replicated, may hold values from 0.25 to 4
- observed_cell: int32 [16384], P(('row', 'col')), may hold values from 0 to 245759
- observed_weight: float32 [16384], P(('row', 'col')), may hold values from 0.5 to 4
- observed_count: int32 [32], P(('row', 'col')), may hold values from 128 to 512, as said below
Outputs:
- new_increment: float32 [4, 60, 32, 1024], P(None, None, 'row', 'col')
- new_residual: float32 [4, 60, 32, 1024], P(None, None, 'row', 'col')
- new_direction: float32 [4, 60, 32, 1024], P(None, None, 'row', 'col')
The draws below stay inside these ranges and needn't reach their ends.
Inputs may be any that keep to these rules, and one draw needn't show every extreme that they name: observed_cell[s] indexes a cell of the tile that slot s belongs to. `observed_count`: a tile has at most 512 live slots, and some tile has exactly 512.
All inputs are finite; a program needn't handle non-finite values.
Results may differ from the reference program's by a relative error of at most 0.00055.
Values sent between devices are 32-bit elements; how exact they have to be, the bound alone decides.
A program may use at most 128 MiB of HBM per device.

```python
import math
import jax
import jax.numpy as jnp
from jax import lax

V = 4
L = 60
M = 8
K = 10
CX = 128
CY = 8
OBS_DEV = 512
NX = 1024
NY = 32
TILES = 32
NOBS = 16384
NTOT = 7864320


def shared_residual(key):
    noise_key = jax.random.fold_in(key, 11)
    return jnp.clip(jax.random.normal(noise_key, (V, L, NY, NX), jnp.float32), -6.0, 6.0)


def draw_residual(key, part):
    return shared_residual(key)


def draw_lanczos(key, part):
    base_field = shared_residual(key)
    fresh = jnp.clip(jax.random.normal(jax.random.fold_in(key, 12), (K, V, L, NY, NX), jnp.float32), -6.0, 6.0)
    mixing = 0.2 + 0.04 * jnp.arange(K, dtype=jnp.float32)
    mixed = (fresh + mixing[:, None, None, None, None] * base_field[None]) / jnp.sqrt(1.0 + mixing * mixing)[:, None, None, None, None]
    return mixed.astype(jnp.bfloat16)


def draw_observed_count(key, part):
    count_key = jax.random.fold_in(key, 21)
    place_key = jax.random.fold_in(key, 22)
    counts = jax.random.randint(count_key, (TILES,), OBS_DEV // 4, OBS_DEV + 1)
    chosen = jax.random.randint(place_key, (), 0, TILES)
    return jnp.where(jnp.arange(TILES) == chosen, OBS_DEV, counts).astype(jnp.int32)


def with_ends(values, rng, least, largest):
    place = [jax.random.randint(jax.random.fold_in(rng, axis), (), 0, length) for axis, length in enumerate(values.shape)]
    longest = values.shape.index(max(values.shape))
    next_to = place[:longest] + [(place[longest] + 1) % values.shape[longest]] + place[longest + 1:]
    return values.at[tuple(place)].set(least).at[tuple(next_to)].set(largest)


def block_scale(own_key, extent, cuts, least, largest):
    gain, own = 1.0, jax.random.fold_in(own_key, 6)
    for axis_at, blocks in cuts:
        draws = jnp.exp(jax.random.uniform(jax.random.fold_in(own, axis_at), (blocks,), jnp.float32, least / len(cuts), largest / len(cuts)))
        gain = gain * jnp.repeat(draws, extent[axis_at] // blocks).reshape([-1 if axis == axis_at else 1 for axis in range(len(extent))])
    return gain


def scatter_about(rng, shape, scale, reach, shards=(), held_as=jnp.bfloat16):
    result = scale * jax.random.normal(rng, shape, jnp.float32)
    if shards:
        result = result * block_scale(rng, shape, shards, -0.22, 0.18)
    return jnp.clip(result, -reach, reach).astype(held_as)


def setup_inputs(seed: int = 0) -> dict:
    seeds = jax.random.split(jax.random.key(seed), 12)
    increment = scatter_about(seeds[0], (V, L, NY, NX), 1.0, 6.0, ((2, 4), (3, 8)), jnp.float32)
    residual = draw_residual(jax.random.fold_in(seeds[11], 71), 0)
    direction = scatter_about(seeds[2], (V, L, NY, NX), 1.0, 6.0, ((2, 4), (3, 8)), jnp.float32)
    lanczos = draw_lanczos(jax.random.fold_in(seeds[11], 71), 0)
    vertical_modes = scatter_about(seeds[4], (V, L, L), L ** -0.5, 0.75, (), jnp.float32)
    amplitude = jnp.clip(jnp.exp(jax.random.uniform(seeds[5], (V, L), jnp.float32, math.log(0.5), math.log(2.0))), 0.5, 2.0)
    length_east = jnp.clip(jnp.exp(jax.random.uniform(seeds[6], (V, M), jnp.float32, math.log(0.25), math.log(4.0))), 0.25, 4.0)
    length_north = jnp.clip(jnp.exp(jax.random.uniform(seeds[7], (V, M), jnp.float32, math.log(0.25), math.log(4.0))), 0.25, 4.0)
    observed_cell = with_ends(jax.random.randint(seeds[8], (NOBS,), 0, V * L * CY * CX), jax.random.fold_in(seeds[8], 1), 0, (V * L * CY * CX) - 1).astype(jnp.int32)
    observed_weight = jnp.clip(jnp.exp(math.log(4.0) - 2.0794415 * jax.random.uniform(seeds[9], (NOBS,), jnp.float32) ** block_scale(seeds[9], (NOBS,), ((0, 32),), -0.2, 0.2)), 0.5, 4.0)
    observed_count = draw_observed_count(jax.random.fold_in(seeds[11], 71), 0)
    return {"increment": increment, "residual": residual, "direction": direction, "lanczos": lanczos, "vertical_modes": vertical_modes, "amplitude": amplitude, "length_east": length_east, "length_north": length_north, "observed_cell": observed_cell, "observed_weight": observed_weight, "observed_count": observed_count}


precise = lax.Precision.HIGHEST

def recursive_filter(field_in, alpha_line):
    decay = alpha_line[:, :, None]
    sequence = jnp.moveaxis(field_in, -1, 0)

    def advance(carry_in, entry):
        carry_out = decay * carry_in + (1.0 - decay) * entry
        return (carry_out, carry_out)
    first_state, smooth = lax.scan(advance, jnp.zeros_like(sequence[0]), sequence)
    second_state, settled = lax.scan(advance, jnp.zeros_like(sequence[0]), smooth, reverse=True)
    boost = jnp.sqrt((1.0 + alpha_line) / (1.0 - alpha_line))[:, :, None, None]
    return jnp.moveaxis(settled, 0, -1) * boost

def along_east(leading, alpha_east):
    return recursive_filter(leading, alpha_east)

def along_north(leading, alpha_north):
    return jnp.swapaxes(recursive_filter(jnp.swapaxes(leading, 2, 3), alpha_north), 2, 3)

def reference(increment, residual, direction, lanczos, vertical_modes, amplitude, length_east, length_north, observed_cell, observed_weight, observed_count):
    alpha_east = jnp.exp(-1.0 / (length_east * CX))
    alpha_north = jnp.exp(-1.0 / (length_north * CY))

    def forward_map(control):
        leading = along_north(along_east(control[:, :M], alpha_east), alpha_north)
        mode_field = jnp.concatenate([leading, control[:, M:]], axis=1)
        return jnp.einsum('vlm,vmyx->vlyx', vertical_modes, mode_field * amplitude[:, :, None, None], precision=precise)

    def adjoint_map(grid_field):
        mode_field = jnp.einsum('vlm,vlyx->vmyx', vertical_modes, grid_field, precision=precise) * amplitude[:, :, None, None]
        leading = along_east(along_north(mode_field[:, :M], alpha_north), alpha_east)
        return jnp.concatenate([leading, mode_field[:, M:]], axis=1)
    grid_field = forward_map(direction)
    ytiles = NY // CY
    xtiles = NX // CX
    tiled = grid_field.reshape(V, L, ytiles, CY, xtiles, CX).transpose(2, 4, 0, 1, 3, 5).reshape(ytiles * xtiles, V * L * CY * CX)
    slots = observed_cell.reshape(ytiles * xtiles, OBS_DEV)
    picked = jnp.take_along_axis(tiled, slots, axis=1)
    live_slots = jnp.arange(OBS_DEV)[None, :] < observed_count[:, None]
    weighted = jnp.where(live_slots, observed_weight.reshape(ytiles * xtiles, OBS_DEV) * picked, 0.0)
    tile_rows = jnp.broadcast_to(jnp.arange(ytiles * xtiles)[:, None], slots.shape)
    spread_tiles = jnp.zeros_like(tiled).at[tile_rows, slots].add(weighted)
    spread = spread_tiles.reshape(ytiles, xtiles, V, L, CY, CX).transpose(2, 3, 0, 4, 1, 5).reshape(V, L, NY, NX)
    image = direction + adjoint_map(spread)
    norm_old = jnp.sum(residual * residual)
    curvature = jnp.sum(direction * image)
    step_size = norm_old / curvature
    new_increment = increment + step_size * direction
    moved = residual - step_size * image
    flat_lanczos = lanczos.reshape(K, -1)
    flat_moved = moved.reshape(-1)

    def intersection_one(vector_row):
        return jnp.sum(vector_row.astype(jnp.float32) * flat_moved)
    intersections = lax.map(intersection_one, flat_lanczos)
    coefficient = intersections / NTOT

    def remove_one(vector_index, running):
        return running - coefficient[vector_index] * flat_lanczos[vector_index].astype(jnp.float32)
    new_flat = lax.fori_loop(0, K, remove_one, flat_moved)
    new_residual = new_flat.reshape(moved.shape)
    norm_new = jnp.sum(new_residual * new_residual)
    new_direction = new_residual + norm_new / norm_old * direction
    return (new_increment, new_residual, new_direction)
```

```python
import functools

import jax
import jax.numpy as jnp
from jax import lax
from jax.experimental import pallas as pl
from jax.experimental.pallas import tpu as pltpu
from jax.sharding import PartitionSpec as P

MESH = pl.DeviceIdType.MESH
f32 = jnp.float32
bf16 = jnp.bfloat16
CHUNK = 32
GRAM = 128
PARTS = 5


def kernel(
    R, C, V, L, M, K, ny, nx, total_cells,
    cnt_ref, dir_hbm, len_e_hbm, len_n_hbm, vm_hbm, amp_hbm, cell_hbm, wgt_hbm,
    res_hbm, inc_hbm, lz_hbm,
    tot_ref, res_ref, inc_ref, dir_ref, img_ref, lz_ref,
    len_ref, vm_ref, amp_ref, cell_ref, wgt_ref,
    tab_ref, own_ref, near_ref, far_ref, mix_ref,
    lead_ref, mom_ref, hot_ref, wsum_ref, gram_ref,
    es_ref, er_ref, ns_ref, nr_ref, rs_ref, rr_ref,
    load_sem, e_ssem, e_rsem, n_ssem, n_rsem, r_ssem, r_rsem,
):
    N = R * C
    I = V * M
    row, col = lax.axis_index("row"), lax.axis_index("col")
    me = row * C + col
    barrier = pltpu.get_barrier_semaphore()

    def place(d):
        peer = lax.rem(me + d, N)
        return (lax.div(peer, C), lax.rem(peer, C))

    def greet(d, carry):
        pl.semaphore_signal(barrier, inc=1, device_id=place(d), device_id_type=MESH)
        return carry

    plane = L * ny
    lead_rows = M * ny
    firsts = [
        pltpu.make_async_copy(len_e_hbm, len_ref.at[0], load_sem.at[3]),
        pltpu.make_async_copy(len_n_hbm, len_ref.at[1], load_sem.at[4]),
    ]
    others = [
        pltpu.make_async_copy(cell_hbm, cell_ref, load_sem.at[5]),
        pltpu.make_async_copy(wgt_hbm, wgt_ref, load_sem.at[6]),
        pltpu.make_async_copy(vm_hbm, vm_ref, load_sem.at[7]),
        pltpu.make_async_copy(amp_hbm, amp_ref, load_sem.at[8]),
    ]
    for v in range(V):
        part = pl.ds(v * plane, lead_rows)
        firsts.append(
            pltpu.make_async_copy(dir_hbm.at[part], dir_ref.at[part], load_sem.at[9 + v])
        )
        part = pl.ds(v * plane + lead_rows, plane - lead_rows)
        others.append(
            pltpu.make_async_copy(dir_hbm.at[part], dir_ref.at[part], load_sem.at[9 + V + v])
        )
    loads = [
        pltpu.make_async_copy(res_hbm, res_ref, load_sem.at[0]),
        pltpu.make_async_copy(lz_hbm, lz_ref, load_sem.at[1]),
        pltpu.make_async_copy(inc_hbm, inc_ref, load_sem.at[2]),
    ]
    for load in firsts + others + loads:
        load.start()
    lax.fori_loop(1, N, greet, 0)
    for load in firsts:
        load.wait()
    for i in range(I):
        v, m = i // M, i % M
        rows = slice(i * ny, (i + 1) * ny)
        for which, size in ((0, nx), (1, ny)):
            length = jnp.broadcast_to(len_ref[which, v : v + 1, m : m + 1], (ny, nx))
            tab_ref[which, rows, :] = -1.0 / (length * float(size))

    lane = lax.broadcasted_iota(jnp.int32, (1, 1, nx), 2)
    sub = lax.broadcasted_iota(jnp.int32, (1, ny, 1), 1)

    def log_alpha(which):
        return tab_ref[which].reshape(I, ny, nx)

    def scans(u, which):
        axis, size, at = ((2, nx, lane), (1, ny, sub))[which]
        power = jnp.exp(log_alpha(which))
        f, g = u, u
        shift = 1
        while shift < size:
            f = f + power * jnp.where(at >= shift, pltpu.roll(f, shift, axis), 0.0)
            g = g + power * jnp.where(at < size - shift, pltpu.roll(g, size - shift, axis), 0.0)
            power = power * power
            shift *= 2
        return f, g

    def weights(log_small, index, count, size):
        at = index.astype(f32)
        left, right, edge = [None], [None], []
        back = jnp.exp(log_small * (size * (float(count - 1) - at)))
        for d in range(count):
            wraps = d > index
            source = jnp.where(wraps, index - d + count, index - d).astype(f32)
            if d > 0:
                left.append(jnp.where(wraps, 0.0, jnp.exp(log_small * float(size * (d - 1)))))
                right.append(
                    jnp.where(wraps, jnp.exp(log_small * float(size * (count - d - 1))), 0.0)
                )
            edge.append(
                back * jnp.exp(log_small * (float(size * (count - 1)) - size * source + 1.0))
            )
        return left, right, edge

    def combine(table, own, received, copies):
        left_w, right_w, edge_w = table
        e, b, e_edge = own
        left = jnp.zeros_like(e)
        right = -edge_w[0] * e_edge
        for d, copy in enumerate(copies, 1):
            copy.wait_recv()
            e, b, e_edge = received(d)
            left += left_w[d] * e
            right += right_w[d] * b - edge_w[d] * e_edge
        for copy in copies:
            copy.wait_send()
        return left, right

    def tables(which):
        size, at = ((nx, lane), (ny, sub))[which]
        log_a = log_alpha(which)
        a = jnp.exp(log_a)
        scale = jnp.sqrt((1.0 - a) / (1.0 + a))
        at = at.astype(f32)
        own_ref[which] = scale.reshape(I * ny, nx)
        near_ref[which] = (scale * jnp.exp(log_a * (at + 1.0))).reshape(I * ny, nx)
        far_ref[which] = (scale * jnp.exp(log_a * (float(size) - at))).reshape(I * ny, nx)

    def east_copies(inst):
        return [
            pltpu.make_async_remote_copy(
                src_ref=es_ref.at[inst],
                dst_ref=er_ref.at[inst, d],
                send_sem=e_ssem.at[inst, d],
                recv_sem=e_rsem.at[inst, d],
                device_id=(row, lax.rem(col + d, C)),
                device_id_type=MESH,
            )
            for d in range(1, C)
        ]

    def north_copies(inst):
        return [
            pltpu.make_async_remote_copy(
                src_ref=ns_ref.at[inst],
                dst_ref=nr_ref.at[inst, d],
                send_sem=n_ssem.at[inst, d],
                recv_sem=n_rsem.at[inst, d],
                device_id=(lax.rem(row + d, R), col),
                device_id_type=MESH,
            )
            for d in range(1, R)
        ]

    small_lane = lax.broadcasted_iota(jnp.int32, (ny, nx), 1)

    def east_start(u, inst):
        f, g = scans(u, 0)
        first = jnp.zeros((ny, nx), f32)
        second = jnp.zeros((ny, nx), f32)
        for i in range(I):
            e = jnp.broadcast_to(f[i, :, nx - 1 : nx], (ny, nx))
            b = jnp.broadcast_to(g[i, :, 0:1], (ny, nx))
            first = jnp.where(small_lane == i, e, first)
            first = jnp.where(small_lane == I + i, b, first)
            second = jnp.where(small_lane == I + i, e, second)
        es_ref[inst, 0] = first
        es_ref[inst, 1] = second
        lead_ref[...] = (f + g - u).reshape(I * ny, nx)
        return east_copies(inst)

    def east_finish(inst, copies):
        left, right = combine(
            east_table,
            (es_ref[inst, 0], es_ref[inst, 0], es_ref[inst, 1]),
            lambda d: (er_ref[inst, d, 0], er_ref[inst, d, 0], er_ref[inst, d, 1]),
            copies,
        )
        for i in range(I):
            rows = slice(i * ny, (i + 1) * ny)
            x = jnp.broadcast_to(left[:, i : i + 1], (ny, nx))
            y = jnp.broadcast_to(right[:, I + i : I + i + 1], (ny, nx))
            lead_ref[rows, :] = (
                own_ref[0, rows, :] * lead_ref[rows, :]
                + near_ref[0, rows, :] * x
                + far_ref[0, rows, :] * y
            )

    def north_start(u, inst):
        f, g = scans(u, 1)
        mom_ref[0] = f.reshape(I * ny, nx)
        mom_ref[1] = g.reshape(I * ny, nx)
        ns_ref[inst, 0] = mom_ref[0, pl.ds(ny - 1, I, stride=ny), :]
        ns_ref[inst, 1] = mom_ref[1, pl.ds(0, I, stride=ny), :]
        lead_ref[...] = (f + g - u).reshape(I * ny, nx)
        return north_copies(inst)

    def north_finish(inst, copies):
        left, right = combine(
            north_table,
            (ns_ref[inst, 0], ns_ref[inst, 1], ns_ref[inst, 0]),
            lambda d: (nr_ref[inst, d, 0], nr_ref[inst, d, 1], nr_ref[inst, d, 0]),
            copies,
        )
        for i in range(I):
            rows = slice(i * ny, (i + 1) * ny)
            x = jnp.broadcast_to(left[i : i + 1, :], (ny, nx))
            y = jnp.broadcast_to(right[i : i + 1, :], (ny, nx))
            lead_ref[rows, :] = (
                own_ref[1, rows, :] * lead_ref[rows, :]
                + near_ref[1, rows, :] * x
                + far_ref[1, rows, :] * y
            )

    u = jnp.concatenate([dir_ref[v * plane : v * plane + M * ny, :] for v in range(V)], axis=0)
    copies = east_start(u.reshape(I, ny, nx), 0)
    pl.semaphore_wait(barrier, N - 1)
    for copy in copies:
        copy.start()

    log_small = jnp.zeros((ny, nx), f32)
    for i in range(I):
        hit = (small_lane == i) | (small_lane == I + i)
        log_small = jnp.where(hit, tab_ref[0, i * ny : (i + 1) * ny, :], log_small)
    east_table = weights(log_small, col, C, nx)
    tables(0)
    for load in others:
        load.wait()

    pad = mix_ref.shape[1] // 2
    cell = cell_ref[...]
    slots = cell.shape[1]
    level = lax.shift_right_logical(cell, (ny * nx).bit_length() - 1)
    spot = cell & (ny * nx - 1)
    hot_ref[...] = jnp.where(
        lax.broadcasted_iota(jnp.int32, (ny * nx, slots), 0) == spot, 1.0, 0.0
    ).astype(bf16)
    live = lax.broadcasted_iota(jnp.int32, (1, slots), 1) < cnt_ref[0]
    rest = jnp.where(live, wgt_ref[...], 0.0)
    at = lax.broadcasted_iota(jnp.int32, (pad, slots), 0)
    hits = [(at + v * L == level) & (at < L) for v in range(V)]
    lhs = []
    for _ in range(3):
        part = rest.astype(bf16).astype(f32)
        lhs += [jnp.where(hit, part, 0.0).astype(bf16) for hit in hits]
        rest = rest - part
    summed = lax.dot_general(
        jnp.concatenate(lhs, axis=0), hot_ref[...], (((1,), (1,)), ((), ())),
        preferred_element_type=f32,
    )
    for v in range(V):
        wsum_ref[v] = sum(
            summed[(n * V + v) * pad : (n * V + v + 1) * pad] for n in range(3)
        )
    mix_ref[...] = jnp.zeros_like(mix_ref)
    for v in range(V):
        mix_ref[v, 0:L, 0:L] = vm_ref[:, v, :] * amp_ref[v : v + 1, :]

    east_finish(0, copies)
    copies = north_start(lead_ref[...].reshape(I, ny, nx), 0)
    for copy in copies:
        copy.start()
    north_table = weights(tab_ref[1, pl.ds(0, I, stride=ny), :], row, R, ny)
    tables(1)

    def split(x):
        high = x.astype(bf16)
        return high, (x - high.astype(f32)).astype(bf16)

    def wide(x):
        high = x.astype(bf16).astype(f32)
        low = x - high
        return jnp.concatenate(
            [high + pltpu.roll(low, pad, 1), high], axis=1
        )[0:pad, :].astype(bf16)

    def tall(x):
        high, low = split(x)
        return jnp.concatenate([high, high, low, jnp.zeros_like(low)], axis=0)

    sides = []
    for v in range(V):
        mixed = mix_ref[v]
        sides.append((wide(mixed), wide(mixed.T)))
    north_finish(0, copies)

    spare = jnp.zeros((pad - L, nx), f32)
    for v in range(V):
        field = jnp.concatenate(
            [
                jnp.concatenate(
                    [
                        lead_ref[pl.ds(v * lead_rows + y, M, stride=ny), :],
                        dir_ref[pl.ds(v * plane + lead_rows + y, L - M, stride=ny), :],
                        spare,
                    ],
                    axis=0,
                )
                for y in range(ny)
            ],
            axis=1,
        )
        grid = jnp.dot(sides[v][0], tall(field), preferred_element_type=f32)
        back = jnp.dot(sides[v][1], tall(grid * wsum_ref[v]), preferred_element_type=f32)
        for y in range(ny):
            img_ref[pl.ds(v * plane + y, L, stride=ny), :] = back[0:L, y * nx : (y + 1) * nx]

    u = jnp.concatenate([img_ref[v * plane : v * plane + M * ny, :] for v in range(V)], axis=0)
    copies = north_start(u.reshape(I, ny, nx), 1)
    for copy in copies:
        copy.start()

    steps = V * plane // CHUNK

    def fold(x):
        return jnp.sum(x.reshape(CHUNK // 8, 8, nx), axis=0)

    loads[0].wait()
    loads[1].wait()
    zero = jnp.zeros((8, nx), f32)

    def first_dots(s, carry):
        rows = pl.ds(pl.multiple_of(s * CHUNK, CHUNK), CHUNK)
        r = res_ref[rows, :]
        out = [carry[0] + fold(r * r)]
        for k in range(K):
            out.append(carry[k + 1] + fold(r * lz_ref[k, rows, :].astype(f32)))
        return tuple(out)

    gram_ref[...] = jnp.zeros_like(gram_ref)

    def gram(s, carry):
        deep = GRAM // 16
        parts = [
            lz_ref[:, pl.ds(pl.multiple_of(s * GRAM + n * 16, 16), 16), :].reshape(K * 16, nx)
            for n in range(deep)
        ]
        x = jnp.concatenate(parts, axis=1)
        gram_ref[...] += lax.dot_general(
            x, x, (((1,), (1,)), ((), ())), preferred_element_type=f32
        )
        return carry

    lax.fori_loop(0, V * plane // GRAM, gram, 0)
    at_row = lax.broadcasted_iota(jnp.int32, (K * 16, K * 16), 0)
    at_col = lax.broadcasted_iota(jnp.int32, (K * 16, K * 16), 1)
    kept = jnp.where((at_row & 15) == (at_col & 15), gram_ref[...], 0.0)
    kept = jnp.sum(kept.reshape(K, 16, K * 16), axis=1)
    kept = jnp.concatenate([kept, jnp.zeros((16 - K, K * 16), f32)], axis=0)
    which_k = lax.shift_right_logical(lax.broadcasted_iota(jnp.int32, (K * 16, nx), 0), 4)
    in_lane = lax.broadcasted_iota(jnp.int32, (K * 16, nx), 1)
    pick = jnp.zeros((K * 16, nx), f32)
    for j in range(K):
        pick = jnp.where(in_lane == which_k + j * K, 1.0, pick)
    spread_out = jnp.dot(
        kept, pick, preferred_element_type=f32, precision=lax.Precision.HIGHEST
    )
    g_lane = lax.broadcasted_iota(jnp.int32, (16, nx), 1)
    g_row = lax.broadcasted_iota(jnp.int32, (16, nx), 0)
    own_row = (g_lane >= g_row * K) & (g_lane < (g_row + 1) * K) & (g_row < K)
    gram_row = jnp.sum(jnp.where(own_row, spread_out, 0.0), axis=0, keepdims=True)
    res_dots = lax.fori_loop(0, steps, first_dots, (zero,) * (K + 1))

    north_finish(1, copies)
    copies = east_start(lead_ref[...].reshape(I, ny, nx), 1)
    for copy in copies:
        copy.start()
    east_finish(1, copies)
    for v in range(V):
        img_ref[v * plane : v * plane + M * ny, :] = lead_ref[v * M * ny : (v + 1) * M * ny, :]

    def second_dots(s, carry):
        rows = pl.ds(pl.multiple_of(s * CHUNK, CHUNK), CHUNK)
        d = dir_ref[rows, :]
        image = d + img_ref[rows, :]
        img_ref[rows, :] = image
        r = res_ref[rows, :]
        out = [
            carry[0] + fold(r * image), carry[1] + fold(image * image), carry[2] + fold(d * image)
        ]
        for k in range(K):
            out.append(carry[k + 3] + fold(image * lz_ref[k, rows, :].astype(f32)))
        return tuple(out)

    img_dots = lax.fori_loop(0, steps, second_dots, (zero,) * (K + 3), unroll=2)

    def reduce_copy(over, along):
        return pltpu.make_async_remote_copy(
            src_ref=rs_ref,
            dst_ref=rr_ref.at[pl.ds(over * C + along, 1)],
            send_sem=r_ssem.at[0],
            recv_sem=r_rsem.at[0],
            device_id=(lax.rem(row + over, R), lax.rem(col + along, C)),
            device_id_type=MESH,
        )

    sums = list(res_dots[1:]) + list(img_dots[3:]) + [res_dots[0]] + list(img_dots[:3])
    rows = [jnp.zeros((K * K, nx), f32)] + [jnp.sum(x, axis=0, keepdims=True) for x in sums]
    rows.append(jnp.zeros((nx - K * K - len(sums), nx), f32))
    packed = jnp.sum(jnp.concatenate(rows, axis=0).T, axis=0, keepdims=True)
    rs_ref[...] = packed + gram_row

    def go(over, carry):
        for along in range(C):
            reduce_copy(over, along).start()
        return carry

    lax.fori_loop(1, R, go, 0)
    for along in range(1, C):
        reduce_copy(0, along).start()
    loads[2].wait()
    every = pltpu.make_async_remote_copy(
        src_ref=rr_ref.at[pl.ds(1, N - 1)],
        dst_ref=rr_ref.at[pl.ds(1, N - 1)],
        send_sem=r_ssem.at[0],
        recv_sem=r_rsem.at[0],
        device_id=(row, lax.rem(col + 1, C)),
        device_id_type=MESH,
    )
    every.wait_recv()
    every.wait_send()
    rr_ref[pl.ds(0, 1)] = rs_ref[...]
    tot_ref[...] = jnp.broadcast_to(jnp.sum(rr_ref[...], axis=0, keepdims=True), (8, nx))


def update(
    K, total_cells, parts,
    tot_ref, res_ref, inc_ref, dir_ref, img_ref, lz_ref, oinc_hbm, ores_hbm, odir_hbm,
    oinc_ref, ores_ref, odir_ref, sem,
):
    flat, nx = res_ref.shape
    totals = tot_ref[0:1, :]
    lane = lax.broadcasted_iota(jnp.int32, (1, nx), 1)

    def total(n):
        return totals[:, n : n + 1]

    first = K * K
    rr, ri, ii, di = (total(first + 2 * K + n) for n in range(4))
    step_size = rr / di
    moments = [total(first + k) - step_size * total(first + K + k) for k in range(K)]
    left, right = jnp.zeros((1, nx), f32), jnp.zeros((1, nx), f32)
    for j in range(K):
        left = jnp.where((lane >= j * K) & (lane < (j + 1) * K), moments[j], left)
    single = jnp.zeros((1, nx), f32)
    for k in range(K):
        hit = lane == k
        for j in range(1, K):
            hit = hit | (lane == j * K + k)
        right = jnp.where(hit, moments[k], right)
        single = jnp.where(lane == k, moments[k], single)
    squares = jnp.sum(left * right * totals, axis=1, keepdims=True)
    crossed = jnp.sum(single * single, axis=1, keepdims=True)
    moved_norm = rr + step_size * (step_size * ii - 2.0 * ri)
    norm_new = moved_norm + (squares / total_cells - 2.0 * crossed) / total_cells
    coefficient = [jnp.broadcast_to(x / total_cells, (CHUNK, nx)) for x in moments]
    step_wide = jnp.broadcast_to(step_size, (CHUNK, nx))
    ratio = jnp.broadcast_to(norm_new / rr, (CHUNK, nx))
    size = flat // parts
    copies = []
    for part in range(parts):

        def advance(s, carry):
            rows = pl.ds(pl.multiple_of(part * size + s * CHUNK, CHUNK), CHUNK)
            d = dir_ref[rows, :]
            new = res_ref[rows, :] - step_wide * img_ref[rows, :]
            for k in range(K):
                new = new - coefficient[k] * lz_ref[k, rows, :].astype(f32)
            oinc_ref[rows, :] = inc_ref[rows, :] + step_wide * d
            ores_ref[rows, :] = new
            odir_ref[rows, :] = new + ratio * d
            return carry

        lax.fori_loop(0, size // CHUNK, advance, 0, unroll=2)
        rows = pl.ds(part * size, size)
        for n, (src, dst) in enumerate(
            ((oinc_ref, oinc_hbm), (ores_ref, ores_hbm), (odir_ref, odir_hbm))
        ):
            copies.append(pltpu.make_async_copy(src.at[rows], dst.at[rows], sem.at[part, n]))
            copies[-1].start()
    for copy in copies:
        copy.wait()


def local(
    R, C,
    increment, residual, direction, lanczos, vertical_modes, amplitude,
    length_east, length_north, observed_cell, observed_weight, observed_count,
):
    V, L, ny, nx = direction.shape
    M = length_east.shape[1]
    K = lanczos.shape[0]
    I = V * M
    N = R * C
    flat = V * L * ny
    slots = observed_cell.shape[0]
    pad = (L + 15) // 16 * 16
    hbm = pl.BlockSpec(memory_space=pltpu.HBM)
    near = pl.BlockSpec(memory_space=pltpu.VMEM)
    field = pltpu.VMEM((flat, nx), f32)
    held = pl.pallas_call(
        functools.partial(kernel, R, C, V, L, M, K, ny, nx, float(flat * nx * N)),
        out_shape=(pltpu.VMEM((8, nx), f32),) + (field,) * 4 + (pltpu.VMEM((K, flat, nx), bf16),),
        in_specs=[pl.BlockSpec(memory_space=pltpu.SMEM)] + [hbm] * 10,
        out_specs=(near,) * 6,
        scratch_shapes=[
            pltpu.VMEM((2, V, M), f32), pltpu.VMEM((L, V, L), f32),
            pltpu.VMEM((V, L), f32), pltpu.VMEM((1, slots), jnp.int32), pltpu.VMEM((1, slots), f32),
            pltpu.VMEM((2, I * ny, nx), f32), pltpu.VMEM((2, I * ny, nx), f32),
            pltpu.VMEM((2, I * ny, nx), f32), pltpu.VMEM((2, I * ny, nx), f32),
            pltpu.VMEM((V, 2 * pad, 2 * pad), f32),
            pltpu.VMEM((I * ny, nx), f32), pltpu.VMEM((2, I * ny, nx), f32),
            pltpu.VMEM((ny * nx, slots), bf16), pltpu.VMEM((V, pad, ny * nx), f32),
            pltpu.VMEM((K * 16, K * 16), f32),
            pltpu.VMEM((2, 2, ny, nx), f32), pltpu.VMEM((2, C, 2, ny, nx), f32),
            pltpu.VMEM((2, 2, I, nx), f32), pltpu.VMEM((2, R, 2, I, nx), f32),
            pltpu.VMEM((1, nx), f32), pltpu.VMEM((N, nx), f32),
            pltpu.SemaphoreType.DMA((9 + 2 * V,)),
            pltpu.SemaphoreType.DMA((2, C)), pltpu.SemaphoreType.DMA((2, C)),
            pltpu.SemaphoreType.DMA((2, R)), pltpu.SemaphoreType.DMA((2, R)),
            pltpu.SemaphoreType.DMA((1,)), pltpu.SemaphoreType.DMA((1,)),
        ],
        compiler_params=pltpu.CompilerParams(
            collective_id=0, has_side_effects=True, vmem_limit_bytes=54 * 2**20
        ),
    )(
        observed_count, direction.reshape(flat, nx), length_east, length_north,
        jnp.transpose(vertical_modes, (1, 0, 2)), amplitude,
        observed_cell.reshape(1, slots), observed_weight.reshape(1, slots),
        residual.reshape(flat, nx), increment.reshape(flat, nx), lanczos.reshape(K, flat, nx),
    )
    done = pl.pallas_call(
        functools.partial(update, K, float(flat * nx * N), PARTS),
        out_shape=(jax.ShapeDtypeStruct((flat, nx), f32),) * 3,
        in_specs=[near] * 6,
        out_specs=(hbm,) * 3,
        scratch_shapes=[
            pltpu.VMEM((flat, nx), f32), pltpu.VMEM((flat, nx), f32), pltpu.VMEM((flat, nx), f32),
            pltpu.SemaphoreType.DMA((PARTS, 3)),
        ],
        compiler_params=pltpu.CompilerParams(vmem_limit_bytes=16 * 2**20),
    )(*held)
    return tuple(x.reshape(V, L, ny, nx) for x in done)


def solution(mesh):
    field = P(None, None, "row", "col")
    tile = P(("row", "col"))
    in_specs = (
        field, field, field, P(None, None, None, "row", "col"),
        P(), P(), P(), P(), tile, tile, tile,
    )
    return jax.shard_map(
        functools.partial(local, mesh.shape["row"], mesh.shape["col"]),
        mesh=mesh, in_specs=in_specs, out_specs=(field,) * 3, check_vma=False,
    )
```

```python
import functools

import jax
import jax.numpy as jnp
from jax import lax
from jax.experimental import pallas as pl
from jax.experimental.pallas import tpu as pltpu
from jax.sharding import PartitionSpec as P

MESH = pl.DeviceIdType.MESH
f32 = jnp.float32
bf16 = jnp.bfloat16
CHUNK = 32
GRAM = 128
PARTS = 5


def kernel(
    R, C, V, L, M, K, ny, nx,
    cnt_hbm, dir_hbm, len_e_hbm, len_n_hbm, vm_hbm, amp_hbm, cell_hbm, wgt_hbm,
    res_hbm, inc_hbm, lz_hbm,
    tot_ref, res_ref, inc_ref, dir_ref, img_ref, lz_ref,
    cnt_ref, len_ref, vm_ref, amp_ref, cell_ref, wgt_ref,
    east_ref, north_ref, end_ref, start_ref, mix_ref, comb_ref, both_ref,
    lead_ref, pair_ref, hot_ref, near_ref, sel_ref, rest_ref, gram_ref,
    es_ref, er_ref, ns_ref, nr_ref, cs_ref, cr_ref, rs_ref, rr_ref,
    load_sem, e_ssem, e_rsem, n_ssem, n_rsem, c_ssem, c_rsem, r_ssem, r_rsem,
):
    N = R * C
    I = V * M
    row, col = lax.axis_index("row"), lax.axis_index("col")
    me = row * C + col
    barrier = pltpu.get_barrier_semaphore()

    def place(d):
        peer = lax.rem(me + d, N)
        return (lax.div(peer, C), lax.rem(peer, C))

    def greet(d, carry):
        pl.semaphore_signal(barrier, inc=1, device_id=place(d), device_id_type=MESH)
        return carry

    plane = L * ny
    lead_rows = M * ny
    rest = L - M
    firsts = [
        pltpu.make_async_copy(len_e_hbm, len_ref.at[0], load_sem.at[3]),
        pltpu.make_async_copy(len_n_hbm, len_ref.at[1], load_sem.at[4]),
    ]
    others = [
        pltpu.make_async_copy(cell_hbm, cell_ref, load_sem.at[5]),
        pltpu.make_async_copy(wgt_hbm, wgt_ref, load_sem.at[6]),
        pltpu.make_async_copy(vm_hbm, vm_ref, load_sem.at[7]),
        pltpu.make_async_copy(amp_hbm, amp_ref, load_sem.at[8]),
        pltpu.make_async_copy(cnt_hbm, cnt_ref, load_sem.at[9 + 2 * V]),
    ]
    leads = []
    for v in range(V):
        part = pl.ds(v * plane, lead_rows)
        leads.append(
            pltpu.make_async_copy(dir_hbm.at[part], dir_ref.at[part], load_sem.at[9 + v])
        )
        part = pl.ds(v * plane + lead_rows, plane - lead_rows)
        others.append(
            pltpu.make_async_copy(dir_hbm.at[part], dir_ref.at[part], load_sem.at[9 + V + v])
        )
    loads = [
        pltpu.make_async_copy(res_hbm, res_ref, load_sem.at[0]),
        pltpu.make_async_copy(lz_hbm, lz_ref, load_sem.at[1]),
        pltpu.make_async_copy(inc_hbm, inc_ref, load_sem.at[2]),
    ]
    for load in firsts + leads + others + loads:
        load.start()
    lax.fori_loop(1, N, greet, 0)
    for load in firsts:
        load.wait()

    lane = lax.broadcasted_iota(jnp.int32, (ny, nx), 1)
    sub = lax.broadcasted_iota(jnp.int32, (ny, nx), 0)
    east_at, north_at = lane.astype(f32), sub.astype(f32)
    inst_lane = lane & (I - 1)
    is_back = (lane & I) != 0
    is_late = lane >= 2 * I
    log_e = jnp.zeros((ny, nx), f32)
    log_n = jnp.zeros((ny, nx), f32)
    for i in range(I):
        v, m = i // M, i % M
        rows = slice(i * ny, (i + 1) * ny)
        e = -1.0 / (jnp.broadcast_to(len_ref[0, v : v + 1, m : m + 1], (ny, nx)) * float(nx))
        n = -1.0 / (jnp.broadcast_to(len_ref[1, v : v + 1, m : m + 1], (ny, nx)) * float(ny))
        log_e = jnp.where(inst_lane == i, e, log_e)
        log_n = jnp.where(inst_lane == i, n, log_n)
        east_ref[rows, :] = e
        north_ref[rows, :] = n
        end_ref[0, rows, :] = jnp.exp(e * (float(nx - 1) - east_at))
        start_ref[0, rows, :] = jnp.exp(e * east_at)
        end_ref[1, rows, :] = jnp.exp(n * (float(ny - 1) - north_at))
        start_ref[1, rows, :] = jnp.exp(n * north_at)
    corner_w = jnp.exp(log_n * jnp.where(is_late, north_at, float(ny - 1) - north_at))

    def every_sub(x):
        shift = ny // 2
        while shift:
            x = x + pltpu.roll(x, shift, 0)
            shift //= 2
        return x

    def split(x):
        high = x.astype(bf16)
        return high, (x - high.astype(f32)).astype(bf16)

    def begin(u, inst):
        for i in range(I):
            rows = slice(i * ny, (i + 1) * ny)
            pair_ref[0, rows, :] = every_sub(u[rows] * end_ref[1, rows, :])
            pair_ref[1, rows, :] = every_sub(u[rows] * start_ref[1, rows, :])
        ns_ref[inst, 0:I] = pair_ref[0, pl.ds(0, I, stride=ny), :]
        ns_ref[inst, I : 2 * I] = pair_ref[1, pl.ds(0, I, stride=ny), :]
        moment = jnp.zeros((ny, nx), f32)
        for i in range(I):
            rows = slice(i * ny, (i + 1) * ny)
            e = jnp.sum(u[rows] * end_ref[0, rows, :], axis=1, keepdims=True)
            b = jnp.sum(u[rows] * start_ref[0, rows, :], axis=1, keepdims=True)
            moment = jnp.where(inst_lane == i, jnp.where(is_back, b, e), moment)
        es_ref[inst] = moment
        cs_ref[inst] = every_sub(moment * corner_w)[0:1]

    def launch(inst):
        for d in range(1, R):
            pltpu.make_async_remote_copy(
                src_ref=ns_ref.at[inst],
                dst_ref=nr_ref.at[inst, d],
                send_sem=n_ssem.at[inst, d],
                recv_sem=n_rsem.at[inst, d],
                device_id=(lax.rem(row + d, R), col),
                device_id_type=MESH,
            ).start()

        def go(over, carry):
            for along in range(C):
                pltpu.make_async_remote_copy(
                    src_ref=cs_ref.at[inst],
                    dst_ref=cr_ref.at[inst, over, pl.ds(along, 1)],
                    send_sem=c_ssem.at[inst, over],
                    recv_sem=c_rsem.at[inst, over],
                    device_id=(lax.rem(row + over, R), lax.rem(col + along, C)),
                    device_id_type=MESH,
                ).start()
            return carry

        lax.fori_loop(1, R, go, 0)
        for d in range(1, C):
            pltpu.make_async_remote_copy(
                src_ref=es_ref.at[inst],
                dst_ref=er_ref.at[inst, d],
                send_sem=e_ssem.at[inst, d],
                recv_sem=e_rsem.at[inst, d],
                device_id=(row, lax.rem(col + d, C)),
                device_id_type=MESH,
            ).start()

    def arrival(inst, kind, d):
        src, dst, send, recv = (
            (ns_ref.at[inst], nr_ref.at[inst, d], n_ssem, n_rsem),
            (es_ref.at[inst], er_ref.at[inst, d], e_ssem, e_rsem),
            (cr_ref.at[inst, d], cr_ref.at[inst, d], c_ssem, c_rsem),
        )[kind]
        return pltpu.make_async_remote_copy(
            src_ref=src, dst_ref=dst, send_sem=send.at[inst, d], recv_sem=recv.at[inst, d],
            device_id=(row, lax.rem(col + 1, C)), device_id_type=MESH,
        )

    def scans(u, log_alpha, axis, size, at):
        power = jnp.exp(log_alpha)
        f, g = u, u
        shift = 1
        while shift < size:
            f = f + power * jnp.where(at >= shift, pltpu.roll(f, shift, axis), 0.0)
            g = g + power * jnp.where(at < size - shift, pltpu.roll(g, size - shift, axis), 0.0)
            power = power * power
            shift *= 2
        return f + g - u

    def inside(u):
        u = u.reshape(I, ny, nx)
        u = scans(u, east_ref[...].reshape(I, ny, nx), 2, nx, lane[None])
        u = scans(u, north_ref[...].reshape(I, ny, nx), 1, ny, sub[None])
        lead_ref[...] = both_ref[0] * u.reshape(I * ny, nx)

    def weights(log_small, d, index, count, size):
        at = index.astype(f32)
        far = d > index
        source = jnp.where(far, index - d + count, index - d).astype(f32)
        step = d.astype(f32)
        left = jnp.where(
            far | (d == 0), 0.0, jnp.exp(log_small * (float(size) * jnp.maximum(step - 1.0, 0.0)))
        )
        right = jnp.where(
            far, jnp.exp(log_small * (float(size) * (float(count - 1) - step))), 0.0
        )
        edge = jnp.exp(
            log_small * (float(size) * (float(2 * count - 2) - at - source) + 1.0)
        )
        return left, right, edge

    def finish(inst):
        for d in range(1, R):
            arrival(inst, 0, d).wait_recv()
        left, right, edge = north_w[0]
        p = jnp.zeros((I, nx), f32)
        q = -edge * ns_ref[inst, 0:I]
        for d in range(1, R):
            left, right, edge = north_w[d]
            p += left * nr_ref[inst, d, 0:I]
            q += right * nr_ref[inst, d, I : 2 * I] - edge * nr_ref[inst, d, 0:I]
        line = jnp.concatenate([p, q], axis=0)
        comb_ref[...] = scans(
            line, log_lines, 1, nx, lax.broadcasted_iota(jnp.int32, (2 * I, nx), 1)
        )
        for i in range(I):
            rows = slice(i * ny, (i + 1) * ny)
            lead_ref[rows, :] += (
                both_ref[1, rows, :] * jnp.broadcast_to(comb_ref[i : i + 1, :], (ny, nx))
                + both_ref[2, rows, :] * jnp.broadcast_to(comb_ref[I + i : I + i + 1, :], (ny, nx))
            )
        for d in range(1, C):
            arrival(inst, 1, d).wait_recv()
        ahead = jnp.zeros((ny, nx), f32)
        echo = col_edge[0:1] * es_ref[inst]
        for d in range(1, C):
            ahead += col_main[d : d + 1] * er_ref[inst, d]
            echo += col_edge[d : d + 1] * er_ref[inst, d]
        lines = ahead - pltpu.roll(echo, I, 1)
        settled = scans(lines, log_n, 0, ny, sub)
        for d in range(1, R):
            arrival(inst, 2, d).wait_recv()
        first = corner_w * lines
        ahead = row_main[0] * first
        echo = row_edge[0] * first
        for d in range(1, R):
            got = cr_ref[inst, d]
            got = col_main * got - pltpu.roll(col_edge * got, I, 1)
            got = jnp.sum(got.reshape(C // ny, ny, nx), axis=0)
            ahead += row_main[d] * got
            echo += row_edge[d] * got
        corner = every_sub(ahead - pltpu.roll(echo, 2 * I, 1))
        settled = lane_scale * (
            settled + lane_low * corner + lane_high * pltpu.roll(corner, 2 * I, 1)
        )
        for i in range(I):
            rows = slice(i * ny, (i + 1) * ny)
            x = jnp.broadcast_to(settled[:, i : i + 1], (ny, nx))
            y = jnp.broadcast_to(settled[:, I + i : I + i + 1], (ny, nx))
            lead_ref[rows, :] += both_ref[3, rows, :] * x + both_ref[4, rows, :] * y

    for load in leads:
        load.wait()
    u = jnp.concatenate([dir_ref[v * plane : v * plane + M * ny, :] for v in range(V)], axis=0)
    begin(u, 0)
    pl.semaphore_wait(barrier, N - 1)
    launch(0)

    alpha_e, alpha_n = jnp.exp(log_e), jnp.exp(log_n)
    lane_scale = jnp.sqrt(
        ((1.0 - alpha_e) / (1.0 + alpha_e)) * ((1.0 - alpha_n) / (1.0 + alpha_n))
    )
    lane_low = jnp.exp(log_n * (north_at + 1.0))
    lane_high = jnp.exp(log_n * (float(ny) - north_at))
    over = lax.broadcasted_iota(jnp.int32, (C, nx), 0)
    odd = (lax.broadcasted_iota(jnp.int32, (C, nx), 1) & I) != 0
    low, high, edge = weights(jnp.broadcast_to(log_e[0:1], (C, nx)), over, col, C, nx)
    col_main = jnp.where(odd, high, low)
    col_edge = jnp.where(odd, 0.0, edge)
    row_main, row_edge, north_w = [], [], []
    log_rows = north_ref[pl.ds(0, I, stride=ny), :]
    for d in range(R):
        step = jnp.full((ny, nx), d, jnp.int32)
        low, high, edge = weights(log_n, step, row, R, ny)
        row_main.append(jnp.where(is_late, high, low))
        row_edge.append(jnp.where(is_late, 0.0, edge))
        north_w.append(weights(log_rows, jnp.full((I, nx), d, jnp.int32), row, R, ny))
    log_lines = east_ref[pl.ds(0, I, stride=ny), :]
    log_lines = jnp.concatenate([log_lines, log_lines], axis=0)
    for i in range(I):
        rows = slice(i * ny, (i + 1) * ny)
        a, b = jnp.exp(east_ref[rows, :]), jnp.exp(north_ref[rows, :])
        scale = jnp.sqrt(((1.0 - a) / (1.0 + a)) * ((1.0 - b) / (1.0 + b)))
        both_ref[0, rows, :] = scale
        both_ref[1, rows, :] = scale * b * start_ref[1, rows, :]
        both_ref[2, rows, :] = scale * b * end_ref[1, rows, :]
        both_ref[3, rows, :] = a * start_ref[0, rows, :]
        both_ref[4, rows, :] = a * end_ref[0, rows, :]
    inside(u)
    for load in others:
        load.wait()

    pad = (L + 15) // 16 * 16
    cell = cell_ref[...]
    slots = cell.shape[1]
    level = lax.shift_right_logical(cell, (ny * nx).bit_length() - 1)
    spot = cell & (ny * nx - 1)
    spot_x = spot & (nx - 1)
    spot_y = lax.shift_right_logical(spot, nx.bit_length() - 1)
    hot_ref[...] = jnp.where(
        lax.broadcasted_iota(jnp.int32, (ny * nx, slots), 0) == spot, 1.0, 0.0
    ).astype(bf16)
    near = jnp.where(
        lax.broadcasted_iota(jnp.int32, (nx, slots), 0) == spot_x, 1.0, 0.0
    ).astype(bf16)
    near_ref[0:nx] = near
    near_ref[nx : 2 * nx] = near
    live = lax.broadcasted_iota(jnp.int32, (1, slots), 1) < cnt_ref[...]
    weight = jnp.where(live, wgt_ref[...], 0.0)
    mix_ref[...] = jnp.zeros_like(mix_ref)
    at = lax.broadcasted_iota(jnp.int32, (pad, slots), 0)
    here = lax.broadcasted_iota(jnp.int32, (ny, slots), 0) == spot_y
    hold = pad - M
    for v in range(V):
        mix_ref[v, 0:L, 0:L] = vm_ref[:, v, :] * amp_ref[v : v + 1, :]
        left = mix_ref[v].T[0:pad, 0:pad]
        parts = []
        for _ in range(3):
            part = left.astype(bf16)
            parts.append(part)
            left = left - part.astype(f32)
        hit = jnp.where((at + v * L == level) & (at < L), 1.0, 0.0).astype(bf16)
        chosen = jnp.dot(jnp.concatenate(parts, axis=0), hit, preferred_element_type=f32)
        chosen = chosen[0:pad] + chosen[pad : 2 * pad] + chosen[2 * pad : 3 * pad]
        rest_ref[v * hold : (v + 1) * hold] = chosen[M:pad]
        for m in range(M):
            i = v * M + m
            sel_ref[i * ny : (i + 1) * ny] = jnp.where(
                here, jnp.broadcast_to(chosen[m : m + 1], (ny, slots)), 0.0
            )

    spare = jnp.zeros((hold - rest, nx), f32)
    beside = jnp.zeros((1, slots), f32)
    for v in range(V):
        held = jnp.concatenate(
            [
                jnp.concatenate(
                    [dir_ref[pl.ds(v * plane + lead_rows + y, rest, stride=ny), :], spare], axis=0
                )
                for y in range(ny)
            ],
            axis=1,
        )
        high, low = split(held)
        seen = jnp.dot(high, hot_ref[...], preferred_element_type=f32)
        seen += jnp.dot(low, hot_ref[...], preferred_element_type=f32)
        beside += jnp.sum(seen * rest_ref[v * hold : (v + 1) * hold], axis=0, keepdims=True)

    finish(0)

    high, low = split(lead_ref[...])
    seen = jnp.dot(
        jnp.concatenate([high, low], axis=1), near_ref[...], preferred_element_type=f32
    )
    grid = jnp.sum(seen * sel_ref[...], axis=0, keepdims=True) + beside
    weighted = weight * grid
    high, low = split(sel_ref[...] * weighted)
    across = (((1,), (1,)), ((), ()))
    u = lax.dot_general(high, near_ref[0:nx], across, preferred_element_type=f32)
    u += lax.dot_general(low, near_ref[0:nx], across, preferred_element_type=f32)
    begin(u, 1)
    launch(1)

    inside(u)
    for v in range(V):
        high, low = split(rest_ref[v * hold : (v + 1) * hold] * weighted)
        back = lax.dot_general(high, hot_ref[...], across, preferred_element_type=f32)
        back += lax.dot_general(low, hot_ref[...], across, preferred_element_type=f32)
        for y in range(ny):
            img_ref[pl.ds(v * plane + lead_rows + y, rest, stride=ny), :] = back[
                0:rest, y * nx : (y + 1) * nx
            ]

    steps = V * plane // CHUNK

    def fold(x):
        return jnp.sum(x.reshape(CHUNK // 8, 8, nx), axis=0)

    loads[0].wait()
    loads[1].wait()
    zero = jnp.zeros((8, nx), f32)

    def first_dots(s, carry):
        rows = pl.ds(pl.multiple_of(s * CHUNK, CHUNK), CHUNK)
        r = res_ref[rows, :]
        out = [carry[0] + fold(r * r)]
        for k in range(K):
            out.append(carry[k + 1] + fold(r * lz_ref[k, rows, :].astype(f32)))
        return tuple(out)

    gram_ref[...] = jnp.zeros_like(gram_ref)

    def gram(s, carry):
        deep = GRAM // 16
        parts = [
            lz_ref[:, pl.ds(pl.multiple_of(s * GRAM + n * 16, 16), 16), :].reshape(K * 16, nx)
            for n in range(deep)
        ]
        x = jnp.concatenate(parts, axis=1)
        gram_ref[...] += lax.dot_general(
            x, x, (((1,), (1,)), ((), ())), preferred_element_type=f32
        )
        return carry

    lax.fori_loop(0, V * plane // GRAM, gram, 0)
    at_row = lax.broadcasted_iota(jnp.int32, (K * 16, K * 16), 0)
    at_col = lax.broadcasted_iota(jnp.int32, (K * 16, K * 16), 1)
    kept = jnp.where((at_row & 15) == (at_col & 15), gram_ref[...], 0.0)
    kept = jnp.sum(kept.reshape(K, 16, K * 16), axis=1)
    kept = jnp.concatenate([kept, jnp.zeros((16 - K, K * 16), f32)], axis=0)
    which_k = lax.shift_right_logical(lax.broadcasted_iota(jnp.int32, (K * 16, nx), 0), 4)
    in_lane = lax.broadcasted_iota(jnp.int32, (K * 16, nx), 1)
    pick = jnp.zeros((K * 16, nx), f32)
    for j in range(K):
        pick = jnp.where(in_lane == which_k + j * K, 1.0, pick)
    spread_out = jnp.dot(
        kept, pick, preferred_element_type=f32, precision=lax.Precision.HIGHEST
    )
    g_lane = lax.broadcasted_iota(jnp.int32, (16, nx), 1)
    g_row = lax.broadcasted_iota(jnp.int32, (16, nx), 0)
    own_row = (g_lane >= g_row * K) & (g_lane < (g_row + 1) * K) & (g_row < K)
    gram_row = jnp.sum(jnp.where(own_row, spread_out, 0.0), axis=0, keepdims=True)
    res_dots = lax.fori_loop(0, steps, first_dots, (zero,) * (K + 1))

    def image_dots(base, mine, carry):
        rows = pl.ds(base, CHUNK)
        d = dir_ref[rows, :]
        image = d + mine
        img_ref[rows, :] = image
        r = res_ref[rows, :]
        out = [
            carry[0] + fold(r * image), carry[1] + fold(image * image), carry[2] + fold(d * image)
        ]
        for k in range(K):
            out.append(carry[k + 3] + fold(image * lz_ref[k, rows, :].astype(f32)))
        return tuple(out)

    turns = (plane - lead_rows) // CHUNK

    def rest_dots(s, carry):
        base = lax.div(s, turns) * plane + lead_rows + lax.rem(s, turns) * CHUNK
        base = pl.multiple_of(base, CHUNK)
        return image_dots(base, img_ref[pl.ds(base, CHUNK), :], carry)

    img_dots = lax.fori_loop(0, V * turns, rest_dots, (zero,) * (K + 3), unroll=2)
    finish(1)
    short = lead_rows // CHUNK

    def lead_dots(s, carry):
        base = pl.multiple_of(lax.div(s, short) * plane + lax.rem(s, short) * CHUNK, CHUNK)
        mine = lead_ref[pl.ds(pl.multiple_of(s * CHUNK, CHUNK), CHUNK), :]
        return image_dots(base, mine, carry)

    img_dots = lax.fori_loop(0, V * short, lead_dots, img_dots, unroll=2)

    def reduce_copy(over, along):
        return pltpu.make_async_remote_copy(
            src_ref=rs_ref,
            dst_ref=rr_ref.at[pl.ds(over * C + along, 1)],
            send_sem=r_ssem.at[0],
            recv_sem=r_rsem.at[0],
            device_id=(lax.rem(row + over, R), lax.rem(col + along, C)),
            device_id_type=MESH,
        )

    sums = list(res_dots[1:]) + list(img_dots[3:]) + [res_dots[0]] + list(img_dots[:3])
    rows = [jnp.zeros((K * K, nx), f32)] + [jnp.sum(x, axis=0, keepdims=True) for x in sums]
    rows.append(jnp.zeros((nx - K * K - len(sums), nx), f32))
    packed = jnp.sum(jnp.concatenate(rows, axis=0).T, axis=0, keepdims=True)
    rs_ref[...] = packed + gram_row

    def go(over, carry):
        for along in range(C):
            reduce_copy(over, along).start()
        return carry

    lax.fori_loop(1, R, go, 0)
    for along in range(1, C):
        reduce_copy(0, along).start()
    loads[2].wait()
    every = pltpu.make_async_remote_copy(
        src_ref=rr_ref.at[pl.ds(1, N - 1)],
        dst_ref=rr_ref.at[pl.ds(1, N - 1)],
        send_sem=r_ssem.at[0],
        recv_sem=r_rsem.at[0],
        device_id=(row, lax.rem(col + 1, C)),
        device_id_type=MESH,
    )
    every.wait_recv()
    every.wait_send()
    rr_ref[pl.ds(0, 1)] = rs_ref[...]
    tot_ref[...] = jnp.broadcast_to(jnp.sum(rr_ref[...], axis=0, keepdims=True), (8, nx))
    for inst in range(2):
        for d in range(1, R):
            arrival(inst, 0, d).wait_send()
            arrival(inst, 2, d).wait_send()
        for d in range(1, C):
            arrival(inst, 1, d).wait_send()


def update(
    K, total_cells, parts,
    tot_ref, res_ref, inc_ref, dir_ref, img_ref, lz_ref, oinc_hbm, ores_hbm, odir_hbm,
    oinc_ref, ores_ref, odir_ref, sem,
):
    flat, nx = res_ref.shape
    totals = tot_ref[0:1, :]
    lane = lax.broadcasted_iota(jnp.int32, (1, nx), 1)

    def total(n):
        return totals[:, n : n + 1]

    first = K * K
    rr, ri, ii, di = (total(first + 2 * K + n) for n in range(4))
    step_size = rr / di
    moments = [total(first + k) - step_size * total(first + K + k) for k in range(K)]
    left, right = jnp.zeros((1, nx), f32), jnp.zeros((1, nx), f32)
    for j in range(K):
        left = jnp.where((lane >= j * K) & (lane < (j + 1) * K), moments[j], left)
    single = jnp.zeros((1, nx), f32)
    for k in range(K):
        hit = lane == k
        for j in range(1, K):
            hit = hit | (lane == j * K + k)
        right = jnp.where(hit, moments[k], right)
        single = jnp.where(lane == k, moments[k], single)
    squares = jnp.sum(left * right * totals, axis=1, keepdims=True)
    crossed = jnp.sum(single * single, axis=1, keepdims=True)
    moved_norm = rr + step_size * (step_size * ii - 2.0 * ri)
    norm_new = moved_norm + (squares / total_cells - 2.0 * crossed) / total_cells
    coefficient = [jnp.broadcast_to(x / total_cells, (CHUNK, nx)) for x in moments]
    step_wide = jnp.broadcast_to(step_size, (CHUNK, nx))
    ratio = jnp.broadcast_to(norm_new / rr, (CHUNK, nx))
    size = flat // parts
    copies = []
    for part in range(parts):

        def advance(s, carry):
            rows = pl.ds(pl.multiple_of(part * size + s * CHUNK, CHUNK), CHUNK)
            d = dir_ref[rows, :]
            new = res_ref[rows, :] - step_wide * img_ref[rows, :]
            for k in range(K):
                new = new - coefficient[k] * lz_ref[k, rows, :].astype(f32)
            oinc_ref[rows, :] = inc_ref[rows, :] + step_wide * d
            ores_ref[rows, :] = new
            odir_ref[rows, :] = new + ratio * d
            return carry

        lax.fori_loop(0, size // CHUNK, advance, 0, unroll=2)
        rows = pl.ds(part * size, size)
        for n, (src, dst) in enumerate(
            ((oinc_ref, oinc_hbm), (ores_ref, ores_hbm), (odir_ref, odir_hbm))
        ):
            copies.append(pltpu.make_async_copy(src.at[rows], dst.at[rows], sem.at[part, n]))
            copies[-1].start()
    for copy in copies:
        copy.wait()


def local(
    R, C,
    increment, residual, direction, lanczos, vertical_modes, amplitude,
    length_east, length_north, observed_cell, observed_weight, observed_count,
):
    V, L, ny, nx = direction.shape
    M = length_east.shape[1]
    K = lanczos.shape[0]
    I = V * M
    N = R * C
    flat = V * L * ny
    slots = observed_cell.shape[0]
    pad = (L + 15) // 16 * 16
    hbm = pl.BlockSpec(memory_space=pltpu.HBM)
    near = pl.BlockSpec(memory_space=pltpu.VMEM)
    field = pltpu.VMEM((flat, nx), f32)
    lead = pltpu.VMEM((I * ny, nx), f32)
    held = pl.pallas_call(
        functools.partial(kernel, R, C, V, L, M, K, ny, nx),
        out_shape=(pltpu.VMEM((8, nx), f32),) + (field,) * 4 + (pltpu.VMEM((K, flat, nx), bf16),),
        in_specs=[hbm] * 11,
        out_specs=(near,) * 6,
        scratch_shapes=[
            pltpu.VMEM((1, 1), jnp.int32),
            pltpu.VMEM((2, V, M), f32), pltpu.VMEM((L, V, L), f32),
            pltpu.VMEM((V, L), f32), pltpu.VMEM((1, slots), jnp.int32), pltpu.VMEM((1, slots), f32),
            lead, lead, pltpu.VMEM((2, I * ny, nx), f32), pltpu.VMEM((2, I * ny, nx), f32),
            pltpu.VMEM((V, 2 * pad, 2 * pad), f32),
            pltpu.VMEM((2 * I, nx), f32), pltpu.VMEM((5, I * ny, nx), f32),
            lead, pltpu.VMEM((2, I * ny, nx), f32),
            pltpu.VMEM((ny * nx, slots), bf16), pltpu.VMEM((2 * nx, slots), bf16),
            pltpu.VMEM((I * ny, slots), f32), pltpu.VMEM((V * (pad - M), slots), f32),
            pltpu.VMEM((K * 16, K * 16), f32),
            pltpu.VMEM((2, ny, nx), f32), pltpu.VMEM((2, C, ny, nx), f32),
            pltpu.VMEM((2, 2 * I, nx), f32), pltpu.VMEM((2, R, 2 * I, nx), f32),
            pltpu.VMEM((2, 1, nx), f32), pltpu.VMEM((2, R, C, nx), f32),
            pltpu.VMEM((1, nx), f32), pltpu.VMEM((N, nx), f32),
            pltpu.SemaphoreType.DMA((10 + 2 * V,)),
            pltpu.SemaphoreType.DMA((2, C)), pltpu.SemaphoreType.DMA((2, C)),
            pltpu.SemaphoreType.DMA((2, R)), pltpu.SemaphoreType.DMA((2, R)),
            pltpu.SemaphoreType.DMA((2, R)), pltpu.SemaphoreType.DMA((2, R)),
            pltpu.SemaphoreType.DMA((1,)), pltpu.SemaphoreType.DMA((1,)),
        ],
        compiler_params=pltpu.CompilerParams(
            collective_id=0, has_side_effects=True, vmem_limit_bytes=54 * 2**20
        ),
    )(
        observed_count.reshape(1, 1), direction.reshape(flat, nx), length_east, length_north,
        jnp.transpose(vertical_modes, (1, 0, 2)), amplitude,
        observed_cell.reshape(1, slots), observed_weight.reshape(1, slots),
        residual.reshape(flat, nx), increment.reshape(flat, nx), lanczos.reshape(K, flat, nx),
    )
    done = pl.pallas_call(
        functools.partial(update, K, float(flat * nx * N), PARTS),
        out_shape=(jax.ShapeDtypeStruct((flat, nx), f32),) * 3,
        in_specs=[near] * 6,
        out_specs=(hbm,) * 3,
        scratch_shapes=[
            pltpu.VMEM((flat, nx), f32), pltpu.VMEM((flat, nx), f32), pltpu.VMEM((flat, nx), f32),
            pltpu.SemaphoreType.DMA((PARTS, 3)),
        ],
        compiler_params=pltpu.CompilerParams(vmem_limit_bytes=16 * 2**20),
    )(*held)
    return tuple(x.reshape(V, L, ny, nx) for x in done)


def solution(mesh):
    field = P(None, None, "row", "col")
    tile = P(("row", "col"))
    in_specs = (
        field, field, field, P(None, None, None, "row", "col"),
        P(), P(), P(), P(), tile, tile, tile,
    )
    return jax.shard_map(
        functools.partial(local, mesh.shape["row"], mesh.shape["col"]),
        mesh=mesh, in_specs=in_specs, out_specs=(field,) * 3, check_vma=False,
    )
```

```python
import functools

import jax
import jax.numpy as jnp
from jax import lax
from jax.experimental import pallas as pl
from jax.experimental.pallas import tpu as pltpu
from jax.sharding import PartitionSpec as P

MESH = pl.DeviceIdType.MESH
f32 = jnp.float32
bf16 = jnp.bfloat16
CHUNK = 32
GRAM = 960
PARTS = 5


def kernel(
    R, C, V, L, M, K, ny, nx,
    cnt_hbm, dir_hbm, len_e_hbm, len_n_hbm, vm_hbm, amp_hbm, cell_hbm, wgt_hbm,
    res_hbm, inc_hbm, lz_hbm,
    tot_ref, res_ref, inc_ref, dir_ref, img_ref, lz_ref,
    cnt_ref, len_ref, vm_ref, amp_ref, cell_ref, wgt_ref,
    east_ref, north_ref, end_ref, start_ref, mix_ref, comb_ref, both_ref,
    lead_ref, pair_ref, hot_ref, near_ref, sel_ref, rest_ref,
    es_ref, er_ref, ns_ref, nr_ref, cs_ref, cr_ref, rs_ref, rr_ref,
    load_sem, e_ssem, e_rsem, n_ssem, n_rsem, c_ssem, c_rsem, r_ssem, r_rsem,
):
    N = R * C
    I = V * M
    row, col = lax.axis_index("row"), lax.axis_index("col")
    me = row * C + col
    barrier = pltpu.get_barrier_semaphore()

    def place(d):
        peer = lax.rem(me + d, N)
        return (lax.div(peer, C), lax.rem(peer, C))

    def greet(d, carry):
        pl.semaphore_signal(barrier, inc=1, device_id=place(d), device_id_type=MESH)
        return carry

    plane = L * ny
    lead_rows = M * ny
    rest = L - M
    firsts = [
        pltpu.make_async_copy(len_e_hbm, len_ref.at[0], load_sem.at[3]),
        pltpu.make_async_copy(len_n_hbm, len_ref.at[1], load_sem.at[4]),
    ]
    others = [
        pltpu.make_async_copy(cell_hbm, cell_ref, load_sem.at[5]),
        pltpu.make_async_copy(wgt_hbm, wgt_ref, load_sem.at[6]),
        pltpu.make_async_copy(vm_hbm, vm_ref, load_sem.at[7]),
        pltpu.make_async_copy(amp_hbm, amp_ref, load_sem.at[8]),
        pltpu.make_async_copy(cnt_hbm, cnt_ref, load_sem.at[9 + 2 * V]),
    ]
    leads = []
    for v in range(V):
        part = pl.ds(v * plane, lead_rows)
        leads.append(
            pltpu.make_async_copy(dir_hbm.at[part], dir_ref.at[part], load_sem.at[9 + v])
        )
        part = pl.ds(v * plane + lead_rows, plane - lead_rows)
        others.append(
            pltpu.make_async_copy(dir_hbm.at[part], dir_ref.at[part], load_sem.at[9 + V + v])
        )
    loads = [
        pltpu.make_async_copy(res_hbm, res_ref, load_sem.at[0]),
        pltpu.make_async_copy(lz_hbm, lz_ref, load_sem.at[1]),
        pltpu.make_async_copy(inc_hbm, inc_ref, load_sem.at[2]),
    ]
    for load in firsts + leads + others + loads:
        load.start()
    lax.fori_loop(1, N, greet, 0)
    for load in firsts:
        load.wait()

    lane = lax.broadcasted_iota(jnp.int32, (ny, nx), 1)
    sub = lax.broadcasted_iota(jnp.int32, (ny, nx), 0)
    east_at, north_at = lane.astype(f32), sub.astype(f32)
    inst_lane = lane & (I - 1)
    is_back = (lane & I) != 0
    is_late = lane >= 2 * I
    log_e = jnp.zeros((ny, nx), f32)
    log_n = jnp.zeros((ny, nx), f32)
    for i in range(I):
        v, m = i // M, i % M
        rows = slice(i * ny, (i + 1) * ny)
        e = -1.0 / (jnp.broadcast_to(len_ref[0, v : v + 1, m : m + 1], (ny, nx)) * float(nx))
        n = -1.0 / (jnp.broadcast_to(len_ref[1, v : v + 1, m : m + 1], (ny, nx)) * float(ny))
        log_e = jnp.where(inst_lane == i, e, log_e)
        log_n = jnp.where(inst_lane == i, n, log_n)
        east_ref[rows, :] = e
        north_ref[rows, :] = n
        end_ref[0, rows, :] = jnp.exp(e * (float(nx - 1) - east_at))
        start_ref[0, rows, :] = jnp.exp(e * east_at)
        end_ref[1, rows, :] = jnp.exp(n * (float(ny - 1) - north_at))
        start_ref[1, rows, :] = jnp.exp(n * north_at)
    corner_w = jnp.exp(log_n * jnp.where(is_late, north_at, float(ny - 1) - north_at))

    def every_sub(x):
        shift = ny // 2
        while shift:
            x = x + pltpu.roll(x, shift, 0)
            shift //= 2
        return x

    def split(x):
        high = x.astype(bf16)
        return high, (x - high.astype(f32)).astype(bf16)

    def begin(u, inst):
        for i in range(I):
            rows = slice(i * ny, (i + 1) * ny)
            pair_ref[0, rows, :] = every_sub(u[rows] * end_ref[1, rows, :])
            pair_ref[1, rows, :] = every_sub(u[rows] * start_ref[1, rows, :])
        ns_ref[inst, 0:I] = pair_ref[0, pl.ds(0, I, stride=ny), :]
        ns_ref[inst, I : 2 * I] = pair_ref[1, pl.ds(0, I, stride=ny), :]
        moment = jnp.zeros((ny, nx), f32)
        for i in range(I):
            rows = slice(i * ny, (i + 1) * ny)
            e = jnp.sum(u[rows] * end_ref[0, rows, :], axis=1, keepdims=True)
            b = jnp.sum(u[rows] * start_ref[0, rows, :], axis=1, keepdims=True)
            moment = jnp.where(inst_lane == i, jnp.where(is_back, b, e), moment)
        es_ref[inst] = moment
        cs_ref[inst] = every_sub(moment * corner_w)[0:1]

    def launch(inst):
        for d in range(1, R):
            pltpu.make_async_remote_copy(
                src_ref=ns_ref.at[inst],
                dst_ref=nr_ref.at[inst, d],
                send_sem=n_ssem.at[inst, d],
                recv_sem=n_rsem.at[inst, d],
                device_id=(lax.rem(row + d, R), col),
                device_id_type=MESH,
            ).start()

        def go(over, carry):
            for along in range(C):
                pltpu.make_async_remote_copy(
                    src_ref=cs_ref.at[inst],
                    dst_ref=cr_ref.at[inst, over, pl.ds(along, 1)],
                    send_sem=c_ssem.at[inst, over],
                    recv_sem=c_rsem.at[inst, over],
                    device_id=(lax.rem(row + over, R), lax.rem(col + along, C)),
                    device_id_type=MESH,
                ).start()
            return carry

        lax.fori_loop(1, R, go, 0)
        for d in range(1, C):
            pltpu.make_async_remote_copy(
                src_ref=es_ref.at[inst],
                dst_ref=er_ref.at[inst, d],
                send_sem=e_ssem.at[inst, d],
                recv_sem=e_rsem.at[inst, d],
                device_id=(row, lax.rem(col + d, C)),
                device_id_type=MESH,
            ).start()

    def arrival(inst, kind, d):
        src, dst, send, recv = (
            (ns_ref.at[inst], nr_ref.at[inst, d], n_ssem, n_rsem),
            (es_ref.at[inst], er_ref.at[inst, d], e_ssem, e_rsem),
            (cr_ref.at[inst, d], cr_ref.at[inst, d], c_ssem, c_rsem),
        )[kind]
        return pltpu.make_async_remote_copy(
            src_ref=src, dst_ref=dst, send_sem=send.at[inst, d], recv_sem=recv.at[inst, d],
            device_id=(row, lax.rem(col + 1, C)), device_id_type=MESH,
        )

    def scans(u, log_alpha, axis, size, at):
        power = jnp.exp(log_alpha)
        f, g = u, u
        shift = 1
        while shift < size:
            f = f + power * jnp.where(at >= shift, pltpu.roll(f, shift, axis), 0.0)
            g = g + power * jnp.where(at < size - shift, pltpu.roll(g, size - shift, axis), 0.0)
            power = power * power
            shift *= 2
        return f + g - u

    def inside(u):
        u = u.reshape(I, ny, nx)
        u = scans(u, east_ref[...].reshape(I, ny, nx), 2, nx, lane[None])
        u = scans(u, north_ref[...].reshape(I, ny, nx), 1, ny, sub[None])
        lead_ref[...] = both_ref[0] * u.reshape(I * ny, nx)

    def weights(log_small, d, index, count, size):
        at = index.astype(f32)
        far = d > index
        source = jnp.where(far, index - d + count, index - d).astype(f32)
        step = d.astype(f32)
        left = jnp.where(
            far | (d == 0), 0.0, jnp.exp(log_small * (float(size) * jnp.maximum(step - 1.0, 0.0)))
        )
        right = jnp.where(
            far, jnp.exp(log_small * (float(size) * (float(count - 1) - step))), 0.0
        )
        edge = jnp.exp(
            log_small * (float(size) * (float(2 * count - 2) - at - source) + 1.0)
        )
        return left, right, edge

    def finish(inst):
        for d in range(1, R):
            arrival(inst, 0, d).wait_recv()
        left, right, edge = north_w[0]
        p = jnp.zeros((I, nx), f32)
        q = -edge * ns_ref[inst, 0:I]
        for d in range(1, R):
            left, right, edge = north_w[d]
            p += left * nr_ref[inst, d, 0:I]
            q += right * nr_ref[inst, d, I : 2 * I] - edge * nr_ref[inst, d, 0:I]
        line = jnp.concatenate([p, q], axis=0)
        comb_ref[...] = scans(
            line, log_lines, 1, nx, lax.broadcasted_iota(jnp.int32, (2 * I, nx), 1)
        )
        for i in range(I):
            rows = slice(i * ny, (i + 1) * ny)
            lead_ref[rows, :] += (
                both_ref[1, rows, :] * jnp.broadcast_to(comb_ref[i : i + 1, :], (ny, nx))
                + both_ref[2, rows, :] * jnp.broadcast_to(comb_ref[I + i : I + i + 1, :], (ny, nx))
            )
        for d in range(1, C):
            arrival(inst, 1, d).wait_recv()
        ahead = jnp.zeros((ny, nx), f32)
        echo = col_edge[0:1] * es_ref[inst]
        for d in range(1, C):
            ahead += col_main[d : d + 1] * er_ref[inst, d]
            echo += col_edge[d : d + 1] * er_ref[inst, d]
        lines = ahead - pltpu.roll(echo, I, 1)
        settled = scans(lines, log_n, 0, ny, sub)
        for d in range(1, R):
            arrival(inst, 2, d).wait_recv()
        first = corner_w * lines
        ahead = row_main[0] * first
        echo = row_edge[0] * first
        for d in range(1, R):
            got = cr_ref[inst, d]
            got = col_main * got - pltpu.roll(col_edge * got, I, 1)
            got = jnp.sum(got.reshape(C // ny, ny, nx), axis=0)
            ahead += row_main[d] * got
            echo += row_edge[d] * got
        corner = every_sub(ahead - pltpu.roll(echo, 2 * I, 1))
        settled = lane_scale * (
            settled + lane_low * corner + lane_high * pltpu.roll(corner, 2 * I, 1)
        )
        for i in range(I):
            rows = slice(i * ny, (i + 1) * ny)
            x = jnp.broadcast_to(settled[:, i : i + 1], (ny, nx))
            y = jnp.broadcast_to(settled[:, I + i : I + i + 1], (ny, nx))
            lead_ref[rows, :] += both_ref[3, rows, :] * x + both_ref[4, rows, :] * y

    for load in leads:
        load.wait()
    u = jnp.concatenate([dir_ref[v * plane : v * plane + M * ny, :] for v in range(V)], axis=0)
    begin(u, 0)
    pl.semaphore_wait(barrier, N - 1)
    launch(0)

    alpha_e, alpha_n = jnp.exp(log_e), jnp.exp(log_n)
    lane_scale = jnp.sqrt(
        ((1.0 - alpha_e) / (1.0 + alpha_e)) * ((1.0 - alpha_n) / (1.0 + alpha_n))
    )
    lane_low = jnp.exp(log_n * (north_at + 1.0))
    lane_high = jnp.exp(log_n * (float(ny) - north_at))
    over = lax.broadcasted_iota(jnp.int32, (C, nx), 0)
    odd = (lax.broadcasted_iota(jnp.int32, (C, nx), 1) & I) != 0
    low, high, edge = weights(jnp.broadcast_to(log_e[0:1], (C, nx)), over, col, C, nx)
    col_main = jnp.where(odd, high, low)
    col_edge = jnp.where(odd, 0.0, edge)
    row_main, row_edge, north_w = [], [], []
    log_rows = north_ref[pl.ds(0, I, stride=ny), :]
    for d in range(R):
        step = jnp.full((ny, nx), d, jnp.int32)
        low, high, edge = weights(log_n, step, row, R, ny)
        row_main.append(jnp.where(is_late, high, low))
        row_edge.append(jnp.where(is_late, 0.0, edge))
        north_w.append(weights(log_rows, jnp.full((I, nx), d, jnp.int32), row, R, ny))
    log_lines = east_ref[pl.ds(0, I, stride=ny), :]
    log_lines = jnp.concatenate([log_lines, log_lines], axis=0)
    for i in range(I):
        rows = slice(i * ny, (i + 1) * ny)
        a, b = jnp.exp(east_ref[rows, :]), jnp.exp(north_ref[rows, :])
        scale = jnp.sqrt(((1.0 - a) / (1.0 + a)) * ((1.0 - b) / (1.0 + b)))
        both_ref[0, rows, :] = scale
        both_ref[1, rows, :] = scale * b * start_ref[1, rows, :]
        both_ref[2, rows, :] = scale * b * end_ref[1, rows, :]
        both_ref[3, rows, :] = a * start_ref[0, rows, :]
        both_ref[4, rows, :] = a * end_ref[0, rows, :]
    inside(u)
    for load in others:
        load.wait()

    pad = (L + 15) // 16 * 16
    cell = cell_ref[...]
    slots = cell.shape[1]
    level = lax.shift_right_logical(cell, (ny * nx).bit_length() - 1)
    spot = cell & (ny * nx - 1)
    spot_x = spot & (nx - 1)
    spot_y = lax.shift_right_logical(spot, nx.bit_length() - 1)
    hot_ref[...] = jnp.where(
        lax.broadcasted_iota(jnp.int32, (ny * nx, slots), 0) == spot, 1.0, 0.0
    ).astype(bf16)
    near = jnp.where(
        lax.broadcasted_iota(jnp.int32, (nx, slots), 0) == spot_x, 1.0, 0.0
    ).astype(bf16)
    near_ref[0:nx] = near
    near_ref[nx : 2 * nx] = near
    live = lax.broadcasted_iota(jnp.int32, (1, slots), 1) < cnt_ref[...]
    weight = jnp.where(live, wgt_ref[...], 0.0)
    mix_ref[...] = jnp.zeros_like(mix_ref)
    at = lax.broadcasted_iota(jnp.int32, (pad, slots), 0)
    here = lax.broadcasted_iota(jnp.int32, (ny, slots), 0) == spot_y
    hold = pad - M
    for v in range(V):
        mix_ref[v, 0:L, 0:L] = vm_ref[:, v, :] * amp_ref[v : v + 1, :]
        left = mix_ref[v].T[0:pad, 0:pad]
        parts = []
        for _ in range(3):
            part = left.astype(bf16)
            parts.append(part)
            left = left - part.astype(f32)
        hit = jnp.where((at + v * L == level) & (at < L), 1.0, 0.0).astype(bf16)
        chosen = jnp.dot(jnp.concatenate(parts, axis=0), hit, preferred_element_type=f32)
        chosen = chosen[0:pad] + chosen[pad : 2 * pad] + chosen[2 * pad : 3 * pad]
        rest_ref[v * hold : (v + 1) * hold] = chosen[M:pad]
        for m in range(M):
            i = v * M + m
            sel_ref[i * ny : (i + 1) * ny] = jnp.where(
                here, jnp.broadcast_to(chosen[m : m + 1], (ny, slots)), 0.0
            )

    spare = jnp.zeros((hold - rest, nx), f32)
    held = jnp.concatenate(
        [
            jnp.concatenate(
                [
                    x
                    for v in range(V)
                    for x in (
                        dir_ref[pl.ds(v * plane + lead_rows + y, rest, stride=ny), :], spare
                    )
                ],
                axis=0,
            )
            for y in range(ny)
        ],
        axis=1,
    )
    seen = jnp.dot(
        jnp.concatenate(split(held), axis=0), hot_ref[...], preferred_element_type=f32
    )
    seen = seen[0 : V * hold] + seen[V * hold :]
    beside = jnp.sum(seen * rest_ref[...], axis=0, keepdims=True)

    loads[0].wait()
    loads[1].wait()
    square = jnp.zeros((8, nx), f32)
    table = jnp.zeros(((K + 2) * 16, K * 16), f32)
    for s in range(V * plane // GRAM):
        r = res_ref[s * GRAM : (s + 1) * GRAM, :]
        square += jnp.sum((r * r).reshape(GRAM // 8, 8, nx), axis=0)
        high, low = split(r)
        wide, tall = [], []
        for n in range(GRAM // 16):
            rows = slice(s * GRAM + n * 16, s * GRAM + (n + 1) * 16)
            block = lz_ref[:, rows, :].reshape(K * 16, nx)
            wide.append(block)
            part = slice(n * 16, (n + 1) * 16)
            tall.append(jnp.concatenate([block, high[part], low[part]], axis=0))
        table += lax.dot_general(
            jnp.concatenate(tall, axis=1), jnp.concatenate(wide, axis=1),
            (((1,), (1,)), ((), ())), preferred_element_type=f32,
        )
    at_row = lax.broadcasted_iota(jnp.int32, table.shape, 0)
    at_col = lax.broadcasted_iota(jnp.int32, table.shape, 1)
    kept = jnp.where((at_row & 15) == (at_col & 15), table, 0.0)
    kept = jnp.sum(kept.reshape(K + 2, 16, K * 16), axis=1)
    kept = jnp.concatenate(
        [kept[0:K], kept[K : K + 1] + kept[K + 1 : K + 2], jnp.zeros((15 - K, K * 16), f32)],
        axis=0,
    )
    which_k = lax.shift_right_logical(lax.broadcasted_iota(jnp.int32, (K * 16, nx), 0), 4)
    in_lane = lax.broadcasted_iota(jnp.int32, (K * 16, nx), 1)
    pick = jnp.zeros((K * 16, nx), f32)
    for j in range(K + 1):
        pick = jnp.where(in_lane == which_k + j * K, 1.0, pick)
    spread_out = jnp.dot(
        kept, pick, preferred_element_type=f32, precision=lax.Precision.HIGHEST
    )
    g_lane = lax.broadcasted_iota(jnp.int32, (16, nx), 1)
    g_row = lax.broadcasted_iota(jnp.int32, (16, nx), 0)
    own_row = (g_lane >= g_row * K) & (g_lane < (g_row + 1) * K) & (g_row <= K)
    gram_row = jnp.sum(jnp.where(own_row, spread_out, 0.0), axis=0, keepdims=True)

    finish(0)

    high, low = split(lead_ref[...])
    seen = jnp.dot(
        jnp.concatenate([high, low], axis=1), near_ref[...], preferred_element_type=f32
    )
    grid = jnp.sum(seen * sel_ref[...], axis=0, keepdims=True) + beside
    weighted = weight * grid
    high, low = split(sel_ref[...] * weighted)
    across = (((1,), (1,)), ((), ()))
    u = lax.dot_general(high, near_ref[0:nx], across, preferred_element_type=f32)
    u += lax.dot_general(low, near_ref[0:nx], across, preferred_element_type=f32)
    begin(u, 1)
    launch(1)

    inside(u)
    back = lax.dot_general(
        jnp.concatenate(split(rest_ref[...] * weighted), axis=0), hot_ref[...], across,
        preferred_element_type=f32,
    )
    back = back[0 : V * hold] + back[V * hold :]
    for v in range(V):
        for y in range(ny):
            img_ref[pl.ds(v * plane + lead_rows + y, rest, stride=ny), :] = back[
                v * hold : v * hold + rest, y * nx : (y + 1) * nx
            ]

    def fold(x):
        return jnp.sum(x.reshape(CHUNK // 8, 8, nx), axis=0)

    zero = jnp.zeros((8, nx), f32)

    def image_dots(base, mine, carry):
        rows = pl.ds(base, CHUNK)
        d = dir_ref[rows, :]
        image = d + mine
        img_ref[rows, :] = image
        r = res_ref[rows, :]
        out = [
            carry[0] + fold(r * image), carry[1] + fold(image * image), carry[2] + fold(d * image)
        ]
        for k in range(K):
            out.append(carry[k + 3] + fold(image * lz_ref[k, rows, :].astype(f32)))
        return tuple(out)

    turns = (plane - lead_rows) // CHUNK

    def rest_dots(s, carry):
        base = lax.div(s, turns) * plane + lead_rows + lax.rem(s, turns) * CHUNK
        base = pl.multiple_of(base, CHUNK)
        return image_dots(base, img_ref[pl.ds(base, CHUNK), :], carry)

    img_dots = lax.fori_loop(0, V * turns, rest_dots, (zero,) * (K + 3), unroll=2)
    finish(1)
    short = lead_rows // CHUNK

    def lead_dots(s, carry):
        base = pl.multiple_of(lax.div(s, short) * plane + lax.rem(s, short) * CHUNK, CHUNK)
        mine = lead_ref[pl.ds(pl.multiple_of(s * CHUNK, CHUNK), CHUNK), :]
        return image_dots(base, mine, carry)

    img_dots = lax.fori_loop(0, V * short, lead_dots, img_dots, unroll=2)

    def reduce_copy(over, along):
        return pltpu.make_async_remote_copy(
            src_ref=rs_ref,
            dst_ref=rr_ref.at[pl.ds(over * C + along, 1)],
            send_sem=r_ssem.at[0],
            recv_sem=r_rsem.at[0],
            device_id=(lax.rem(row + over, R), lax.rem(col + along, C)),
            device_id_type=MESH,
        )

    sums = list(img_dots[3:]) + [square] + list(img_dots[:3])
    rows = [jnp.zeros((K * K + K, nx), f32)] + [jnp.sum(x, axis=0, keepdims=True) for x in sums]
    rows.append(jnp.zeros((nx - K * K - K - len(sums), nx), f32))
    packed = jnp.sum(jnp.concatenate(rows, axis=0).T, axis=0, keepdims=True)
    rs_ref[...] = packed + gram_row

    def go(over, carry):
        for along in range(C):
            reduce_copy(over, along).start()
        return carry

    lax.fori_loop(1, R, go, 0)
    for along in range(1, C):
        reduce_copy(0, along).start()
    loads[2].wait()
    every = pltpu.make_async_remote_copy(
        src_ref=rr_ref.at[pl.ds(1, N - 1)],
        dst_ref=rr_ref.at[pl.ds(1, N - 1)],
        send_sem=r_ssem.at[0],
        recv_sem=r_rsem.at[0],
        device_id=(row, lax.rem(col + 1, C)),
        device_id_type=MESH,
    )
    every.wait_recv()
    every.wait_send()
    rr_ref[pl.ds(0, 1)] = rs_ref[...]
    tot_ref[...] = jnp.broadcast_to(jnp.sum(rr_ref[...], axis=0, keepdims=True), (8, nx))
    for inst in range(2):
        for d in range(1, R):
            arrival(inst, 0, d).wait_send()
            arrival(inst, 2, d).wait_send()
        for d in range(1, C):
            arrival(inst, 1, d).wait_send()


def update(
    K, total_cells, parts,
    tot_ref, res_ref, inc_ref, dir_ref, img_ref, lz_ref, oinc_hbm, ores_hbm, odir_hbm,
    oinc_ref, ores_ref, odir_ref, sem,
):
    flat, nx = res_ref.shape
    totals = tot_ref[0:1, :]
    lane = lax.broadcasted_iota(jnp.int32, (1, nx), 1)

    def total(n):
        return totals[:, n : n + 1]

    first = K * K
    rr, ri, ii, di = (total(first + 2 * K + n) for n in range(4))
    step_size = rr / di
    moments = [total(first + k) - step_size * total(first + K + k) for k in range(K)]
    left, right = jnp.zeros((1, nx), f32), jnp.zeros((1, nx), f32)
    for j in range(K):
        left = jnp.where((lane >= j * K) & (lane < (j + 1) * K), moments[j], left)
    single = jnp.zeros((1, nx), f32)
    for k in range(K):
        hit = lane == k
        for j in range(1, K):
            hit = hit | (lane == j * K + k)
        right = jnp.where(hit, moments[k], right)
        single = jnp.where(lane == k, moments[k], single)
    squares = jnp.sum(left * right * totals, axis=1, keepdims=True)
    crossed = jnp.sum(single * single, axis=1, keepdims=True)
    moved_norm = rr + step_size * (step_size * ii - 2.0 * ri)
    norm_new = moved_norm + (squares / total_cells - 2.0 * crossed) / total_cells
    coefficient = [jnp.broadcast_to(x / total_cells, (CHUNK, nx)) for x in moments]
    step_wide = jnp.broadcast_to(step_size, (CHUNK, nx))
    ratio = jnp.broadcast_to(norm_new / rr, (CHUNK, nx))
    size = flat // parts
    copies = []
    for part in range(parts):

        def advance(s, carry):
            rows = pl.ds(pl.multiple_of(part * size + s * CHUNK, CHUNK), CHUNK)
            d = dir_ref[rows, :]
            new = res_ref[rows, :] - step_wide * img_ref[rows, :]
            for k in range(K):
                new = new - coefficient[k] * lz_ref[k, rows, :].astype(f32)
            oinc_ref[rows, :] = inc_ref[rows, :] + step_wide * d
            ores_ref[rows, :] = new
            odir_ref[rows, :] = new + ratio * d
            return carry

        lax.fori_loop(0, size // CHUNK, advance, 0, unroll=2)
        rows = pl.ds(part * size, size)
        for n, (src, dst) in enumerate(
            ((oinc_ref, oinc_hbm), (ores_ref, ores_hbm), (odir_ref, odir_hbm))
        ):
            copies.append(pltpu.make_async_copy(src.at[rows], dst.at[rows], sem.at[part, n]))
            copies[-1].start()
    for copy in copies:
        copy.wait()


def local(
    R, C,
    increment, residual, direction, lanczos, vertical_modes, amplitude,
    length_east, length_north, observed_cell, observed_weight, observed_count,
):
    V, L, ny, nx = direction.shape
    M = length_east.shape[1]
    K = lanczos.shape[0]
    I = V * M
    N = R * C
    flat = V * L * ny
    slots = observed_cell.shape[0]
    pad = (L + 15) // 16 * 16
    hbm = pl.BlockSpec(memory_space=pltpu.HBM)
    near = pl.BlockSpec(memory_space=pltpu.VMEM)
    field = pltpu.VMEM((flat, nx), f32)
    lead = pltpu.VMEM((I * ny, nx), f32)
    held = pl.pallas_call(
        functools.partial(kernel, R, C, V, L, M, K, ny, nx),
        out_shape=(pltpu.VMEM((8, nx), f32),) + (field,) * 4 + (pltpu.VMEM((K, flat, nx), bf16),),
        in_specs=[hbm] * 11,
        out_specs=(near,) * 6,
        scratch_shapes=[
            pltpu.VMEM((1, 1), jnp.int32),
            pltpu.VMEM((2, V, M), f32), pltpu.VMEM((L, V, L), f32),
            pltpu.VMEM((V, L), f32), pltpu.VMEM((1, slots), jnp.int32), pltpu.VMEM((1, slots), f32),
            lead, lead, pltpu.VMEM((2, I * ny, nx), f32), pltpu.VMEM((2, I * ny, nx), f32),
            pltpu.VMEM((V, 2 * pad, 2 * pad), f32),
            pltpu.VMEM((2 * I, nx), f32), pltpu.VMEM((5, I * ny, nx), f32),
            lead, pltpu.VMEM((2, I * ny, nx), f32),
            pltpu.VMEM((ny * nx, slots), bf16), pltpu.VMEM((2 * nx, slots), bf16),
            pltpu.VMEM((I * ny, slots), f32), pltpu.VMEM((V * (pad - M), slots), f32),
            pltpu.VMEM((2, ny, nx), f32), pltpu.VMEM((2, C, ny, nx), f32),
            pltpu.VMEM((2, 2 * I, nx), f32), pltpu.VMEM((2, R, 2 * I, nx), f32),
            pltpu.VMEM((2, 1, nx), f32), pltpu.VMEM((2, R, C, nx), f32),
            pltpu.VMEM((1, nx), f32), pltpu.VMEM((N, nx), f32),
            pltpu.SemaphoreType.DMA((10 + 2 * V,)),
            pltpu.SemaphoreType.DMA((2, C)), pltpu.SemaphoreType.DMA((2, C)),
            pltpu.SemaphoreType.DMA((2, R)), pltpu.SemaphoreType.DMA((2, R)),
            pltpu.SemaphoreType.DMA((2, R)), pltpu.SemaphoreType.DMA((2, R)),
            pltpu.SemaphoreType.DMA((1,)), pltpu.SemaphoreType.DMA((1,)),
        ],
        compiler_params=pltpu.CompilerParams(
            collective_id=0, has_side_effects=True, vmem_limit_bytes=54 * 2**20
        ),
    )(
        observed_count.reshape(1, 1), direction.reshape(flat, nx), length_east, length_north,
        jnp.transpose(vertical_modes, (1, 0, 2)), amplitude,
        observed_cell.reshape(1, slots), observed_weight.reshape(1, slots),
        residual.reshape(flat, nx), increment.reshape(flat, nx), lanczos.reshape(K, flat, nx),
    )
    done = pl.pallas_call(
        functools.partial(update, K, float(flat * nx * N), PARTS),
        out_shape=(jax.ShapeDtypeStruct((flat, nx), f32),) * 3,
        in_specs=[near] * 6,
        out_specs=(hbm,) * 3,
        scratch_shapes=[
            pltpu.VMEM((flat, nx), f32), pltpu.VMEM((flat, nx), f32), pltpu.VMEM((flat, nx), f32),
            pltpu.SemaphoreType.DMA((PARTS, 3)),
        ],
        compiler_params=pltpu.CompilerParams(vmem_limit_bytes=16 * 2**20),
    )(*held)
    return tuple(x.reshape(V, L, ny, nx) for x in done)


def solution(mesh):
    field = P(None, None, "row", "col")
    tile = P(("row", "col"))
    in_specs = (
        field, field, field, P(None, None, None, "row", "col"),
        P(), P(), P(), P(), tile, tile, tile,
    )
    return jax.shard_map(
        functools.partial(local, mesh.shape["row"], mesh.shape["col"]),
        mesh=mesh, in_specs=in_specs, out_specs=(field,) * 3, check_vma=False,
    )
```

```python
import functools

import jax
import jax.numpy as jnp
from jax import lax
from jax.experimental import pallas as pl
from jax.experimental.pallas import tpu as pltpu
from jax.sharding import PartitionSpec as P

MESH = pl.DeviceIdType.MESH
f32 = jnp.float32
bf16 = jnp.bfloat16
CHUNK = 32
PARTS = 5


def kernel(
    R, C, V, L, M, K, ny, nx,
    cnt_hbm, dir_hbm, len_e_hbm, len_n_hbm, vm_hbm, amp_hbm, cell_hbm, wgt_hbm,
    res_hbm, inc_hbm, lz_hbm,
    tot_ref, res_ref, inc_ref, dir_ref, img_ref, lz_ref,
    cnt_ref, len_ref, vm_ref, amp_ref, cell_ref, wgt_ref,
    east_ref, north_ref, end_ref, start_ref, mix_ref, comb_ref, both_ref,
    lead_ref, pair_ref, hot_ref, near_ref, sel_ref, rest_ref,
    es_ref, er_ref, ns_ref, nr_ref, cs_ref, cr_ref, rs_ref, rr_ref,
    load_sem, e_ssem, e_rsem, n_ssem, n_rsem, c_ssem, c_rsem, r_ssem, r_rsem,
):
    N = R * C
    I = V * M
    row, col = lax.axis_index("row"), lax.axis_index("col")
    me = row * C + col
    barrier = pltpu.get_barrier_semaphore()

    def place(d):
        peer = lax.rem(me + d, N)
        return (lax.div(peer, C), lax.rem(peer, C))

    def greet(d, carry):
        pl.semaphore_signal(barrier, inc=1, device_id=place(d), device_id_type=MESH)
        return carry

    plane = L * ny
    lead_rows = M * ny
    rest = L - M
    firsts = [
        pltpu.make_async_copy(len_e_hbm, len_ref.at[0], load_sem.at[3]),
        pltpu.make_async_copy(len_n_hbm, len_ref.at[1], load_sem.at[4]),
    ]
    others = [
        pltpu.make_async_copy(cell_hbm, cell_ref, load_sem.at[5]),
        pltpu.make_async_copy(wgt_hbm, wgt_ref, load_sem.at[6]),
        pltpu.make_async_copy(vm_hbm, vm_ref, load_sem.at[7]),
        pltpu.make_async_copy(amp_hbm, amp_ref, load_sem.at[8]),
        pltpu.make_async_copy(cnt_hbm, cnt_ref, load_sem.at[9 + 2 * V]),
    ]
    leads = []
    for v in range(V):
        part = pl.ds(v * plane, lead_rows)
        leads.append(
            pltpu.make_async_copy(dir_hbm.at[part], dir_ref.at[part], load_sem.at[9 + v])
        )
        part = pl.ds(v * plane + lead_rows, plane - lead_rows)
        others.append(
            pltpu.make_async_copy(dir_hbm.at[part], dir_ref.at[part], load_sem.at[9 + V + v])
        )
    loads = [
        pltpu.make_async_copy(res_hbm, res_ref, load_sem.at[0]),
        pltpu.make_async_copy(lz_hbm, lz_ref, load_sem.at[1]),
        pltpu.make_async_copy(inc_hbm, inc_ref, load_sem.at[2]),
    ]
    for load in firsts + leads + others + loads:
        load.start()
    lax.fori_loop(1, N, greet, 0)
    for load in firsts:
        load.wait()

    lane = lax.broadcasted_iota(jnp.int32, (ny, nx), 1)
    sub = lax.broadcasted_iota(jnp.int32, (ny, nx), 0)
    east_at, north_at = lane.astype(f32), sub.astype(f32)
    inst_lane = lane & (I - 1)
    is_back = (lane & I) != 0
    is_late = lane >= 2 * I
    log_e = jnp.zeros((ny, nx), f32)
    log_n = jnp.zeros((ny, nx), f32)
    for i in range(I):
        v, m = i // M, i % M
        rows = slice(i * ny, (i + 1) * ny)
        e = -1.0 / (jnp.broadcast_to(len_ref[0, v : v + 1, m : m + 1], (ny, nx)) * float(nx))
        n = -1.0 / (jnp.broadcast_to(len_ref[1, v : v + 1, m : m + 1], (ny, nx)) * float(ny))
        log_e = jnp.where(inst_lane == i, e, log_e)
        log_n = jnp.where(inst_lane == i, n, log_n)
        east_ref[rows, :] = e
        north_ref[rows, :] = n
        end_ref[0, rows, :] = jnp.exp(e * (float(nx - 1) - east_at))
        start_ref[0, rows, :] = jnp.exp(e * east_at)
        end_ref[1, rows, :] = jnp.exp(n * (float(ny - 1) - north_at))
        start_ref[1, rows, :] = jnp.exp(n * north_at)
    corner_w = jnp.exp(log_n * jnp.where(is_late, north_at, float(ny - 1) - north_at))

    def every_sub(x):
        shift = ny // 2
        while shift:
            x = x + pltpu.roll(x, shift, 0)
            shift //= 2
        return x

    def split(x):
        high = x.astype(bf16)
        return high, (x - high.astype(f32)).astype(bf16)

    def begin(u, inst):
        for i in range(I):
            rows = slice(i * ny, (i + 1) * ny)
            pair_ref[0, rows, :] = every_sub(u[rows] * end_ref[1, rows, :])
            pair_ref[1, rows, :] = every_sub(u[rows] * start_ref[1, rows, :])
        ns_ref[inst, 0:I] = pair_ref[0, pl.ds(0, I, stride=ny), :]
        ns_ref[inst, I : 2 * I] = pair_ref[1, pl.ds(0, I, stride=ny), :]
        moment = jnp.zeros((ny, nx), f32)
        for i in range(I):
            rows = slice(i * ny, (i + 1) * ny)
            e = jnp.sum(u[rows] * end_ref[0, rows, :], axis=1, keepdims=True)
            b = jnp.sum(u[rows] * start_ref[0, rows, :], axis=1, keepdims=True)
            moment = jnp.where(inst_lane == i, jnp.where(is_back, b, e), moment)
        es_ref[inst] = moment
        cs_ref[inst] = every_sub(moment * corner_w)[0:1]

    def launch(inst):
        for d in range(1, R):
            pltpu.make_async_remote_copy(
                src_ref=ns_ref.at[inst],
                dst_ref=nr_ref.at[inst, d],
                send_sem=n_ssem.at[inst, d],
                recv_sem=n_rsem.at[inst, d],
                device_id=(lax.rem(row + d, R), col),
                device_id_type=MESH,
            ).start()

        def go(over, carry):
            for along in range(C):
                pltpu.make_async_remote_copy(
                    src_ref=cs_ref.at[inst],
                    dst_ref=cr_ref.at[inst, over, pl.ds(along, 1)],
                    send_sem=c_ssem.at[inst, over],
                    recv_sem=c_rsem.at[inst, over],
                    device_id=(lax.rem(row + over, R), lax.rem(col + along, C)),
                    device_id_type=MESH,
                ).start()
            return carry

        lax.fori_loop(1, R, go, 0)
        for d in range(1, C):
            pltpu.make_async_remote_copy(
                src_ref=es_ref.at[inst],
                dst_ref=er_ref.at[inst, d],
                send_sem=e_ssem.at[inst, d],
                recv_sem=e_rsem.at[inst, d],
                device_id=(row, lax.rem(col + d, C)),
                device_id_type=MESH,
            ).start()

    def arrival(inst, kind, d):
        src, dst, send, recv = (
            (ns_ref.at[inst], nr_ref.at[inst, d], n_ssem, n_rsem),
            (es_ref.at[inst], er_ref.at[inst, d], e_ssem, e_rsem),
            (cr_ref.at[inst, d], cr_ref.at[inst, d], c_ssem, c_rsem),
        )[kind]
        return pltpu.make_async_remote_copy(
            src_ref=src, dst_ref=dst, send_sem=send.at[inst, d], recv_sem=recv.at[inst, d],
            device_id=(row, lax.rem(col + 1, C)), device_id_type=MESH,
        )

    def scans(u, log_alpha, axis, size, at):
        power = jnp.exp(log_alpha)
        f, g = u, u
        shift = 1
        while shift < size:
            f = f + power * jnp.where(at >= shift, pltpu.roll(f, shift, axis), 0.0)
            g = g + power * jnp.where(at < size - shift, pltpu.roll(g, size - shift, axis), 0.0)
            power = power * power
            shift *= 2
        return f + g - u

    def inside(u):
        u = u.reshape(I, ny, nx)
        u = scans(u, east_ref[...].reshape(I, ny, nx), 2, nx, lane[None])
        u = scans(u, north_ref[...].reshape(I, ny, nx), 1, ny, sub[None])
        lead_ref[...] = both_ref[0] * u.reshape(I * ny, nx)

    def weights(log_small, d, index, count, size):
        at = index.astype(f32)
        far = d > index
        source = jnp.where(far, index - d + count, index - d).astype(f32)
        step = d.astype(f32)
        left = jnp.where(
            far | (d == 0), 0.0, jnp.exp(log_small * (float(size) * jnp.maximum(step - 1.0, 0.0)))
        )
        right = jnp.where(
            far, jnp.exp(log_small * (float(size) * (float(count - 1) - step))), 0.0
        )
        edge = jnp.exp(
            log_small * (float(size) * (float(2 * count - 2) - at - source) + 1.0)
        )
        return left, right, edge

    def finish(inst):
        for d in range(1, R):
            arrival(inst, 0, d).wait_recv()
        left, right, edge = north_w[0]
        p = jnp.zeros((I, nx), f32)
        q = -edge * ns_ref[inst, 0:I]
        for d in range(1, R):
            left, right, edge = north_w[d]
            p += left * nr_ref[inst, d, 0:I]
            q += right * nr_ref[inst, d, I : 2 * I] - edge * nr_ref[inst, d, 0:I]
        line = jnp.concatenate([p, q], axis=0)
        comb_ref[...] = scans(
            line, log_lines, 1, nx, lax.broadcasted_iota(jnp.int32, (2 * I, nx), 1)
        )
        for i in range(I):
            rows = slice(i * ny, (i + 1) * ny)
            lead_ref[rows, :] += (
                both_ref[1, rows, :] * jnp.broadcast_to(comb_ref[i : i + 1, :], (ny, nx))
                + both_ref[2, rows, :] * jnp.broadcast_to(comb_ref[I + i : I + i + 1, :], (ny, nx))
            )
        for d in range(1, C):
            arrival(inst, 1, d).wait_recv()
        ahead = jnp.zeros((ny, nx), f32)
        echo = col_edge[0:1] * es_ref[inst]
        for d in range(1, C):
            ahead += col_main[d : d + 1] * er_ref[inst, d]
            echo += col_edge[d : d + 1] * er_ref[inst, d]
        lines = ahead - pltpu.roll(echo, I, 1)
        settled = scans(lines, log_n, 0, ny, sub)
        for d in range(1, R):
            arrival(inst, 2, d).wait_recv()
        first = corner_w * lines
        ahead = row_main[0] * first
        echo = row_edge[0] * first
        for d in range(1, R):
            got = cr_ref[inst, d]
            got = col_main * got - pltpu.roll(col_edge * got, I, 1)
            got = jnp.sum(got.reshape(C // ny, ny, nx), axis=0)
            ahead += row_main[d] * got
            echo += row_edge[d] * got
        corner = every_sub(ahead - pltpu.roll(echo, 2 * I, 1))
        settled = lane_scale * (
            settled + lane_low * corner + lane_high * pltpu.roll(corner, 2 * I, 1)
        )
        for i in range(I):
            rows = slice(i * ny, (i + 1) * ny)
            x = jnp.broadcast_to(settled[:, i : i + 1], (ny, nx))
            y = jnp.broadcast_to(settled[:, I + i : I + i + 1], (ny, nx))
            lead_ref[rows, :] += both_ref[3, rows, :] * x + both_ref[4, rows, :] * y

    for load in leads:
        load.wait()
    u = jnp.concatenate([dir_ref[v * plane : v * plane + M * ny, :] for v in range(V)], axis=0)
    begin(u, 0)
    pl.semaphore_wait(barrier, N - 1)
    launch(0)

    alpha_e, alpha_n = jnp.exp(log_e), jnp.exp(log_n)
    lane_scale = jnp.sqrt(
        ((1.0 - alpha_e) / (1.0 + alpha_e)) * ((1.0 - alpha_n) / (1.0 + alpha_n))
    )
    lane_low = jnp.exp(log_n * (north_at + 1.0))
    lane_high = jnp.exp(log_n * (float(ny) - north_at))
    over = lax.broadcasted_iota(jnp.int32, (C, nx), 0)
    odd = (lax.broadcasted_iota(jnp.int32, (C, nx), 1) & I) != 0
    low, high, edge = weights(jnp.broadcast_to(log_e[0:1], (C, nx)), over, col, C, nx)
    col_main = jnp.where(odd, high, low)
    col_edge = jnp.where(odd, 0.0, edge)
    row_main, row_edge, north_w = [], [], []
    log_rows = north_ref[pl.ds(0, I, stride=ny), :]
    for d in range(R):
        step = jnp.full((ny, nx), d, jnp.int32)
        low, high, edge = weights(log_n, step, row, R, ny)
        row_main.append(jnp.where(is_late, high, low))
        row_edge.append(jnp.where(is_late, 0.0, edge))
        north_w.append(weights(log_rows, jnp.full((I, nx), d, jnp.int32), row, R, ny))
    log_lines = east_ref[pl.ds(0, I, stride=ny), :]
    log_lines = jnp.concatenate([log_lines, log_lines], axis=0)
    for i in range(I):
        rows = slice(i * ny, (i + 1) * ny)
        a, b = jnp.exp(east_ref[rows, :]), jnp.exp(north_ref[rows, :])
        scale = jnp.sqrt(((1.0 - a) / (1.0 + a)) * ((1.0 - b) / (1.0 + b)))
        both_ref[0, rows, :] = scale
        both_ref[1, rows, :] = scale * b * start_ref[1, rows, :]
        both_ref[2, rows, :] = scale * b * end_ref[1, rows, :]
        both_ref[3, rows, :] = a * start_ref[0, rows, :]
        both_ref[4, rows, :] = a * end_ref[0, rows, :]
    inside(u)
    for load in others:
        load.wait()

    pad = (L + 15) // 16 * 16
    cell = cell_ref[...]
    slots = cell.shape[1]
    level = lax.shift_right_logical(cell, (ny * nx).bit_length() - 1)
    spot = cell & (ny * nx - 1)
    spot_x = spot & (nx - 1)
    spot_y = lax.shift_right_logical(spot, nx.bit_length() - 1)
    hot_ref[...] = jnp.where(
        lax.broadcasted_iota(jnp.int32, (ny * nx, slots), 0) == spot, 1.0, 0.0
    ).astype(bf16)
    near = jnp.where(
        lax.broadcasted_iota(jnp.int32, (nx, slots), 0) == spot_x, 1.0, 0.0
    ).astype(bf16)
    near_ref[0:nx] = near
    near_ref[nx : 2 * nx] = near
    live = lax.broadcasted_iota(jnp.int32, (1, slots), 1) < cnt_ref[...]
    weight = jnp.where(live, wgt_ref[...], 0.0)
    mix_ref[...] = jnp.zeros_like(mix_ref)
    at = lax.broadcasted_iota(jnp.int32, (pad, slots), 0)
    here = lax.broadcasted_iota(jnp.int32, (ny, slots), 0) == spot_y
    hold = pad - M
    for v in range(V):
        mix_ref[v, 0:L, 0:L] = vm_ref[:, v, :] * amp_ref[v : v + 1, :]
        left = mix_ref[v].T[0:pad, 0:pad]
        parts = []
        for _ in range(3):
            part = left.astype(bf16)
            parts.append(part)
            left = left - part.astype(f32)
        hit = jnp.where((at + v * L == level) & (at < L), 1.0, 0.0).astype(bf16)
        chosen = jnp.dot(jnp.concatenate(parts, axis=0), hit, preferred_element_type=f32)
        chosen = chosen[0:pad] + chosen[pad : 2 * pad] + chosen[2 * pad : 3 * pad]
        rest_ref[v * hold : (v + 1) * hold] = chosen[M:pad]
        for m in range(M):
            i = v * M + m
            sel_ref[i * ny : (i + 1) * ny] = jnp.where(
                here, jnp.broadcast_to(chosen[m : m + 1], (ny, slots)), 0.0
            )

    spare = jnp.zeros((hold - rest, nx), f32)
    held = jnp.concatenate(
        [
            jnp.concatenate(
                [
                    x
                    for v in range(V)
                    for x in (
                        dir_ref[pl.ds(v * plane + lead_rows + y, rest, stride=ny), :], spare
                    )
                ],
                axis=0,
            )
            for y in range(ny)
        ],
        axis=1,
    )
    seen = jnp.dot(
        jnp.concatenate(split(held), axis=0), hot_ref[...], preferred_element_type=f32
    )
    seen = seen[0 : V * hold] + seen[V * hold :]
    beside = jnp.sum(seen * rest_ref[...], axis=0, keepdims=True)

    def products(s, image):
        r = res_ref[s * half : (s + 1) * half, :]
        extra = list(split(r)) + image
        wide, tall = [], []
        for n in range(half // 16):
            rows = slice(s * half + n * 16, s * half + (n + 1) * 16)
            block = lz_ref[:, rows, :].reshape(K * 16, nx)
            wide.append(block)
            part = slice(n * 16, (n + 1) * 16)
            tall.append(jnp.concatenate([block] + [x[part] for x in extra], axis=0))
        table = lax.dot_general(
            jnp.concatenate(tall, axis=1), jnp.concatenate(wide, axis=1),
            (((1,), (1,)), ((), ())), preferred_element_type=f32,
        )
        return table, fold(r * r)

    def fold(x):
        return jnp.sum(x.reshape(x.shape[0] // 8, 8, nx), axis=0)

    half = V // 2 * plane
    loads[0].wait()
    loads[1].wait()
    table_a, square = products(0, [])

    finish(0)

    high, low = split(lead_ref[...])
    seen = jnp.dot(
        jnp.concatenate([high, low], axis=1), near_ref[...], preferred_element_type=f32
    )
    grid = jnp.sum(seen * sel_ref[...], axis=0, keepdims=True) + beside
    weighted = weight * grid
    high, low = split(sel_ref[...] * weighted)
    across = (((1,), (1,)), ((), ()))
    u = lax.dot_general(high, near_ref[0:nx], across, preferred_element_type=f32)
    u += lax.dot_general(low, near_ref[0:nx], across, preferred_element_type=f32)
    begin(u, 1)
    launch(1)

    inside(u)
    back = lax.dot_general(
        jnp.concatenate(split(rest_ref[...] * weighted), axis=0), hot_ref[...], across,
        preferred_element_type=f32,
    )
    back = back[0 : V * hold] + back[V * hold :]
    for v in range(V):
        for y in range(ny):
            img_ref[pl.ds(v * plane + lead_rows + y, rest, stride=ny), :] = back[
                v * hold : v * hold + rest, y * nx : (y + 1) * nx
            ]

    zero = jnp.zeros((8, nx), f32)

    def image_dots(base, mine, carry):
        rows = pl.ds(base, CHUNK)
        d = dir_ref[rows, :]
        image = d + mine
        img_ref[rows, :] = image
        r = res_ref[rows, :]
        out = [
            carry[0] + fold(r * image), carry[1] + fold(image * image), carry[2] + fold(d * image)
        ]
        for k in range(K):
            out.append(carry[k + 3] + fold(image * lz_ref[k, rows, :].astype(f32)))
        return tuple(out)

    turns = (plane - lead_rows) // CHUNK

    def rest_dots(s, carry):
        base = lax.div(s, turns) * plane + lead_rows + lax.rem(s, turns) * CHUNK
        base = pl.multiple_of(base, CHUNK)
        return image_dots(base, img_ref[pl.ds(base, CHUNK), :], carry)

    img_dots = lax.fori_loop(0, V // 2 * turns, rest_dots, (zero,) * (K + 3), unroll=2)
    few, images = list(img_dots[:3]), []
    for v in range(V // 2, V):
        rows = slice(v * plane + lead_rows, (v + 1) * plane)
        d, r = dir_ref[rows, :], res_ref[rows, :]
        image = d + img_ref[rows, :]
        img_ref[rows, :] = image
        few = [x + fold(y * image) for x, y in zip(few, (r, image, d))]
        images += [jnp.zeros((lead_rows, nx), f32), image]
    img_dots = tuple(few) + img_dots[3:]
    table, more = products(1, list(split(jnp.concatenate(images, axis=0))))
    square += more
    at_row = lax.broadcasted_iota(jnp.int32, table.shape, 0)
    at_col = lax.broadcasted_iota(jnp.int32, table.shape, 1)
    table += jnp.concatenate([table_a, jnp.zeros((32, K * 16), f32)], axis=0)
    kept = jnp.where((at_row & 15) == (at_col & 15), table, 0.0)
    kept = jnp.sum(kept.reshape(K + 4, 16, K * 16), axis=1)
    kept = jnp.concatenate(
        [
            kept[0:K], kept[K : K + 1] + kept[K + 1 : K + 2],
            kept[K + 2 : K + 3] + kept[K + 3 : K + 4], jnp.zeros((14 - K, K * 16), f32),
        ],
        axis=0,
    )
    which_k = lax.shift_right_logical(lax.broadcasted_iota(jnp.int32, (K * 16, nx), 0), 4)
    in_lane = lax.broadcasted_iota(jnp.int32, (K * 16, nx), 1)
    pick = jnp.zeros((K * 16, nx), f32)
    for j in range(K + 2):
        pick = jnp.where(in_lane == which_k + j * K, 1.0, pick)
    spread_out = jnp.dot(
        kept, pick, preferred_element_type=f32, precision=lax.Precision.HIGHEST
    )
    g_lane = lax.broadcasted_iota(jnp.int32, (16, nx), 1)
    g_row = lax.broadcasted_iota(jnp.int32, (16, nx), 0)
    own_row = (g_lane >= g_row * K) & (g_lane < (g_row + 1) * K) & (g_row < K + 2)
    gram_row = jnp.sum(jnp.where(own_row, spread_out, 0.0), axis=0, keepdims=True)
    finish(1)
    short = lead_rows // CHUNK

    def lead_dots(s, carry):
        base = pl.multiple_of(lax.div(s, short) * plane + lax.rem(s, short) * CHUNK, CHUNK)
        mine = lead_ref[pl.ds(pl.multiple_of(s * CHUNK, CHUNK), CHUNK), :]
        return image_dots(base, mine, carry)

    img_dots = lax.fori_loop(0, V * short, lead_dots, img_dots, unroll=2)

    def reduce_copy(over, along):
        return pltpu.make_async_remote_copy(
            src_ref=rs_ref,
            dst_ref=rr_ref.at[pl.ds(over * C + along, 1)],
            send_sem=r_ssem.at[0],
            recv_sem=r_rsem.at[0],
            device_id=(lax.rem(row + over, R), lax.rem(col + along, C)),
            device_id_type=MESH,
        )

    sums = list(img_dots[3:]) + [square] + list(img_dots[:3])
    rows = [jnp.zeros((K * K + K, nx), f32)] + [jnp.sum(x, axis=0, keepdims=True) for x in sums]
    rows.append(jnp.zeros((nx - K * K - K - len(sums), nx), f32))
    packed = jnp.sum(jnp.concatenate(rows, axis=0).T, axis=0, keepdims=True)
    rs_ref[...] = packed + gram_row

    def go(over, carry):
        for along in range(C):
            reduce_copy(over, along).start()
        return carry

    lax.fori_loop(1, R, go, 0)
    for along in range(1, C):
        reduce_copy(0, along).start()
    loads[2].wait()
    every = pltpu.make_async_remote_copy(
        src_ref=rr_ref.at[pl.ds(1, N - 1)],
        dst_ref=rr_ref.at[pl.ds(1, N - 1)],
        send_sem=r_ssem.at[0],
        recv_sem=r_rsem.at[0],
        device_id=(row, lax.rem(col + 1, C)),
        device_id_type=MESH,
    )
    every.wait_recv()
    every.wait_send()
    rr_ref[pl.ds(0, 1)] = rs_ref[...]
    tot_ref[...] = jnp.broadcast_to(jnp.sum(rr_ref[...], axis=0, keepdims=True), (8, nx))
    for inst in range(2):
        for d in range(1, R):
            arrival(inst, 0, d).wait_send()
            arrival(inst, 2, d).wait_send()
        for d in range(1, C):
            arrival(inst, 1, d).wait_send()


def update(
    K, total_cells, parts,
    tot_ref, res_ref, inc_ref, dir_ref, img_ref, lz_ref, oinc_hbm, ores_hbm, odir_hbm,
    oinc_ref, ores_ref, odir_ref, sem,
):
    flat, nx = res_ref.shape
    totals = tot_ref[0:1, :]
    lane = lax.broadcasted_iota(jnp.int32, (1, nx), 1)

    def total(n):
        return totals[:, n : n + 1]

    first = K * K
    rr, ri, ii, di = (total(first + 2 * K + n) for n in range(4))
    step_size = rr / di
    moments = [total(first + k) - step_size * total(first + K + k) for k in range(K)]
    left, right = jnp.zeros((1, nx), f32), jnp.zeros((1, nx), f32)
    for j in range(K):
        left = jnp.where((lane >= j * K) & (lane < (j + 1) * K), moments[j], left)
    single = jnp.zeros((1, nx), f32)
    for k in range(K):
        hit = lane == k
        for j in range(1, K):
            hit = hit | (lane == j * K + k)
        right = jnp.where(hit, moments[k], right)
        single = jnp.where(lane == k, moments[k], single)
    squares = jnp.sum(left * right * totals, axis=1, keepdims=True)
    crossed = jnp.sum(single * single, axis=1, keepdims=True)
    moved_norm = rr + step_size * (step_size * ii - 2.0 * ri)
    norm_new = moved_norm + (squares / total_cells - 2.0 * crossed) / total_cells
    coefficient = [jnp.broadcast_to(x / total_cells, (CHUNK, nx)) for x in moments]
    step_wide = jnp.broadcast_to(step_size, (CHUNK, nx))
    ratio = jnp.broadcast_to(norm_new / rr, (CHUNK, nx))
    oinc_ref[...] = inc_ref[...] + jnp.broadcast_to(step_size, (flat, nx)) * dir_ref[...]
    copies = [pltpu.make_async_copy(oinc_ref, oinc_hbm, sem.at[0, 2])]
    copies[0].start()
    size = flat // parts
    for part in range(parts):

        def advance(s, carry):
            rows = pl.ds(pl.multiple_of(part * size + s * CHUNK, CHUNK), CHUNK)
            new = res_ref[rows, :] - step_wide * img_ref[rows, :]
            for k in range(K):
                new = new - coefficient[k] * lz_ref[k, rows, :].astype(f32)
            ores_ref[rows, :] = new
            odir_ref[rows, :] = new + ratio * dir_ref[rows, :]
            return carry

        lax.fori_loop(0, size // CHUNK, advance, 0, unroll=4)
        rows = pl.ds(part * size, size)
        for n, (src, dst) in enumerate(((ores_ref, ores_hbm), (odir_ref, odir_hbm))):
            copies.append(pltpu.make_async_copy(src.at[rows], dst.at[rows], sem.at[part, n]))
            copies[-1].start()
    for copy in copies:
        copy.wait()


def local(
    R, C,
    increment, residual, direction, lanczos, vertical_modes, amplitude,
    length_east, length_north, observed_cell, observed_weight, observed_count,
):
    V, L, ny, nx = direction.shape
    M = length_east.shape[1]
    K = lanczos.shape[0]
    I = V * M
    N = R * C
    flat = V * L * ny
    slots = observed_cell.shape[0]
    pad = (L + 15) // 16 * 16
    hbm = pl.BlockSpec(memory_space=pltpu.HBM)
    near = pl.BlockSpec(memory_space=pltpu.VMEM)
    field = pltpu.VMEM((flat, nx), f32)
    lead = pltpu.VMEM((I * ny, nx), f32)
    held = pl.pallas_call(
        functools.partial(kernel, R, C, V, L, M, K, ny, nx),
        out_shape=(pltpu.VMEM((8, nx), f32),) + (field,) * 4 + (pltpu.VMEM((K, flat, nx), bf16),),
        in_specs=[hbm] * 11,
        out_specs=(near,) * 6,
        scratch_shapes=[
            pltpu.VMEM((1, 1), jnp.int32),
            pltpu.VMEM((2, V, M), f32), pltpu.VMEM((L, V, L), f32),
            pltpu.VMEM((V, L), f32), pltpu.VMEM((1, slots), jnp.int32), pltpu.VMEM((1, slots), f32),
            lead, lead, pltpu.VMEM((2, I * ny, nx), f32), pltpu.VMEM((2, I * ny, nx), f32),
            pltpu.VMEM((V, 2 * pad, 2 * pad), f32),
            pltpu.VMEM((2 * I, nx), f32), pltpu.VMEM((5, I * ny, nx), f32),
            lead, pltpu.VMEM((2, I * ny, nx), f32),
            pltpu.VMEM((ny * nx, slots), bf16), pltpu.VMEM((2 * nx, slots), bf16),
            pltpu.VMEM((I * ny, slots), f32), pltpu.VMEM((V * (pad - M), slots), f32),
            pltpu.VMEM((2, ny, nx), f32), pltpu.VMEM((2, C, ny, nx), f32),
            pltpu.VMEM((2, 2 * I, nx), f32), pltpu.VMEM((2, R, 2 * I, nx), f32),
            pltpu.VMEM((2, 1, nx), f32), pltpu.VMEM((2, R, C, nx), f32),
            pltpu.VMEM((1, nx), f32), pltpu.VMEM((N, nx), f32),
            pltpu.SemaphoreType.DMA((10 + 2 * V,)),
            pltpu.SemaphoreType.DMA((2, C)), pltpu.SemaphoreType.DMA((2, C)),
            pltpu.SemaphoreType.DMA((2, R)), pltpu.SemaphoreType.DMA((2, R)),
            pltpu.SemaphoreType.DMA((2, R)), pltpu.SemaphoreType.DMA((2, R)),
            pltpu.SemaphoreType.DMA((1,)), pltpu.SemaphoreType.DMA((1,)),
        ],
        compiler_params=pltpu.CompilerParams(
            collective_id=0, has_side_effects=True, vmem_limit_bytes=54 * 2**20
        ),
    )(
        observed_count.reshape(1, 1), direction.reshape(flat, nx), length_east, length_north,
        jnp.transpose(vertical_modes, (1, 0, 2)), amplitude,
        observed_cell.reshape(1, slots), observed_weight.reshape(1, slots),
        residual.reshape(flat, nx), increment.reshape(flat, nx), lanczos.reshape(K, flat, nx),
    )
    done = pl.pallas_call(
        functools.partial(update, K, float(flat * nx * N), PARTS),
        out_shape=(jax.ShapeDtypeStruct((flat, nx), f32),) * 3,
        in_specs=[near] * 6,
        out_specs=(hbm,) * 3,
        scratch_shapes=[
            pltpu.VMEM((flat, nx), f32), pltpu.VMEM((flat, nx), f32), pltpu.VMEM((flat, nx), f32),
            pltpu.SemaphoreType.DMA((PARTS, 3)),
        ],
        compiler_params=pltpu.CompilerParams(vmem_limit_bytes=16 * 2**20),
    )(*held)
    return tuple(x.reshape(V, L, ny, nx) for x in done)


def solution(mesh):
    field = P(None, None, "row", "col")
    tile = P(("row", "col"))
    in_specs = (
        field, field, field, P(None, None, None, "row", "col"),
        P(), P(), P(), P(), tile, tile, tile,
    )
    return jax.shard_map(
        functools.partial(local, mesh.shape["row"], mesh.shape["col"]),
        mesh=mesh, in_specs=in_specs, out_specs=(field,) * 3, check_vma=False,
    )
```

```python
import functools

import jax
import jax.numpy as jnp
from jax import lax
from jax.experimental import pallas as pl
from jax.experimental.pallas import tpu as pltpu
from jax.sharding import PartitionSpec as P

MESH = pl.DeviceIdType.MESH
f32 = jnp.float32
bf16 = jnp.bfloat16
CHUNK = 32
PARTS = 5


def kernel(
    R, C, V, L, M, K, ny, nx,
    cnt_hbm, dir_hbm, len_e_hbm, len_n_hbm, vm_hbm, amp_hbm, cell_hbm, wgt_hbm,
    res_hbm, inc_hbm, lz_hbm,
    tot_ref, res_ref, inc_ref, dir_ref, img_ref, lz_ref,
    cnt_ref, len_ref, vm_ref, amp_ref, cell_ref, wgt_ref,
    east_ref, north_ref, end_ref, start_ref, mix_ref, comb_ref, both_ref,
    lead_ref, pair_ref, hot_ref, near_ref, sel_ref, rest_ref,
    es_ref, er_ref, ns_ref, nr_ref, cs_ref, cr_ref, rs_ref, rr_ref,
    load_sem, e_ssem, e_rsem, n_ssem, n_rsem, c_ssem, c_rsem, r_ssem, r_rsem,
):
    N = R * C
    I = V * M
    row, col = lax.axis_index("row"), lax.axis_index("col")
    me = row * C + col
    barrier = pltpu.get_barrier_semaphore()

    def place(d):
        peer = lax.rem(me + d, N)
        return (lax.div(peer, C), lax.rem(peer, C))

    def greet(d, carry):
        pl.semaphore_signal(barrier, inc=1, device_id=place(d), device_id_type=MESH)
        return carry

    plane = L * ny
    lead_rows = M * ny
    rest = L - M
    firsts = [
        pltpu.make_async_copy(len_e_hbm, len_ref.at[0], load_sem.at[3]),
        pltpu.make_async_copy(len_n_hbm, len_ref.at[1], load_sem.at[4]),
    ]
    others = [
        pltpu.make_async_copy(cell_hbm, cell_ref, load_sem.at[5]),
        pltpu.make_async_copy(wgt_hbm, wgt_ref, load_sem.at[6]),
        pltpu.make_async_copy(vm_hbm, vm_ref, load_sem.at[7]),
        pltpu.make_async_copy(amp_hbm, amp_ref, load_sem.at[8]),
        pltpu.make_async_copy(cnt_hbm, cnt_ref, load_sem.at[9 + 2 * V]),
    ]
    leads = []
    for v in range(V):
        part = pl.ds(v * plane, lead_rows)
        leads.append(
            pltpu.make_async_copy(dir_hbm.at[part], dir_ref.at[part], load_sem.at[9 + v])
        )
        part = pl.ds(v * plane + lead_rows, plane - lead_rows)
        others.append(
            pltpu.make_async_copy(dir_hbm.at[part], dir_ref.at[part], load_sem.at[9 + V + v])
        )
    loads = [
        pltpu.make_async_copy(res_hbm, res_ref, load_sem.at[0]),
        pltpu.make_async_copy(lz_hbm, lz_ref, load_sem.at[1]),
        pltpu.make_async_copy(inc_hbm, inc_ref, load_sem.at[2]),
    ]
    lax.fori_loop(1, N, greet, 0)
    for load in firsts + leads + others + loads:
        load.start()
    for load in firsts:
        load.wait()

    lane = lax.broadcasted_iota(jnp.int32, (ny, nx), 1)
    sub = lax.broadcasted_iota(jnp.int32, (ny, nx), 0)
    east_at, north_at = lane.astype(f32), sub.astype(f32)
    inst_lane = lane & (I - 1)
    is_back = (lane & I) != 0
    is_late = lane >= 2 * I
    log_e = jnp.zeros((ny, nx), f32)
    log_n = jnp.zeros((ny, nx), f32)
    for i in range(I):
        v, m = i // M, i % M
        rows = slice(i * ny, (i + 1) * ny)
        e = -1.0 / (jnp.broadcast_to(len_ref[0, v : v + 1, m : m + 1], (ny, nx)) * float(nx))
        n = -1.0 / (jnp.broadcast_to(len_ref[1, v : v + 1, m : m + 1], (ny, nx)) * float(ny))
        log_e = jnp.where(inst_lane == i, e, log_e)
        log_n = jnp.where(inst_lane == i, n, log_n)
        east_ref[rows, :] = e
        north_ref[rows, :] = n
        end_ref[0, rows, :] = jnp.exp(e * (float(nx - 1) - east_at))
        start_ref[0, rows, :] = jnp.exp(e * east_at)
        end_ref[1, rows, :] = jnp.exp(n * (float(ny - 1) - north_at))
        start_ref[1, rows, :] = jnp.exp(n * north_at)
    corner_w = jnp.exp(log_n * jnp.where(is_late, north_at, float(ny - 1) - north_at))

    def every_sub(x):
        shift = ny // 2
        while shift:
            x = x + pltpu.roll(x, shift, 0)
            shift //= 2
        return x

    def split(x):
        high = x.astype(bf16)
        return high, (x - high.astype(f32)).astype(bf16)

    def scans(u, log_alpha, axis, size, at):
        power = jnp.exp(log_alpha)
        f, g = u, u
        shift = 1
        while shift < size:
            f = f + power * jnp.where(at >= shift, pltpu.roll(f, shift, axis), 0.0)
            g = g + power * jnp.where(at < size - shift, pltpu.roll(g, size - shift, axis), 0.0)
            power = power * power
            shift *= 2
        return f + g - u

    def smooth(x):
        return scans(x, log_lines, 1, nx, lax.broadcasted_iota(jnp.int32, (2 * I, nx), 1))

    def begin(u, inst):
        for i in range(I):
            rows = slice(i * ny, (i + 1) * ny)
            pair_ref[0, rows, :] = every_sub(u[rows] * end_ref[1, rows, :])
            pair_ref[1, rows, :] = every_sub(u[rows] * start_ref[1, rows, :])
        line = jnp.concatenate(
            [pair_ref[n, pl.ds(0, I, stride=ny), :] for n in range(2)], axis=0
        )
        ns_ref[inst] = smooth(line)
        moment = jnp.zeros((ny, nx), f32)
        for i in range(I):
            rows = slice(i * ny, (i + 1) * ny)
            e = jnp.sum(u[rows] * end_ref[0, rows, :], axis=1, keepdims=True)
            b = jnp.sum(u[rows] * start_ref[0, rows, :], axis=1, keepdims=True)
            moment = jnp.where(inst_lane == i, jnp.where(is_back, b, e), moment)
        es_ref[inst] = moment
        cs_ref[inst] = every_sub(moment * corner_w)[0:1]

    def launch(inst):
        for d in range(1, R):
            pltpu.make_async_remote_copy(
                src_ref=ns_ref.at[inst],
                dst_ref=nr_ref.at[inst, d],
                send_sem=n_ssem.at[inst, d],
                recv_sem=n_rsem.at[inst, d],
                device_id=(lax.rem(row + d, R), col),
                device_id_type=MESH,
            ).start()

        def go(over, carry):
            for along in range(C):
                pltpu.make_async_remote_copy(
                    src_ref=cs_ref.at[inst],
                    dst_ref=cr_ref.at[inst, over, pl.ds(along, 1)],
                    send_sem=c_ssem.at[inst, over],
                    recv_sem=c_rsem.at[inst, over],
                    device_id=(lax.rem(row + over, R), lax.rem(col + along, C)),
                    device_id_type=MESH,
                ).start()
            return carry

        lax.fori_loop(1, R, go, 0)
        for d in range(1, C):
            pltpu.make_async_remote_copy(
                src_ref=es_ref.at[inst],
                dst_ref=er_ref.at[inst, d],
                send_sem=e_ssem.at[inst, d],
                recv_sem=e_rsem.at[inst, d],
                device_id=(row, lax.rem(col + d, C)),
                device_id_type=MESH,
            ).start()

    def arrival(inst, kind, d):
        src, dst, send, recv = (
            (ns_ref.at[inst], nr_ref.at[inst, d], n_ssem, n_rsem),
            (es_ref.at[inst], er_ref.at[inst, d], e_ssem, e_rsem),
            (cr_ref.at[inst, d], cr_ref.at[inst, d], c_ssem, c_rsem),
        )[kind]
        return pltpu.make_async_remote_copy(
            src_ref=src, dst_ref=dst, send_sem=send.at[inst, d], recv_sem=recv.at[inst, d],
            device_id=(row, lax.rem(col + 1, C)), device_id_type=MESH,
        )

    def inside(u):
        u = u.reshape(I, ny, nx)
        u = scans(u, east_ref[...].reshape(I, ny, nx), 2, nx, lane[None])
        u = scans(u, north_ref[...].reshape(I, ny, nx), 1, ny, sub[None])
        lead_ref[...] = both_ref[0] * u.reshape(I * ny, nx)

    def weights(log_small, d, index, count, size):
        at = index.astype(f32)
        far = d > index
        source = jnp.where(far, index - d + count, index - d).astype(f32)
        step = d.astype(f32)
        left = jnp.where(
            far | (d == 0), 0.0, jnp.exp(log_small * (float(size) * jnp.maximum(step - 1.0, 0.0)))
        )
        right = jnp.where(
            far, jnp.exp(log_small * (float(size) * (float(count - 1) - step))), 0.0
        )
        edge = jnp.exp(
            log_small * (float(size) * (float(2 * count - 2) - at - source) + 1.0)
        )
        return left, right, edge

    def finish(inst):
        for d in range(1, C):
            arrival(inst, 1, d).wait_recv()
        ahead = jnp.zeros((ny, nx), f32)
        echo = col_edge[0:1] * es_ref[inst]
        for d in range(1, C):
            ahead += col_main[d : d + 1] * er_ref[inst, d]
            echo += col_edge[d : d + 1] * er_ref[inst, d]
        lines = ahead - pltpu.roll(echo, I, 1)
        settled = scans(lines, log_n, 0, ny, sub)
        for d in range(1, R):
            arrival(inst, 2, d).wait_recv()
        first = corner_w * lines
        ahead = row_main[0] * first
        echo = row_edge[0] * first
        for d in range(1, R):
            got = cr_ref[inst, d]
            got = col_main * got - pltpu.roll(col_edge * got, I, 1)
            got = jnp.sum(got.reshape(C // ny, ny, nx), axis=0)
            ahead += row_main[d] * got
            echo += row_edge[d] * got
        corner = every_sub(ahead - pltpu.roll(echo, 2 * I, 1))
        settled = lane_scale * (
            settled + lane_low * corner + lane_high * pltpu.roll(corner, 2 * I, 1)
        )
        for d in range(1, R):
            arrival(inst, 0, d).wait_recv()
        left, right, edge = north_w[0]
        p = jnp.zeros((I, nx), f32)
        q = -edge * ns_ref[inst, 0:I]
        for d in range(1, R):
            left, right, edge = north_w[d]
            p += left * nr_ref[inst, d, 0:I]
            q += right * nr_ref[inst, d, I : 2 * I] - edge * nr_ref[inst, d, 0:I]
        line = jnp.concatenate([p, q], axis=0)
        comb_ref[...] = line
        for i in range(I):
            rows = slice(i * ny, (i + 1) * ny)
            x = jnp.broadcast_to(settled[:, i : i + 1], (ny, nx))
            y = jnp.broadcast_to(settled[:, I + i : I + i + 1], (ny, nx))
            p = jnp.broadcast_to(comb_ref[i : i + 1, :], (ny, nx))
            q = jnp.broadcast_to(comb_ref[I + i : I + i + 1, :], (ny, nx))
            lead_ref[rows, :] += (
                both_ref[1, rows, :] * p + both_ref[2, rows, :] * q
                + both_ref[3, rows, :] * x + both_ref[4, rows, :] * y
            )

    log_lines = east_ref[pl.ds(0, I, stride=ny), :]
    log_lines = jnp.concatenate([log_lines, log_lines], axis=0)
    for load in leads:
        load.wait()
    u = jnp.concatenate([dir_ref[v * plane : v * plane + M * ny, :] for v in range(V)], axis=0)
    begin(u, 0)
    pl.semaphore_wait(barrier, N - 1)
    launch(0)

    alpha_e, alpha_n = jnp.exp(log_e), jnp.exp(log_n)
    lane_scale = jnp.sqrt(
        ((1.0 - alpha_e) / (1.0 + alpha_e)) * ((1.0 - alpha_n) / (1.0 + alpha_n))
    )
    lane_low = jnp.exp(log_n * (north_at + 1.0))
    lane_high = jnp.exp(log_n * (float(ny) - north_at))
    over = lax.broadcasted_iota(jnp.int32, (C, nx), 0)
    odd = (lax.broadcasted_iota(jnp.int32, (C, nx), 1) & I) != 0
    low, high, edge = weights(jnp.broadcast_to(log_e[0:1], (C, nx)), over, col, C, nx)
    col_main = jnp.where(odd, high, low)
    col_edge = jnp.where(odd, 0.0, edge)
    row_main, row_edge, north_w = [], [], []
    log_rows = north_ref[pl.ds(0, I, stride=ny), :]
    for d in range(R):
        step = jnp.full((ny, nx), d, jnp.int32)
        low, high, edge = weights(log_n, step, row, R, ny)
        row_main.append(jnp.where(is_late, high, low))
        row_edge.append(jnp.where(is_late, 0.0, edge))
        north_w.append(weights(log_rows, jnp.full((I, nx), d, jnp.int32), row, R, ny))
    for i in range(I):
        rows = slice(i * ny, (i + 1) * ny)
        a, b = jnp.exp(east_ref[rows, :]), jnp.exp(north_ref[rows, :])
        scale = jnp.sqrt(((1.0 - a) / (1.0 + a)) * ((1.0 - b) / (1.0 + b)))
        both_ref[0, rows, :] = scale
        both_ref[1, rows, :] = scale * b * start_ref[1, rows, :]
        both_ref[2, rows, :] = scale * b * end_ref[1, rows, :]
        both_ref[3, rows, :] = a * start_ref[0, rows, :]
        both_ref[4, rows, :] = a * end_ref[0, rows, :]
    inside(u)
    for load in others:
        load.wait()

    pad = (L + 15) // 16 * 16
    cell = cell_ref[...]
    slots = cell.shape[1]
    level = lax.shift_right_logical(cell, (ny * nx).bit_length() - 1)
    spot = cell & (ny * nx - 1)
    spot_x = spot & (nx - 1)
    spot_y = lax.shift_right_logical(spot, nx.bit_length() - 1)
    hot_ref[...] = jnp.where(
        lax.broadcasted_iota(jnp.int32, (ny * nx, slots), 0) == spot, 1.0, 0.0
    ).astype(bf16)
    near = jnp.where(
        lax.broadcasted_iota(jnp.int32, (nx, slots), 0) == spot_x, 1.0, 0.0
    ).astype(bf16)
    near_ref[0:nx] = near
    near_ref[nx : 2 * nx] = near
    live = lax.broadcasted_iota(jnp.int32, (1, slots), 1) < cnt_ref[...]
    weight = jnp.where(live, wgt_ref[...], 0.0)
    mix_ref[...] = jnp.zeros_like(mix_ref)
    at = lax.broadcasted_iota(jnp.int32, (pad, slots), 0)
    here = lax.broadcasted_iota(jnp.int32, (ny, slots), 0) == spot_y
    hold = pad - M
    for v in range(V):
        mix_ref[v, 0:L, 0:L] = vm_ref[:, v, :] * amp_ref[v : v + 1, :]
        left = mix_ref[v].T[0:pad, 0:pad]
        parts = []
        for _ in range(3):
            part = left.astype(bf16)
            parts.append(part)
            left = left - part.astype(f32)
        hit = jnp.where((at + v * L == level) & (at < L), 1.0, 0.0).astype(bf16)
        chosen = jnp.dot(jnp.concatenate(parts, axis=0), hit, preferred_element_type=f32)
        chosen = chosen[0:pad] + chosen[pad : 2 * pad] + chosen[2 * pad : 3 * pad]
        rest_ref[v * hold : (v + 1) * hold] = chosen[M:pad]
        for m in range(M):
            i = v * M + m
            sel_ref[i * ny : (i + 1) * ny] = jnp.where(
                here, jnp.broadcast_to(chosen[m : m + 1], (ny, slots)), 0.0
            )

    spare = jnp.zeros((hold - rest, nx), f32)
    held = jnp.concatenate(
        [
            jnp.concatenate(
                [
                    x
                    for v in range(V)
                    for x in (
                        dir_ref[pl.ds(v * plane + lead_rows + y, rest, stride=ny), :], spare
                    )
                ],
                axis=0,
            )
            for y in range(ny)
        ],
        axis=1,
    )
    seen = jnp.dot(
        jnp.concatenate(split(held), axis=0), hot_ref[...], preferred_element_type=f32
    )
    seen = seen[0 : V * hold] + seen[V * hold :]
    beside = jnp.sum(seen * rest_ref[...], axis=0, keepdims=True)

    def products(s, image):
        r = res_ref[s * half : (s + 1) * half, :]
        extra = list(split(r)) + image
        wide, tall = [], []
        for n in range(half // 16):
            rows = slice(s * half + n * 16, s * half + (n + 1) * 16)
            block = lz_ref[:, rows, :].reshape(K * 16, nx)
            wide.append(block)
            part = slice(n * 16, (n + 1) * 16)
            tall.append(jnp.concatenate([block] + [x[part] for x in extra], axis=0))
        table = lax.dot_general(
            jnp.concatenate(tall, axis=1), jnp.concatenate(wide, axis=1),
            (((1,), (1,)), ((), ())), preferred_element_type=f32,
        )
        return table, fold(r * r)

    def fold(x):
        return jnp.sum(x.reshape(x.shape[0] // 8, 8, nx), axis=0)

    half = V // 2 * plane
    loads[0].wait()
    loads[1].wait()
    table_a, square = products(0, [])

    finish(0)

    high, low = split(lead_ref[...])
    seen = jnp.dot(
        jnp.concatenate([high, low], axis=1), near_ref[...], preferred_element_type=f32
    )
    grid = jnp.sum(seen * sel_ref[...], axis=0, keepdims=True) + beside
    weighted = weight * grid
    high, low = split(sel_ref[...] * weighted)
    across = (((1,), (1,)), ((), ()))
    u = lax.dot_general(high, near_ref[0:nx], across, preferred_element_type=f32)
    u += lax.dot_general(low, near_ref[0:nx], across, preferred_element_type=f32)
    begin(u, 1)
    launch(1)

    inside(u)
    back = lax.dot_general(
        jnp.concatenate(split(rest_ref[...] * weighted), axis=0), hot_ref[...], across,
        preferred_element_type=f32,
    )
    back = back[0 : V * hold] + back[V * hold :]
    for v in range(V):
        for y in range(ny):
            img_ref[pl.ds(v * plane + lead_rows + y, rest, stride=ny), :] = back[
                v * hold : v * hold + rest, y * nx : (y + 1) * nx
            ]

    zero = jnp.zeros((8, nx), f32)

    def image_dots(base, mine, carry):
        rows = pl.ds(base, CHUNK)
        d = dir_ref[rows, :]
        image = d + mine
        img_ref[rows, :] = image
        r = res_ref[rows, :]
        out = [
            carry[0] + fold(r * image), carry[1] + fold(image * image), carry[2] + fold(d * image)
        ]
        for k in range(K):
            out.append(carry[k + 3] + fold(image * lz_ref[k, rows, :].astype(f32)))
        return tuple(out)

    turns = (plane - lead_rows) // CHUNK

    def rest_dots(s, carry):
        base = lax.div(s, turns) * plane + lead_rows + lax.rem(s, turns) * CHUNK
        base = pl.multiple_of(base, CHUNK)
        return image_dots(base, img_ref[pl.ds(base, CHUNK), :], carry)

    img_dots = lax.fori_loop(0, V // 2 * turns, rest_dots, (zero,) * (K + 3), unroll=2)
    few, images = list(img_dots[:3]), []
    for v in range(V // 2, V):
        rows = slice(v * plane + lead_rows, (v + 1) * plane)
        d, r = dir_ref[rows, :], res_ref[rows, :]
        image = d + img_ref[rows, :]
        img_ref[rows, :] = image
        few = [x + fold(y * image) for x, y in zip(few, (r, image, d))]
        images += [jnp.zeros((lead_rows, nx), f32), image]
    img_dots = tuple(few) + img_dots[3:]
    table, more = products(1, list(split(jnp.concatenate(images, axis=0))))
    square += more
    at_row = lax.broadcasted_iota(jnp.int32, table.shape, 0)
    at_col = lax.broadcasted_iota(jnp.int32, table.shape, 1)
    table += jnp.concatenate([table_a, jnp.zeros((32, K * 16), f32)], axis=0)
    kept = jnp.where((at_row & 15) == (at_col & 15), table, 0.0)
    kept = jnp.sum(kept.reshape(K + 4, 16, K * 16), axis=1)
    kept = jnp.concatenate(
        [
            kept[0:K], kept[K : K + 1] + kept[K + 1 : K + 2],
            kept[K + 2 : K + 3] + kept[K + 3 : K + 4], jnp.zeros((14 - K, K * 16), f32),
        ],
        axis=0,
    )
    which_k = lax.shift_right_logical(lax.broadcasted_iota(jnp.int32, (K * 16, nx), 0), 4)
    in_lane = lax.broadcasted_iota(jnp.int32, (K * 16, nx), 1)
    pick = jnp.zeros((K * 16, nx), f32)
    for j in range(K + 2):
        pick = jnp.where(in_lane == which_k + j * K, 1.0, pick)
    spread_out = jnp.dot(
        kept, pick, preferred_element_type=f32, precision=lax.Precision.HIGHEST
    )
    g_lane = lax.broadcasted_iota(jnp.int32, (16, nx), 1)
    g_row = lax.broadcasted_iota(jnp.int32, (16, nx), 0)
    own_row = (g_lane >= g_row * K) & (g_lane < (g_row + 1) * K) & (g_row < K + 2)
    gram_row = jnp.sum(jnp.where(own_row, spread_out, 0.0), axis=0, keepdims=True)
    finish(1)
    short = lead_rows // CHUNK

    def lead_dots(s, carry):
        base = pl.multiple_of(lax.div(s, short) * plane + lax.rem(s, short) * CHUNK, CHUNK)
        mine = lead_ref[pl.ds(pl.multiple_of(s * CHUNK, CHUNK), CHUNK), :]
        return image_dots(base, mine, carry)

    img_dots = lax.fori_loop(0, V * short, lead_dots, img_dots, unroll=2)

    def reduce_copy(over, along):
        return pltpu.make_async_remote_copy(
            src_ref=rs_ref,
            dst_ref=rr_ref.at[pl.ds(over * C + along, 1)],
            send_sem=r_ssem.at[0],
            recv_sem=r_rsem.at[0],
            device_id=(lax.rem(row + over, R), lax.rem(col + along, C)),
            device_id_type=MESH,
        )

    sums = list(img_dots[3:]) + [square] + list(img_dots[:3])
    rows = [jnp.zeros((K * K + K, nx), f32)] + [jnp.sum(x, axis=0, keepdims=True) for x in sums]
    rows.append(jnp.zeros((nx - K * K - K - len(sums), nx), f32))
    packed = jnp.sum(jnp.concatenate(rows, axis=0).T, axis=0, keepdims=True)
    rs_ref[...] = packed + gram_row

    def go(over, carry):
        for along in range(C):
            reduce_copy(over, along).start()
        return carry

    lax.fori_loop(1, R, go, 0)
    for along in range(1, C):
        reduce_copy(0, along).start()
    loads[2].wait()
    for inst in range(2):
        for d in range(1, R):
            arrival(inst, 0, d).wait_send()
            arrival(inst, 2, d).wait_send()
        for d in range(1, C):
            arrival(inst, 1, d).wait_send()
    every = pltpu.make_async_remote_copy(
        src_ref=rr_ref.at[pl.ds(1, N - 1)],
        dst_ref=rr_ref.at[pl.ds(1, N - 1)],
        send_sem=r_ssem.at[0],
        recv_sem=r_rsem.at[0],
        device_id=(row, lax.rem(col + 1, C)),
        device_id_type=MESH,
    )
    rr_ref[pl.ds(0, 1)] = rs_ref[...]
    every.wait_recv()
    tot_ref[...] = every_sub(jnp.sum(rr_ref[...].reshape(N // 8, 8, nx), axis=0))
    every.wait_send()


def update(
    K, total_cells, parts,
    tot_ref, res_ref, inc_ref, dir_ref, img_ref, lz_ref, oinc_hbm, ores_hbm, odir_hbm,
    oinc_ref, ores_ref, odir_ref, sem,
):
    flat, nx = res_ref.shape
    totals = tot_ref[0:1, :]
    lane = lax.broadcasted_iota(jnp.int32, (1, nx), 1)

    def total(n):
        return totals[:, n : n + 1]

    first = K * K
    rr, ri, ii, di = (total(first + 2 * K + n) for n in range(4))
    step_size = rr / di
    moments = [total(first + k) - step_size * total(first + K + k) for k in range(K)]
    left, right = jnp.zeros((1, nx), f32), jnp.zeros((1, nx), f32)
    for j in range(K):
        left = jnp.where((lane >= j * K) & (lane < (j + 1) * K), moments[j], left)
    single = jnp.zeros((1, nx), f32)
    for k in range(K):
        hit = lane == k
        for j in range(1, K):
            hit = hit | (lane == j * K + k)
        right = jnp.where(hit, moments[k], right)
        single = jnp.where(lane == k, moments[k], single)
    squares = jnp.sum(left * right * totals, axis=1, keepdims=True)
    crossed = jnp.sum(single * single, axis=1, keepdims=True)
    moved_norm = rr + step_size * (step_size * ii - 2.0 * ri)
    norm_new = moved_norm + (squares / total_cells - 2.0 * crossed) / total_cells
    coefficient = [jnp.broadcast_to(x / total_cells, (CHUNK, nx)) for x in moments]
    step_wide = jnp.broadcast_to(step_size, (CHUNK, nx))
    ratio = jnp.broadcast_to(norm_new / rr, (CHUNK, nx))
    oinc_ref[...] = inc_ref[...] + jnp.broadcast_to(step_size, (flat, nx)) * dir_ref[...]
    copies = [pltpu.make_async_copy(oinc_ref, oinc_hbm, sem.at[0, 2])]
    copies[0].start()
    size = flat // parts
    for part in range(parts):

        def advance(s, carry):
            rows = pl.ds(pl.multiple_of(part * size + s * CHUNK, CHUNK), CHUNK)
            new = res_ref[rows, :] - step_wide * img_ref[rows, :]
            for k in range(K):
                new = new - coefficient[k] * lz_ref[k, rows, :].astype(f32)
            ores_ref[rows, :] = new
            odir_ref[rows, :] = new + ratio * dir_ref[rows, :]
            return carry

        lax.fori_loop(0, size // CHUNK, advance, 0, unroll=4)
        rows = pl.ds(part * size, size)
        for n, (src, dst) in enumerate(((ores_ref, ores_hbm), (odir_ref, odir_hbm))):
            copies.append(pltpu.make_async_copy(src.at[rows], dst.at[rows], sem.at[part, n]))
            copies[-1].start()
    for copy in copies:
        copy.wait()


def local(
    R, C,
    increment, residual, direction, lanczos, vertical_modes, amplitude,
    length_east, length_north, observed_cell, observed_weight, observed_count,
):
    V, L, ny, nx = direction.shape
    M = length_east.shape[1]
    K = lanczos.shape[0]
    I = V * M
    N = R * C
    flat = V * L * ny
    slots = observed_cell.shape[0]
    pad = (L + 15) // 16 * 16
    hbm = pl.BlockSpec(memory_space=pltpu.HBM)
    near = pl.BlockSpec(memory_space=pltpu.VMEM)
    field = pltpu.VMEM((flat, nx), f32)
    lead = pltpu.VMEM((I * ny, nx), f32)
    held = pl.pallas_call(
        functools.partial(kernel, R, C, V, L, M, K, ny, nx),
        out_shape=(pltpu.VMEM((8, nx), f32),) + (field,) * 4 + (pltpu.VMEM((K, flat, nx), bf16),),
        in_specs=[hbm] * 11,
        out_specs=(near,) * 6,
        scratch_shapes=[
            pltpu.VMEM((1, 1), jnp.int32),
            pltpu.VMEM((2, V, M), f32), pltpu.VMEM((L, V, L), f32),
            pltpu.VMEM((V, L), f32), pltpu.VMEM((1, slots), jnp.int32), pltpu.VMEM((1, slots), f32),
            lead, lead, pltpu.VMEM((2, I * ny, nx), f32), pltpu.VMEM((2, I * ny, nx), f32),
            pltpu.VMEM((V, 2 * pad, 2 * pad), f32),
            pltpu.VMEM((2 * I, nx), f32), pltpu.VMEM((5, I * ny, nx), f32),
            lead, pltpu.VMEM((2, I * ny, nx), f32),
            pltpu.VMEM((ny * nx, slots), bf16), pltpu.VMEM((2 * nx, slots), bf16),
            pltpu.VMEM((I * ny, slots), f32), pltpu.VMEM((V * (pad - M), slots), f32),
            pltpu.VMEM((2, ny, nx), f32), pltpu.VMEM((2, C, ny, nx), f32),
            pltpu.VMEM((2, 2 * I, nx), f32), pltpu.VMEM((2, R, 2 * I, nx), f32),
            pltpu.VMEM((2, 1, nx), f32), pltpu.VMEM((2, R, C, nx), f32),
            pltpu.VMEM((1, nx), f32), pltpu.VMEM((N, nx), f32),
            pltpu.SemaphoreType.DMA((10 + 2 * V,)),
            pltpu.SemaphoreType.DMA((2, C)), pltpu.SemaphoreType.DMA((2, C)),
            pltpu.SemaphoreType.DMA((2, R)), pltpu.SemaphoreType.DMA((2, R)),
            pltpu.SemaphoreType.DMA((2, R)), pltpu.SemaphoreType.DMA((2, R)),
            pltpu.SemaphoreType.DMA((1,)), pltpu.SemaphoreType.DMA((1,)),
        ],
        compiler_params=pltpu.CompilerParams(
            collective_id=0, has_side_effects=True, vmem_limit_bytes=54 * 2**20
        ),
    )(
        observed_count.reshape(1, 1), direction.reshape(flat, nx), length_east, length_north,
        jnp.transpose(vertical_modes, (1, 0, 2)), amplitude,
        observed_cell.reshape(1, slots), observed_weight.reshape(1, slots),
        residual.reshape(flat, nx), increment.reshape(flat, nx), lanczos.reshape(K, flat, nx),
    )
    done = pl.pallas_call(
        functools.partial(update, K, float(flat * nx * N), PARTS),
        out_shape=(jax.ShapeDtypeStruct((flat, nx), f32),) * 3,
        in_specs=[near] * 6,
        out_specs=(hbm,) * 3,
        scratch_shapes=[
            pltpu.VMEM((flat, nx), f32), pltpu.VMEM((flat, nx), f32), pltpu.VMEM((flat, nx), f32),
            pltpu.SemaphoreType.DMA((PARTS, 3)),
        ],
        compiler_params=pltpu.CompilerParams(vmem_limit_bytes=16 * 2**20),
    )(*held)
    return tuple(x.reshape(V, L, ny, nx) for x in done)


def solution(mesh):
    field = P(None, None, "row", "col")
    tile = P(("row", "col"))
    in_specs = (
        field, field, field, P(None, None, None, "row", "col"),
        P(), P(), P(), P(), tile, tile, tile,
    )
    return jax.shard_map(
        functools.partial(local, mesh.shape["row"], mesh.shape["col"]),
        mesh=mesh, in_specs=in_specs, out_specs=(field,) * 3, check_vma=False,
    )
```

```python
import functools

import jax
import jax.numpy as jnp
from jax import lax
from jax.experimental import pallas as pl
from jax.experimental.pallas import tpu as pltpu
from jax.sharding import PartitionSpec as P

MESH = pl.DeviceIdType.MESH
f32 = jnp.float32
bf16 = jnp.bfloat16
CHUNK = 32
PARTS = 5


def kernel(
    R, C, V, L, M, K, ny, nx,
    cnt_hbm, dir_hbm, len_e_hbm, len_n_hbm, vm_hbm, amp_hbm, cell_hbm, wgt_hbm,
    res_hbm, inc_hbm, lz_hbm,
    tot_ref, res_ref, inc_ref, dir_ref, img_ref, lz_ref,
    cnt_ref, len_ref, vm_ref, amp_ref, cell_ref, wgt_ref,
    east_ref, north_ref, end_ref, start_ref, mix_ref, comb_ref, both_ref,
    lead_ref, pair_ref, hot_ref, near_ref, sel_ref, rest_ref,
    es_ref, er_ref, ns_ref, nr_ref, cs_ref, cr_ref, rs_ref, rr_ref,
    load_sem, e_ssem, e_rsem, n_ssem, n_rsem, c_ssem, c_rsem, r_ssem, r_rsem,
):
    N = R * C
    I = V * M
    row, col = lax.axis_index("row"), lax.axis_index("col")
    me = row * C + col
    barrier = pltpu.get_barrier_semaphore()

    def place(d):
        peer = lax.rem(me + d, N)
        return (lax.div(peer, C), lax.rem(peer, C))

    def greet(d, carry):
        pl.semaphore_signal(barrier, inc=1, device_id=place(d), device_id_type=MESH)
        return carry

    plane = L * ny
    lead_rows = M * ny
    rest = L - M
    firsts = [
        pltpu.make_async_copy(len_e_hbm, len_ref.at[0], load_sem.at[3]),
        pltpu.make_async_copy(len_n_hbm, len_ref.at[1], load_sem.at[4]),
    ]
    others = [
        pltpu.make_async_copy(cell_hbm, cell_ref, load_sem.at[5]),
        pltpu.make_async_copy(wgt_hbm, wgt_ref, load_sem.at[6]),
        pltpu.make_async_copy(vm_hbm, vm_ref, load_sem.at[7]),
        pltpu.make_async_copy(amp_hbm, amp_ref, load_sem.at[8]),
        pltpu.make_async_copy(cnt_hbm, cnt_ref, load_sem.at[9 + 2 * V]),
    ]
    leads = []
    for v in range(V):
        part = pl.ds(v * plane, lead_rows)
        leads.append(
            pltpu.make_async_copy(dir_hbm.at[part], dir_ref.at[part], load_sem.at[9 + v])
        )
        part = pl.ds(v * plane + lead_rows, plane - lead_rows)
        others.append(
            pltpu.make_async_copy(dir_hbm.at[part], dir_ref.at[part], load_sem.at[9 + V + v])
        )
    loads = [
        pltpu.make_async_copy(res_hbm, res_ref, load_sem.at[0]),
        pltpu.make_async_copy(lz_hbm, lz_ref, load_sem.at[1]),
        pltpu.make_async_copy(inc_hbm, inc_ref, load_sem.at[2]),
    ]
    lax.fori_loop(1, N, greet, 0)
    for load in firsts + leads + others + loads:
        load.start()
    for load in firsts:
        load.wait()

    lane = lax.broadcasted_iota(jnp.int32, (ny, nx), 1)
    sub = lax.broadcasted_iota(jnp.int32, (ny, nx), 0)
    east_at, north_at = lane.astype(f32), sub.astype(f32)
    inst_lane = lane & (I - 1)
    is_back = (lane & I) != 0
    is_late = lane >= 2 * I
    log_e = jnp.zeros((ny, nx), f32)
    log_n = jnp.zeros((ny, nx), f32)
    for i in range(I):
        v, m = i // M, i % M
        rows = slice(i * ny, (i + 1) * ny)
        e = -1.0 / (jnp.broadcast_to(len_ref[0, v : v + 1, m : m + 1], (ny, nx)) * float(nx))
        n = -1.0 / (jnp.broadcast_to(len_ref[1, v : v + 1, m : m + 1], (ny, nx)) * float(ny))
        log_e = jnp.where(inst_lane == i, e, log_e)
        log_n = jnp.where(inst_lane == i, n, log_n)
        east_ref[rows, :] = e
        north_ref[rows, :] = n
        end_ref[0, rows, :] = jnp.exp(e * (float(nx - 1) - east_at))
        start_ref[0, rows, :] = jnp.exp(e * east_at)
        end_ref[1, rows, :] = jnp.exp(n * (float(ny - 1) - north_at))
        start_ref[1, rows, :] = jnp.exp(n * north_at)
    corner_w = jnp.exp(log_n * jnp.where(is_late, north_at, float(ny - 1) - north_at))

    def every_sub(x):
        shift = ny // 2
        while shift:
            x = x + pltpu.roll(x, shift, 0)
            shift //= 2
        return x

    def split(x):
        high = x.astype(bf16)
        return high, (x - high.astype(f32)).astype(bf16)

    def scans(u, log_alpha, axis, size, at):
        power = jnp.exp(log_alpha)
        f, g = u, u
        shift = 1
        while shift < size:
            f = f + power * jnp.where(at >= shift, pltpu.roll(f, shift, axis), 0.0)
            g = g + power * jnp.where(at < size - shift, pltpu.roll(g, size - shift, axis), 0.0)
            power = power * power
            shift *= 2
        return f + g - u

    def smooth(x):
        return scans(x, log_lines, 1, nx, lax.broadcasted_iota(jnp.int32, (2 * I, nx), 1))

    def begin(u, inst):
        for i in range(I):
            rows = slice(i * ny, (i + 1) * ny)
            pair_ref[0, rows, :] = every_sub(u[rows] * end_ref[1, rows, :])
            pair_ref[1, rows, :] = every_sub(u[rows] * start_ref[1, rows, :])
        line = jnp.concatenate(
            [pair_ref[n, pl.ds(0, I, stride=ny), :] for n in range(2)], axis=0
        )
        ns_ref[inst] = smooth(line)
        moment = jnp.zeros((ny, nx), f32)
        for i in range(I):
            rows = slice(i * ny, (i + 1) * ny)
            e = jnp.sum(u[rows] * end_ref[0, rows, :], axis=1, keepdims=True)
            b = jnp.sum(u[rows] * start_ref[0, rows, :], axis=1, keepdims=True)
            moment = jnp.where(inst_lane == i, jnp.where(is_back, b, e), moment)
        es_ref[inst] = moment
        cs_ref[inst] = every_sub(moment * corner_w)[0:1]

    def launch(inst):
        for d in range(1, R):
            pltpu.make_async_remote_copy(
                src_ref=ns_ref.at[inst],
                dst_ref=nr_ref.at[inst, d],
                send_sem=n_ssem.at[inst, d],
                recv_sem=n_rsem.at[inst, d],
                device_id=(lax.rem(row + d, R), col),
                device_id_type=MESH,
            ).start()

        def go(over, carry):
            for along in range(C):
                pltpu.make_async_remote_copy(
                    src_ref=cs_ref.at[inst],
                    dst_ref=cr_ref.at[inst, over, pl.ds(along, 1)],
                    send_sem=c_ssem.at[inst, over],
                    recv_sem=c_rsem.at[inst, over],
                    device_id=(lax.rem(row + over, R), lax.rem(col + along, C)),
                    device_id_type=MESH,
                ).start()
            return carry

        lax.fori_loop(1, R, go, 0)
        for d in range(1, C):
            pltpu.make_async_remote_copy(
                src_ref=es_ref.at[inst],
                dst_ref=er_ref.at[inst, d],
                send_sem=e_ssem.at[inst, d],
                recv_sem=e_rsem.at[inst, d],
                device_id=(row, lax.rem(col + d, C)),
                device_id_type=MESH,
            ).start()

    def arrival(inst, kind, d):
        src, dst, send, recv = (
            (ns_ref.at[inst], nr_ref.at[inst, d], n_ssem, n_rsem),
            (es_ref.at[inst], er_ref.at[inst, d], e_ssem, e_rsem),
            (cr_ref.at[inst, d], cr_ref.at[inst, d], c_ssem, c_rsem),
        )[kind]
        return pltpu.make_async_remote_copy(
            src_ref=src, dst_ref=dst, send_sem=send.at[inst, d], recv_sem=recv.at[inst, d],
            device_id=(row, lax.rem(col + 1, C)), device_id_type=MESH,
        )

    def inside(u):
        u = u.reshape(I, ny, nx)
        u = scans(u, east_ref[...].reshape(I, ny, nx), 2, nx, lane[None])
        u = scans(u, north_ref[...].reshape(I, ny, nx), 1, ny, sub[None])
        lead_ref[...] = both_ref[0] * u.reshape(I * ny, nx)

    def weights(log_small, d, index, count, size):
        at = index.astype(f32)
        far = d > index
        source = jnp.where(far, index - d + count, index - d).astype(f32)
        step = d.astype(f32)
        left = jnp.where(
            far | (d == 0), 0.0, jnp.exp(log_small * (float(size) * jnp.maximum(step - 1.0, 0.0)))
        )
        right = jnp.where(
            far, jnp.exp(log_small * (float(size) * (float(count - 1) - step))), 0.0
        )
        edge = jnp.exp(
            log_small * (float(size) * (float(2 * count - 2) - at - source) + 1.0)
        )
        return left, right, edge

    def finish(inst):
        for d in range(1, C):
            arrival(inst, 1, d).wait_recv()
        ahead = jnp.zeros((ny, nx), f32)
        echo = col_edge[0:1] * es_ref[inst]
        for d in range(1, C):
            ahead += col_main[d : d + 1] * er_ref[inst, d]
            echo += col_edge[d : d + 1] * er_ref[inst, d]
        lines = ahead - pltpu.roll(echo, I, 1)
        settled = scans(lines, log_n, 0, ny, sub)
        for d in range(1, R):
            arrival(inst, 2, d).wait_recv()
        first = corner_w * lines
        ahead = row_main[0] * first
        echo = row_edge[0] * first
        for d in range(1, R):
            got = cr_ref[inst, d]
            got = col_main * got - pltpu.roll(col_edge * got, I, 1)
            got = jnp.sum(got.reshape(C // ny, ny, nx), axis=0)
            ahead += row_main[d] * got
            echo += row_edge[d] * got
        corner = every_sub(ahead - pltpu.roll(echo, 2 * I, 1))
        settled = lane_scale * (
            settled + lane_low * corner + lane_high * pltpu.roll(corner, 2 * I, 1)
        )
        for d in range(1, R):
            arrival(inst, 0, d).wait_recv()
        left, right, edge = north_w[0]
        p = jnp.zeros((I, nx), f32)
        q = -edge * ns_ref[inst, 0:I]
        for d in range(1, R):
            left, right, edge = north_w[d]
            p += left * nr_ref[inst, d, 0:I]
            q += right * nr_ref[inst, d, I : 2 * I] - edge * nr_ref[inst, d, 0:I]
        line = jnp.concatenate([p, q], axis=0)
        comb_ref[...] = line
        for i in range(I):
            rows = slice(i * ny, (i + 1) * ny)
            x = jnp.broadcast_to(settled[:, i : i + 1], (ny, nx))
            y = jnp.broadcast_to(settled[:, I + i : I + i + 1], (ny, nx))
            p = jnp.broadcast_to(comb_ref[i : i + 1, :], (ny, nx))
            q = jnp.broadcast_to(comb_ref[I + i : I + i + 1, :], (ny, nx))
            lead_ref[rows, :] += (
                both_ref[1, rows, :] * p + both_ref[2, rows, :] * q
                + both_ref[3, rows, :] * x + both_ref[4, rows, :] * y
            )

    log_lines = east_ref[pl.ds(0, I, stride=ny), :]
    log_lines = jnp.concatenate([log_lines, log_lines], axis=0)
    for load in leads:
        load.wait()
    u = jnp.concatenate([dir_ref[v * plane : v * plane + M * ny, :] for v in range(V)], axis=0)
    begin(u, 0)
    pl.semaphore_wait(barrier, N - 1)
    launch(0)

    alpha_e, alpha_n = jnp.exp(log_e), jnp.exp(log_n)
    lane_scale = jnp.sqrt(
        ((1.0 - alpha_e) / (1.0 + alpha_e)) * ((1.0 - alpha_n) / (1.0 + alpha_n))
    )
    lane_low = jnp.exp(log_n * (north_at + 1.0))
    lane_high = jnp.exp(log_n * (float(ny) - north_at))
    over = lax.broadcasted_iota(jnp.int32, (C, nx), 0)
    odd = (lax.broadcasted_iota(jnp.int32, (C, nx), 1) & I) != 0
    low, high, edge = weights(jnp.broadcast_to(log_e[0:1], (C, nx)), over, col, C, nx)
    col_main = jnp.where(odd, high, low)
    col_edge = jnp.where(odd, 0.0, edge)
    row_main, row_edge, north_w = [], [], []
    log_rows = north_ref[pl.ds(0, I, stride=ny), :]
    for d in range(R):
        step = jnp.full((ny, nx), d, jnp.int32)
        low, high, edge = weights(log_n, step, row, R, ny)
        row_main.append(jnp.where(is_late, high, low))
        row_edge.append(jnp.where(is_late, 0.0, edge))
        north_w.append(weights(log_rows, jnp.full((I, nx), d, jnp.int32), row, R, ny))
    for i in range(I):
        rows = slice(i * ny, (i + 1) * ny)
        a, b = jnp.exp(east_ref[rows, :]), jnp.exp(north_ref[rows, :])
        scale = jnp.sqrt(((1.0 - a) / (1.0 + a)) * ((1.0 - b) / (1.0 + b)))
        both_ref[0, rows, :] = scale
        both_ref[1, rows, :] = scale * b * start_ref[1, rows, :]
        both_ref[2, rows, :] = scale * b * end_ref[1, rows, :]
        both_ref[3, rows, :] = a * start_ref[0, rows, :]
        both_ref[4, rows, :] = a * end_ref[0, rows, :]
    inside(u)
    for load in others:
        load.wait()

    pad = (L + 15) // 16 * 16
    cell = cell_ref[...]
    slots = cell.shape[1]
    level = lax.shift_right_logical(cell, (ny * nx).bit_length() - 1)
    spot = cell & (ny * nx - 1)
    spot_x = spot & (nx - 1)
    spot_y = lax.shift_right_logical(spot, nx.bit_length() - 1)
    hot_ref[...] = jnp.where(
        lax.broadcasted_iota(jnp.int32, (ny * nx, slots), 0) == spot, 1.0, 0.0
    ).astype(bf16)
    near = jnp.where(
        lax.broadcasted_iota(jnp.int32, (nx, slots), 0) == spot_x, 1.0, 0.0
    ).astype(bf16)
    near_ref[0:nx] = near
    near_ref[nx : 2 * nx] = near
    live = lax.broadcasted_iota(jnp.int32, (1, slots), 1) < cnt_ref[...]
    weight = jnp.where(live, wgt_ref[...], 0.0)
    mix_ref[...] = jnp.zeros_like(mix_ref)
    at = lax.broadcasted_iota(jnp.int32, (pad, slots), 0)
    here = lax.broadcasted_iota(jnp.int32, (ny, slots), 0) == spot_y
    hold = pad - M
    for v in range(V):
        mix_ref[v, 0:L, 0:L] = vm_ref[:, v, :] * amp_ref[v : v + 1, :]
        left = mix_ref[v].T[0:pad, 0:pad]
        parts = []
        for _ in range(3):
            part = left.astype(bf16)
            parts.append(part)
            left = left - part.astype(f32)
        hit = jnp.where((at + v * L == level) & (at < L), 1.0, 0.0).astype(bf16)
        chosen = jnp.dot(jnp.concatenate(parts, axis=0), hit, preferred_element_type=f32)
        chosen = chosen[0:pad] + chosen[pad : 2 * pad] + chosen[2 * pad : 3 * pad]
        rest_ref[v * hold : (v + 1) * hold] = chosen[M:pad]
        for m in range(M):
            i = v * M + m
            sel_ref[i * ny : (i + 1) * ny] = jnp.where(
                here, jnp.broadcast_to(chosen[m : m + 1], (ny, slots)), 0.0
            )

    spare = jnp.zeros((hold - rest, nx), f32)
    held = jnp.concatenate(
        [
            jnp.concatenate(
                [
                    x
                    for v in range(V)
                    for x in (
                        dir_ref[pl.ds(v * plane + lead_rows + y, rest, stride=ny), :], spare
                    )
                ],
                axis=0,
            )
            for y in range(ny)
        ],
        axis=1,
    )
    seen = jnp.dot(
        jnp.concatenate(split(held), axis=0), hot_ref[...], preferred_element_type=f32
    )
    seen = seen[0 : V * hold] + seen[V * hold :]
    beside = jnp.sum(seen * rest_ref[...], axis=0, keepdims=True)

    def products(s, image):
        r = res_ref[s * half : (s + 1) * half, :]
        extra = list(split(r)) + image
        wide, tall = [], []
        for n in range(half // 16):
            rows = slice(s * half + n * 16, s * half + (n + 1) * 16)
            block = lz_ref[:, rows, :].reshape(K * 16, nx)
            wide.append(block)
            part = slice(n * 16, (n + 1) * 16)
            tall.append(jnp.concatenate([block] + [x[part] for x in extra], axis=0))
        table = lax.dot_general(
            jnp.concatenate(tall, axis=1), jnp.concatenate(wide, axis=1),
            (((1,), (1,)), ((), ())), preferred_element_type=f32,
        )
        return table, fold(r * r)

    def fold(x):
        return jnp.sum(x.reshape(x.shape[0] // 8, 8, nx), axis=0)

    half = V // 2 * plane
    loads[0].wait()
    loads[1].wait()
    table_a, square = products(0, [])

    finish(0)

    high, low = split(lead_ref[...])
    seen = jnp.dot(
        jnp.concatenate([high, low], axis=1), near_ref[...], preferred_element_type=f32
    )
    grid = jnp.sum(seen * sel_ref[...], axis=0, keepdims=True) + beside
    weighted = weight * grid
    high, low = split(sel_ref[...] * weighted)
    across = (((1,), (1,)), ((), ()))
    u = lax.dot_general(high, near_ref[0:nx], across, preferred_element_type=f32)
    u += lax.dot_general(low, near_ref[0:nx], across, preferred_element_type=f32)
    begin(u, 1)
    launch(1)

    inside(u)
    back = lax.dot_general(
        jnp.concatenate(split(rest_ref[...] * weighted), axis=0), hot_ref[...], across,
        preferred_element_type=f32,
    )
    back = back[0 : V * hold] + back[V * hold :]
    for v in range(V):
        for y in range(ny):
            img_ref[pl.ds(v * plane + lead_rows + y, rest, stride=ny), :] = back[
                v * hold : v * hold + rest, y * nx : (y + 1) * nx
            ]

    zero = jnp.zeros((8, nx), f32)

    def image_dots(base, mine, carry):
        rows = pl.ds(base, CHUNK)
        d = dir_ref[rows, :]
        image = d + mine
        img_ref[rows, :] = image
        r = res_ref[rows, :]
        out = [
            carry[0] + fold(r * image), carry[1] + fold(image * image), carry[2] + fold(d * image)
        ]
        for k in range(K):
            out.append(carry[k + 3] + fold(image * lz_ref[k, rows, :].astype(f32)))
        return tuple(out)

    turns = (plane - lead_rows) // CHUNK

    def rest_dots(s, carry):
        base = lax.div(s, turns) * plane + lead_rows + lax.rem(s, turns) * CHUNK
        base = pl.multiple_of(base, CHUNK)
        return image_dots(base, img_ref[pl.ds(base, CHUNK), :], carry)

    img_dots = lax.fori_loop(0, V // 2 * turns, rest_dots, (zero,) * (K + 3), unroll=2)
    few, images = list(img_dots[:3]), []
    for v in range(V // 2, V):
        rows = slice(v * plane + lead_rows, (v + 1) * plane)
        d, r = dir_ref[rows, :], res_ref[rows, :]
        image = d + img_ref[rows, :]
        img_ref[rows, :] = image
        few = [x + fold(y * image) for x, y in zip(few, (r, image, d))]
        images += [jnp.zeros((lead_rows, nx), f32), image]
    img_dots = tuple(few) + img_dots[3:]
    table, more = products(1, list(split(jnp.concatenate(images, axis=0))))
    square += more
    at_row = lax.broadcasted_iota(jnp.int32, table.shape, 0)
    at_col = lax.broadcasted_iota(jnp.int32, table.shape, 1)
    table += jnp.concatenate([table_a, jnp.zeros((32, K * 16), f32)], axis=0)
    kept = jnp.where((at_row & 15) == (at_col & 15), table, 0.0)
    kept = jnp.sum(kept.reshape(K + 4, 16, K * 16), axis=1)
    kept = jnp.concatenate(
        [
            kept[0:K], kept[K : K + 1] + kept[K + 1 : K + 2],
            kept[K + 2 : K + 3] + kept[K + 3 : K + 4], jnp.zeros((14 - K, K * 16), f32),
        ],
        axis=0,
    )
    which_k = lax.shift_right_logical(lax.broadcasted_iota(jnp.int32, (K * 16, nx), 0), 4)
    in_lane = lax.broadcasted_iota(jnp.int32, (K * 16, nx), 1)
    pick = jnp.zeros((K * 16, nx), f32)
    for j in range(K + 2):
        pick = jnp.where(in_lane == which_k + j * K, 1.0, pick)
    spread_out = jnp.dot(
        kept, pick, preferred_element_type=f32, precision=lax.Precision.HIGHEST
    )
    g_lane = lax.broadcasted_iota(jnp.int32, (16, nx), 1)
    g_row = lax.broadcasted_iota(jnp.int32, (16, nx), 0)
    own_row = (g_lane >= g_row * K) & (g_lane < (g_row + 1) * K) & (g_row < K + 2)
    gram_row = jnp.sum(jnp.where(own_row, spread_out, 0.0), axis=0, keepdims=True)
    finish(1)
    short = lead_rows // CHUNK

    def lead_dots(s, carry):
        base = pl.multiple_of(lax.div(s, short) * plane + lax.rem(s, short) * CHUNK, CHUNK)
        mine = lead_ref[pl.ds(pl.multiple_of(s * CHUNK, CHUNK), CHUNK), :]
        return image_dots(base, mine, carry)

    img_dots = lax.fori_loop(0, V * short, lead_dots, img_dots, unroll=2)

    def reduce_copy(over, along):
        return pltpu.make_async_remote_copy(
            src_ref=rs_ref,
            dst_ref=rr_ref.at[pl.ds(over * C + along, 1)],
            send_sem=r_ssem.at[0],
            recv_sem=r_rsem.at[0],
            device_id=(lax.rem(row + over, R), lax.rem(col + along, C)),
            device_id_type=MESH,
        )

    sums = list(img_dots[3:]) + [square] + list(img_dots[:3])
    rows = [jnp.zeros((K * K + K, nx), f32)] + [jnp.sum(x, axis=0, keepdims=True) for x in sums]
    rows.append(jnp.zeros((nx - K * K - K - len(sums), nx), f32))
    packed = jnp.sum(jnp.concatenate(rows, axis=0).T, axis=0, keepdims=True)
    rs_ref[...] = packed + gram_row

    def go(over, carry):
        for along in range(C):
            reduce_copy(over, along).start()
        return carry

    lax.fori_loop(1, R, go, 0)
    for along in range(1, C):
        reduce_copy(0, along).start()
    loads[2].wait()
    for inst in range(2):
        for d in range(1, R):
            arrival(inst, 0, d).wait_send()
            arrival(inst, 2, d).wait_send()
        for d in range(1, C):
            arrival(inst, 1, d).wait_send()
    every = pltpu.make_async_remote_copy(
        src_ref=rr_ref.at[pl.ds(1, N - 1)],
        dst_ref=rr_ref.at[pl.ds(1, N - 1)],
        send_sem=r_ssem.at[0],
        recv_sem=r_rsem.at[0],
        device_id=(row, lax.rem(col + 1, C)),
        device_id_type=MESH,
    )
    rr_ref[pl.ds(0, 1)] = rs_ref[...]
    every.wait_recv()
    tot_ref[...] = every_sub(jnp.sum(rr_ref[...].reshape(N // 8, 8, nx), axis=0))
    every.wait_send()


def update(
    K, total_cells, parts,
    tot_ref, res_ref, inc_ref, dir_ref, img_ref, lz_ref, oinc_hbm, ores_hbm, odir_hbm,
    oinc_ref, ores_ref, odir_ref, sem,
):
    flat, nx = res_ref.shape
    totals = tot_ref[0:1, :]
    lane = lax.broadcasted_iota(jnp.int32, (1, nx), 1)

    def total(n):
        return totals[:, n : n + 1]

    first = K * K
    rr, ri, ii, di = (total(first + 2 * K + n) for n in range(4))
    step_size = rr / di
    moments = [total(first + k) - step_size * total(first + K + k) for k in range(K)]
    left, right = jnp.zeros((1, nx), f32), jnp.zeros((1, nx), f32)
    for j in range(K):
        left = jnp.where((lane >= j * K) & (lane < (j + 1) * K), moments[j], left)
    single = jnp.zeros((1, nx), f32)
    for k in range(K):
        hit = lane == k
        for j in range(1, K):
            hit = hit | (lane == j * K + k)
        right = jnp.where(hit, moments[k], right)
        single = jnp.where(lane == k, moments[k], single)
    squares = jnp.sum(left * right * totals, axis=1, keepdims=True)
    crossed = jnp.sum(single * single, axis=1, keepdims=True)
    moved_norm = rr + step_size * (step_size * ii - 2.0 * ri)
    norm_new = moved_norm + (squares / total_cells - 2.0 * crossed) / total_cells
    coefficient = [jnp.broadcast_to(x / total_cells, (CHUNK, nx)) for x in moments]
    step_wide = jnp.broadcast_to(step_size, (CHUNK, nx))
    ratio = jnp.broadcast_to(norm_new / rr, (CHUNK, nx))
    size = flat // parts
    copies = []
    for part in range(parts):
        rows = pl.ds(part * size, size)
        oinc_ref[rows, :] = (
            inc_ref[rows, :] + jnp.broadcast_to(step_size, (size, nx)) * dir_ref[rows, :]
        )
        copies.append(pltpu.make_async_copy(oinc_ref.at[rows], oinc_hbm.at[rows], sem.at[part, 2]))
        copies[-1].start()
    for part in range(parts):

        def advance(s, carry):
            rows = pl.ds(pl.multiple_of(part * size + s * CHUNK, CHUNK), CHUNK)
            new = res_ref[rows, :] - step_wide * img_ref[rows, :]
            for k in range(K):
                new = new - coefficient[k] * lz_ref[k, rows, :].astype(f32)
            ores_ref[rows, :] = new
            odir_ref[rows, :] = new + ratio * dir_ref[rows, :]
            return carry

        lax.fori_loop(0, size // CHUNK, advance, 0, unroll=4)
        rows = pl.ds(part * size, size)
        for n, (src, dst) in enumerate(((ores_ref, ores_hbm), (odir_ref, odir_hbm))):
            copies.append(pltpu.make_async_copy(src.at[rows], dst.at[rows], sem.at[part, n]))
            copies[-1].start()
    for copy in copies:
        copy.wait()


def local(
    R, C,
    increment, residual, direction, lanczos, vertical_modes, amplitude,
    length_east, length_north, observed_cell, observed_weight, observed_count,
):
    V, L, ny, nx = direction.shape
    M = length_east.shape[1]
    K = lanczos.shape[0]
    I = V * M
    N = R * C
    flat = V * L * ny
    slots = observed_cell.shape[0]
    pad = (L + 15) // 16 * 16
    hbm = pl.BlockSpec(memory_space=pltpu.HBM)
    near = pl.BlockSpec(memory_space=pltpu.VMEM)
    field = pltpu.VMEM((flat, nx), f32)
    lead = pltpu.VMEM((I * ny, nx), f32)
    held = pl.pallas_call(
        functools.partial(kernel, R, C, V, L, M, K, ny, nx),
        out_shape=(pltpu.VMEM((8, nx), f32),) + (field,) * 4 + (pltpu.VMEM((K, flat, nx), bf16),),
        in_specs=[hbm] * 11,
        out_specs=(near,) * 6,
        scratch_shapes=[
            pltpu.VMEM((1, 1), jnp.int32),
            pltpu.VMEM((2, V, M), f32), pltpu.VMEM((L, V, L), f32),
            pltpu.VMEM((V, L), f32), pltpu.VMEM((1, slots), jnp.int32), pltpu.VMEM((1, slots), f32),
            lead, lead, pltpu.VMEM((2, I * ny, nx), f32), pltpu.VMEM((2, I * ny, nx), f32),
            pltpu.VMEM((V, 2 * pad, 2 * pad), f32),
            pltpu.VMEM((2 * I, nx), f32), pltpu.VMEM((5, I * ny, nx), f32),
            lead, pltpu.VMEM((2, I * ny, nx), f32),
            pltpu.VMEM((ny * nx, slots), bf16), pltpu.VMEM((2 * nx, slots), bf16),
            pltpu.VMEM((I * ny, slots), f32), pltpu.VMEM((V * (pad - M), slots), f32),
            pltpu.VMEM((2, ny, nx), f32), pltpu.VMEM((2, C, ny, nx), f32),
            pltpu.VMEM((2, 2 * I, nx), f32), pltpu.VMEM((2, R, 2 * I, nx), f32),
            pltpu.VMEM((2, 1, nx), f32), pltpu.VMEM((2, R, C, nx), f32),
            pltpu.VMEM((1, nx), f32), pltpu.VMEM((N, nx), f32),
            pltpu.SemaphoreType.DMA((10 + 2 * V,)),
            pltpu.SemaphoreType.DMA((2, C)), pltpu.SemaphoreType.DMA((2, C)),
            pltpu.SemaphoreType.DMA((2, R)), pltpu.SemaphoreType.DMA((2, R)),
            pltpu.SemaphoreType.DMA((2, R)), pltpu.SemaphoreType.DMA((2, R)),
            pltpu.SemaphoreType.DMA((1,)), pltpu.SemaphoreType.DMA((1,)),
        ],
        compiler_params=pltpu.CompilerParams(
            collective_id=0, has_side_effects=True, vmem_limit_bytes=54 * 2**20
        ),
    )(
        observed_count.reshape(1, 1), direction.reshape(flat, nx), length_east, length_north,
        jnp.transpose(vertical_modes, (1, 0, 2)), amplitude,
        observed_cell.reshape(1, slots), observed_weight.reshape(1, slots),
        residual.reshape(flat, nx), increment.reshape(flat, nx), lanczos.reshape(K, flat, nx),
    )
    done = pl.pallas_call(
        functools.partial(update, K, float(flat * nx * N), PARTS),
        out_shape=(jax.ShapeDtypeStruct((flat, nx), f32),) * 3,
        in_specs=[near] * 6,
        out_specs=(hbm,) * 3,
        scratch_shapes=[
            pltpu.VMEM((flat, nx), f32), pltpu.VMEM((flat, nx), f32), pltpu.VMEM((flat, nx), f32),
            pltpu.SemaphoreType.DMA((PARTS, 3)),
        ],
        compiler_params=pltpu.CompilerParams(vmem_limit_bytes=16 * 2**20),
    )(*held)
    return tuple(x.reshape(V, L, ny, nx) for x in done)


def solution(mesh):
    field = P(None, None, "row", "col")
    tile = P(("row", "col"))
    in_specs = (
        field, field, field, P(None, None, None, "row", "col"),
        P(), P(), P(), P(), tile, tile, tile,
    )
    return jax.shard_map(
        functools.partial(local, mesh.shape["row"], mesh.shape["col"]),
        mesh=mesh, in_specs=in_specs, out_specs=(field,) * 3, check_vma=False,
    )
```

```python
import functools

import jax
import jax.numpy as jnp
from jax import lax
from jax.experimental import pallas as pl
from jax.experimental.pallas import tpu as pltpu
from jax.sharding import PartitionSpec as P

MESH = pl.DeviceIdType.MESH
f32 = jnp.float32
bf16 = jnp.bfloat16
CHUNK = 32
PARTS = 5


def kernel(
    R, C, V, L, M, K, ny, nx,
    cnt_hbm, dir_hbm, len_e_hbm, len_n_hbm, vm_hbm, amp_hbm, cell_hbm, wgt_hbm,
    res_hbm, inc_hbm, lz_hbm,
    tot_ref, res_ref, inc_ref, dir_ref, img_ref, lz_ref,
    cnt_ref, len_ref, vm_ref, amp_ref, cell_ref, wgt_ref,
    east_ref, north_ref, end_ref, start_ref, mix_ref, comb_ref, both_ref,
    lead_ref, pair_ref, hot_ref, near_ref, sel_ref, rest_ref,
    es_ref, er_ref, ns_ref, nr_ref, cs_ref, cr_ref, rs_ref, rr_ref,
    load_sem, e_ssem, e_rsem, n_ssem, n_rsem, c_ssem, c_rsem, r_ssem, r_rsem,
):
    N = R * C
    I = V * M
    row, col = lax.axis_index("row"), lax.axis_index("col")
    me = row * C + col
    barrier = pltpu.get_barrier_semaphore()

    def place(d):
        peer = lax.rem(me + d, N)
        return (lax.div(peer, C), lax.rem(peer, C))

    def greet(d, carry):
        pl.semaphore_signal(barrier, inc=1, device_id=place(d), device_id_type=MESH)
        return carry

    plane = L * ny
    lead_rows = M * ny
    rest = L - M
    firsts = [
        pltpu.make_async_copy(len_e_hbm, len_ref.at[0], load_sem.at[3]),
        pltpu.make_async_copy(len_n_hbm, len_ref.at[1], load_sem.at[4]),
    ]
    others = [
        pltpu.make_async_copy(cell_hbm, cell_ref, load_sem.at[5]),
        pltpu.make_async_copy(wgt_hbm, wgt_ref, load_sem.at[6]),
        pltpu.make_async_copy(vm_hbm, vm_ref, load_sem.at[7]),
        pltpu.make_async_copy(amp_hbm, amp_ref, load_sem.at[8]),
        pltpu.make_async_copy(cnt_hbm, cnt_ref, load_sem.at[9 + 2 * V]),
    ]
    leads = []
    for v in range(V):
        part = pl.ds(v * plane, lead_rows)
        leads.append(
            pltpu.make_async_copy(dir_hbm.at[part], dir_ref.at[part], load_sem.at[9 + v])
        )
        part = pl.ds(v * plane + lead_rows, plane - lead_rows)
        others.append(
            pltpu.make_async_copy(dir_hbm.at[part], dir_ref.at[part], load_sem.at[9 + V + v])
        )
    loads = [
        pltpu.make_async_copy(res_hbm, res_ref, load_sem.at[0]),
        pltpu.make_async_copy(lz_hbm, lz_ref, load_sem.at[1]),
        pltpu.make_async_copy(inc_hbm, inc_ref, load_sem.at[2]),
    ]
    lax.fori_loop(1, N, greet, 0)
    for load in firsts + leads + others + loads:
        load.start()
    for load in firsts:
        load.wait()

    lane = lax.broadcasted_iota(jnp.int32, (ny, nx), 1)
    sub = lax.broadcasted_iota(jnp.int32, (ny, nx), 0)
    east_at, north_at = lane.astype(f32), sub.astype(f32)
    inst_lane = lane & (I - 1)
    is_back = (lane & I) != 0
    is_late = lane >= 2 * I
    log_e = jnp.zeros((ny, nx), f32)
    log_n = jnp.zeros((ny, nx), f32)
    for i in range(I):
        v, m = i // M, i % M
        rows = slice(i * ny, (i + 1) * ny)
        e = -1.0 / (jnp.broadcast_to(len_ref[0, v : v + 1, m : m + 1], (ny, nx)) * float(nx))
        n = -1.0 / (jnp.broadcast_to(len_ref[1, v : v + 1, m : m + 1], (ny, nx)) * float(ny))
        log_e = jnp.where(inst_lane == i, e, log_e)
        log_n = jnp.where(inst_lane == i, n, log_n)
        east_ref[rows, :] = e
        north_ref[rows, :] = n
        end_ref[0, rows, :] = jnp.exp(e * (float(nx - 1) - east_at))
        start_ref[0, rows, :] = jnp.exp(e * east_at)
        end_ref[1, rows, :] = jnp.exp(n * (float(ny - 1) - north_at))
        start_ref[1, rows, :] = jnp.exp(n * north_at)
    corner_w = jnp.exp(log_n * jnp.where(is_late, north_at, float(ny - 1) - north_at))

    def every_sub(x):
        shift = ny // 2
        while shift:
            x = x + pltpu.roll(x, shift, 0)
            shift //= 2
        return x

    def split(x):
        high = x.astype(bf16)
        return high, (x - high.astype(f32)).astype(bf16)

    def scans(u, log_alpha, axis, size, at):
        power = jnp.exp(log_alpha)
        f, g = u, u
        shift = 1
        while shift < size:
            f = f + power * jnp.where(at >= shift, pltpu.roll(f, shift, axis), 0.0)
            g = g + power * jnp.where(at < size - shift, pltpu.roll(g, size - shift, axis), 0.0)
            power = power * power
            shift *= 2
        return f + g - u

    def smooth(x):
        return scans(x, log_lines, 1, nx, lax.broadcasted_iota(jnp.int32, (2 * I, nx), 1))

    def begin(u, inst):
        for i in range(I):
            rows = slice(i * ny, (i + 1) * ny)
            pair_ref[0, rows, :] = every_sub(u[rows] * end_ref[1, rows, :])
            pair_ref[1, rows, :] = every_sub(u[rows] * start_ref[1, rows, :])
        line = jnp.concatenate(
            [pair_ref[n, pl.ds(0, I, stride=ny), :] for n in range(2)], axis=0
        )
        ns_ref[inst] = smooth(line)
        moment = jnp.zeros((ny, nx), f32)
        for i in range(I):
            rows = slice(i * ny, (i + 1) * ny)
            e = jnp.sum(u[rows] * end_ref[0, rows, :], axis=1, keepdims=True)
            b = jnp.sum(u[rows] * start_ref[0, rows, :], axis=1, keepdims=True)
            moment = jnp.where(inst_lane == i, jnp.where(is_back, b, e), moment)
        es_ref[inst] = moment
        cs_ref[inst] = every_sub(moment * corner_w)[0:1]

    def launch(inst):
        for d in range(1, R):
            pltpu.make_async_remote_copy(
                src_ref=ns_ref.at[inst],
                dst_ref=nr_ref.at[inst, d],
                send_sem=n_ssem.at[inst, d],
                recv_sem=n_rsem.at[inst, d],
                device_id=(lax.rem(row + d, R), col),
                device_id_type=MESH,
            ).start()

        def go(over, carry):
            for along in range(C):
                pltpu.make_async_remote_copy(
                    src_ref=cs_ref.at[inst],
                    dst_ref=cr_ref.at[inst, over, pl.ds(along, 1)],
                    send_sem=c_ssem.at[inst, over],
                    recv_sem=c_rsem.at[inst, over],
                    device_id=(lax.rem(row + over, R), lax.rem(col + along, C)),
                    device_id_type=MESH,
                ).start()
            return carry

        lax.fori_loop(1, R, go, 0)
        for d in range(1, C):
            pltpu.make_async_remote_copy(
                src_ref=es_ref.at[inst],
                dst_ref=er_ref.at[inst, d],
                send_sem=e_ssem.at[inst, d],
                recv_sem=e_rsem.at[inst, d],
                device_id=(row, lax.rem(col + d, C)),
                device_id_type=MESH,
            ).start()

    def arrival(inst, kind, d):
        src, dst, send, recv = (
            (ns_ref.at[inst], nr_ref.at[inst, d], n_ssem, n_rsem),
            (es_ref.at[inst], er_ref.at[inst, d], e_ssem, e_rsem),
            (cr_ref.at[inst, d], cr_ref.at[inst, d], c_ssem, c_rsem),
        )[kind]
        return pltpu.make_async_remote_copy(
            src_ref=src, dst_ref=dst, send_sem=send.at[inst, d], recv_sem=recv.at[inst, d],
            device_id=(row, lax.rem(col + 1, C)), device_id_type=MESH,
        )

    def inside(u):
        u = u.reshape(I, ny, nx)
        u = scans(u, east_ref[...].reshape(I, ny, nx), 2, nx, lane[None])
        u = scans(u, north_ref[...].reshape(I, ny, nx), 1, ny, sub[None])
        lead_ref[...] = both_ref[0] * u.reshape(I * ny, nx)

    def weights(log_small, d, index, count, size):
        at = index.astype(f32)
        far = d > index
        source = jnp.where(far, index - d + count, index - d).astype(f32)
        step = d.astype(f32)
        left = jnp.where(
            far | (d == 0), 0.0, jnp.exp(log_small * (float(size) * jnp.maximum(step - 1.0, 0.0)))
        )
        right = jnp.where(
            far, jnp.exp(log_small * (float(size) * (float(count - 1) - step))), 0.0
        )
        edge = jnp.exp(
            log_small * (float(size) * (float(2 * count - 2) - at - source) + 1.0)
        )
        return left, right, edge

    def finish(inst):
        for d in range(1, C):
            arrival(inst, 1, d).wait_recv()
        ahead = jnp.zeros((ny, nx), f32)
        echo = col_edge[0:1] * es_ref[inst]
        for d in range(1, C):
            ahead += col_main[d : d + 1] * er_ref[inst, d]
            echo += col_edge[d : d + 1] * er_ref[inst, d]
        lines = ahead - pltpu.roll(echo, I, 1)
        settled = scans(lines, log_n, 0, ny, sub)
        for d in range(1, R):
            arrival(inst, 2, d).wait_recv()
        first = corner_w * lines
        ahead = row_main[0] * first
        echo = row_edge[0] * first
        for d in range(1, R):
            got = cr_ref[inst, d]
            got = col_main * got - pltpu.roll(col_edge * got, I, 1)
            got = jnp.sum(got.reshape(C // ny, ny, nx), axis=0)
            ahead += row_main[d] * got
            echo += row_edge[d] * got
        corner = every_sub(ahead - pltpu.roll(echo, 2 * I, 1))
        settled = lane_scale * (
            settled + lane_low * corner + lane_high * pltpu.roll(corner, 2 * I, 1)
        )
        for d in range(1, R):
            arrival(inst, 0, d).wait_recv()
        left, right, edge = north_w[0]
        p = jnp.zeros((I, nx), f32)
        q = -edge * ns_ref[inst, 0:I]
        for d in range(1, R):
            left, right, edge = north_w[d]
            p += left * nr_ref[inst, d, 0:I]
            q += right * nr_ref[inst, d, I : 2 * I] - edge * nr_ref[inst, d, 0:I]
        line = jnp.concatenate([p, q], axis=0)
        comb_ref[...] = line
        for i in range(I):
            rows = slice(i * ny, (i + 1) * ny)
            x = jnp.broadcast_to(settled[:, i : i + 1], (ny, nx))
            y = jnp.broadcast_to(settled[:, I + i : I + i + 1], (ny, nx))
            p = jnp.broadcast_to(comb_ref[i : i + 1, :], (ny, nx))
            q = jnp.broadcast_to(comb_ref[I + i : I + i + 1, :], (ny, nx))
            lead_ref[rows, :] += (
                both_ref[1, rows, :] * p + both_ref[2, rows, :] * q
                + both_ref[3, rows, :] * x + both_ref[4, rows, :] * y
            )

    log_lines = east_ref[pl.ds(0, I, stride=ny), :]
    log_lines = jnp.concatenate([log_lines, log_lines], axis=0)
    for load in leads:
        load.wait()
    u = jnp.concatenate([dir_ref[v * plane : v * plane + M * ny, :] for v in range(V)], axis=0)
    begin(u, 0)
    pl.semaphore_wait(barrier, N - 1)
    launch(0)

    alpha_e, alpha_n = jnp.exp(log_e), jnp.exp(log_n)
    lane_scale = jnp.sqrt(
        ((1.0 - alpha_e) / (1.0 + alpha_e)) * ((1.0 - alpha_n) / (1.0 + alpha_n))
    )
    lane_low = jnp.exp(log_n * (north_at + 1.0))
    lane_high = jnp.exp(log_n * (float(ny) - north_at))
    over = lax.broadcasted_iota(jnp.int32, (C, nx), 0)
    odd = (lax.broadcasted_iota(jnp.int32, (C, nx), 1) & I) != 0
    low, high, edge = weights(jnp.broadcast_to(log_e[0:1], (C, nx)), over, col, C, nx)
    col_main = jnp.where(odd, high, low)
    col_edge = jnp.where(odd, 0.0, edge)
    row_main, row_edge, north_w = [], [], []
    log_rows = north_ref[pl.ds(0, I, stride=ny), :]
    for d in range(R):
        step = jnp.full((ny, nx), d, jnp.int32)
        low, high, edge = weights(log_n, step, row, R, ny)
        row_main.append(jnp.where(is_late, high, low))
        row_edge.append(jnp.where(is_late, 0.0, edge))
        north_w.append(weights(log_rows, jnp.full((I, nx), d, jnp.int32), row, R, ny))
    for i in range(I):
        rows = slice(i * ny, (i + 1) * ny)
        a, b = jnp.exp(east_ref[rows, :]), jnp.exp(north_ref[rows, :])
        scale = jnp.sqrt(((1.0 - a) / (1.0 + a)) * ((1.0 - b) / (1.0 + b)))
        both_ref[0, rows, :] = scale
        both_ref[1, rows, :] = scale * b * start_ref[1, rows, :]
        both_ref[2, rows, :] = scale * b * end_ref[1, rows, :]
        both_ref[3, rows, :] = a * start_ref[0, rows, :]
        both_ref[4, rows, :] = a * end_ref[0, rows, :]
    inside(u)
    for load in others:
        load.wait()

    pad = (L + 15) // 16 * 16
    cell = cell_ref[...]
    slots = cell.shape[1]
    level = lax.shift_right_logical(cell, (ny * nx).bit_length() - 1)
    spot = cell & (ny * nx - 1)
    spot_x = spot & (nx - 1)
    spot_y = lax.shift_right_logical(spot, nx.bit_length() - 1)
    hot_ref[...] = jnp.where(
        lax.broadcasted_iota(jnp.int32, (ny * nx, slots), 0) == spot, 1.0, 0.0
    ).astype(bf16)
    near = jnp.where(
        lax.broadcasted_iota(jnp.int32, (nx, slots), 0) == spot_x, 1.0, 0.0
    ).astype(bf16)
    near_ref[0:nx] = near
    near_ref[nx : 2 * nx] = near
    live = lax.broadcasted_iota(jnp.int32, (1, slots), 1) < cnt_ref[...]
    weight = jnp.where(live, wgt_ref[...], 0.0)
    mix_ref[...] = jnp.zeros_like(mix_ref)
    at = lax.broadcasted_iota(jnp.int32, (pad, slots), 0)
    here = lax.broadcasted_iota(jnp.int32, (ny, slots), 0) == spot_y
    hold = pad - M
    for v in range(V):
        mix_ref[v, 0:L, 0:L] = vm_ref[:, v, :] * amp_ref[v : v + 1, :]
        left = mix_ref[v].T[0:pad, 0:pad]
        parts = []
        for _ in range(3):
            part = left.astype(bf16)
            parts.append(part)
            left = left - part.astype(f32)
        hit = jnp.where((at + v * L == level) & (at < L), 1.0, 0.0).astype(bf16)
        chosen = jnp.dot(jnp.concatenate(parts, axis=0), hit, preferred_element_type=f32)
        chosen = chosen[0:pad] + chosen[pad : 2 * pad] + chosen[2 * pad : 3 * pad]
        rest_ref[v * hold : (v + 1) * hold] = chosen[M:pad]
        for m in range(M):
            i = v * M + m
            sel_ref[i * ny : (i + 1) * ny] = jnp.where(
                here, jnp.broadcast_to(chosen[m : m + 1], (ny, slots)), 0.0
            )

    spare = jnp.zeros((hold - rest, nx), f32)
    held = jnp.concatenate(
        [
            jnp.concatenate(
                [
                    x
                    for v in range(V)
                    for x in (
                        dir_ref[pl.ds(v * plane + lead_rows + y, rest, stride=ny), :], spare
                    )
                ],
                axis=0,
            )
            for y in range(ny)
        ],
        axis=1,
    )
    seen = jnp.dot(
        jnp.concatenate(split(held), axis=0), hot_ref[...], preferred_element_type=f32
    )
    seen = seen[0 : V * hold] + seen[V * hold :]
    beside = jnp.sum(seen * rest_ref[...], axis=0, keepdims=True)

    def products(s, image):
        r = res_ref[s * half : (s + 1) * half, :]
        extra = list(split(r)) + image
        wide, tall = [], []
        for n in range(half // 16):
            rows = slice(s * half + n * 16, s * half + (n + 1) * 16)
            block = lz_ref[:, rows, :].reshape(K * 16, nx)
            wide.append(block)
            part = slice(n * 16, (n + 1) * 16)
            tall.append(jnp.concatenate([block] + [x[part] for x in extra], axis=0))
        table = lax.dot_general(
            jnp.concatenate(tall, axis=1), jnp.concatenate(wide, axis=1),
            (((1,), (1,)), ((), ())), preferred_element_type=f32,
        )
        return table, fold(r * r)

    def fold(x):
        return jnp.sum(x.reshape(x.shape[0] // 8, 8, nx), axis=0)

    half = V // 2 * plane
    loads[0].wait()
    loads[1].wait()
    table_a, square = products(0, [])

    finish(0)

    high, low = split(lead_ref[...])
    seen = jnp.dot(
        jnp.concatenate([high, low], axis=1), near_ref[...], preferred_element_type=f32
    )
    grid = jnp.sum(seen * sel_ref[...], axis=0, keepdims=True) + beside
    weighted = weight * grid
    high, low = split(sel_ref[...] * weighted)
    across = (((1,), (1,)), ((), ()))
    u = lax.dot_general(high, near_ref[0:nx], across, preferred_element_type=f32)
    u += lax.dot_general(low, near_ref[0:nx], across, preferred_element_type=f32)
    begin(u, 1)
    launch(1)

    inside(u)
    back = lax.dot_general(
        jnp.concatenate(split(rest_ref[...] * weighted), axis=0), hot_ref[...], across,
        preferred_element_type=f32,
    )
    back = back[0 : V * hold] + back[V * hold :]
    for v in range(V):
        for y in range(ny):
            img_ref[pl.ds(v * plane + lead_rows + y, rest, stride=ny), :] = back[
                v * hold : v * hold + rest, y * nx : (y + 1) * nx
            ]

    zero = jnp.zeros((8, nx), f32)

    def image_dots(base, mine, carry):
        rows = pl.ds(base, CHUNK)
        d = dir_ref[rows, :]
        image = d + mine
        img_ref[rows, :] = image
        r = res_ref[rows, :]
        out = [
            carry[0] + fold(r * image), carry[1] + fold(image * image), carry[2] + fold(d * image)
        ]
        for k in range(K):
            out.append(carry[k + 3] + fold(image * lz_ref[k, rows, :].astype(f32)))
        return tuple(out)

    turns = (plane - lead_rows) // CHUNK

    def rest_dots(s, carry):
        base = lax.div(s, turns) * plane + lead_rows + lax.rem(s, turns) * CHUNK
        base = pl.multiple_of(base, CHUNK)
        return image_dots(base, img_ref[pl.ds(base, CHUNK), :], carry)

    img_dots = lax.fori_loop(0, V // 2 * turns, rest_dots, (zero,) * (K + 3), unroll=2)
    few, images = list(img_dots[:3]), []
    for v in range(V // 2, V):
        rows = slice(v * plane + lead_rows, (v + 1) * plane)
        d, r = dir_ref[rows, :], res_ref[rows, :]
        image = d + img_ref[rows, :]
        img_ref[rows, :] = image
        few = [x + fold(y * image) for x, y in zip(few, (r, image, d))]
        images += [jnp.zeros((lead_rows, nx), f32), image]
    img_dots = tuple(few) + img_dots[3:]
    table, more = products(1, list(split(jnp.concatenate(images, axis=0))))
    square += more
    at_row = lax.broadcasted_iota(jnp.int32, table.shape, 0)
    at_col = lax.broadcasted_iota(jnp.int32, table.shape, 1)
    table += jnp.concatenate([table_a, jnp.zeros((32, K * 16), f32)], axis=0)
    kept = jnp.where((at_row & 15) == (at_col & 15), table, 0.0)
    kept = jnp.sum(kept.reshape(K + 4, 16, K * 16), axis=1)
    kept = jnp.concatenate(
        [
            kept[0:K], kept[K : K + 1] + kept[K + 1 : K + 2],
            kept[K + 2 : K + 3] + kept[K + 3 : K + 4], jnp.zeros((14 - K, K * 16), f32),
        ],
        axis=0,
    )
    which_k = lax.shift_right_logical(lax.broadcasted_iota(jnp.int32, (K * 16, nx), 0), 4)
    in_lane = lax.broadcasted_iota(jnp.int32, (K * 16, nx), 1)
    pick = jnp.zeros((K * 16, nx), f32)
    for j in range(K + 2):
        pick = jnp.where(in_lane == which_k + j * K, 1.0, pick)
    spread_out = jnp.dot(
        kept, pick, preferred_element_type=f32, precision=lax.Precision.HIGHEST
    )
    g_lane = lax.broadcasted_iota(jnp.int32, (16, nx), 1)
    g_row = lax.broadcasted_iota(jnp.int32, (16, nx), 0)
    own_row = (g_lane >= g_row * K) & (g_lane < (g_row + 1) * K) & (g_row < K + 2)
    gram_row = jnp.sum(jnp.where(own_row, spread_out, 0.0), axis=0, keepdims=True)
    finish(1)
    short = lead_rows // CHUNK

    def lead_dots(s, carry):
        base = pl.multiple_of(lax.div(s, short) * plane + lax.rem(s, short) * CHUNK, CHUNK)
        mine = lead_ref[pl.ds(pl.multiple_of(s * CHUNK, CHUNK), CHUNK), :]
        return image_dots(base, mine, carry)

    img_dots = lax.fori_loop(0, V * short, lead_dots, img_dots, unroll=2)

    def reduce_copy(over, along):
        return pltpu.make_async_remote_copy(
            src_ref=rs_ref,
            dst_ref=rr_ref.at[pl.ds(over * C + along, 1)],
            send_sem=r_ssem.at[0],
            recv_sem=r_rsem.at[0],
            device_id=(lax.rem(row + over, R), lax.rem(col + along, C)),
            device_id_type=MESH,
        )

    sums = list(img_dots[3:]) + [square] + list(img_dots[:3])
    rows = [jnp.sum(x, axis=0, keepdims=True) for x in sums]
    rows.append(jnp.zeros((32 - len(sums), nx), f32))
    packed = jnp.sum(jnp.concatenate(rows, axis=0).T, axis=0, keepdims=True)
    packed = jnp.concatenate([packed, jnp.zeros((1, nx - 32), f32)], axis=1)
    packed = pltpu.roll(packed, K * K + K, 1)
    rs_ref[...] = packed + gram_row

    def go(over, carry):
        for along in range(C):
            reduce_copy(over, along).start()
        return carry

    lax.fori_loop(1, R, go, 0)
    for along in range(1, C):
        reduce_copy(0, along).start()
    loads[2].wait()
    for inst in range(2):
        for d in range(1, R):
            arrival(inst, 0, d).wait_send()
            arrival(inst, 2, d).wait_send()
        for d in range(1, C):
            arrival(inst, 1, d).wait_send()
    every = pltpu.make_async_remote_copy(
        src_ref=rr_ref.at[pl.ds(1, N - 1)],
        dst_ref=rr_ref.at[pl.ds(1, N - 1)],
        send_sem=r_ssem.at[0],
        recv_sem=r_rsem.at[0],
        device_id=(row, lax.rem(col + 1, C)),
        device_id_type=MESH,
    )
    rr_ref[pl.ds(0, 1)] = rs_ref[...]
    every.wait_recv()
    tot_ref[...] = every_sub(jnp.sum(rr_ref[...].reshape(N // 8, 8, nx), axis=0))
    every.wait_send()


def update(
    K, total_cells, parts,
    tot_ref, res_ref, inc_ref, dir_ref, img_ref, lz_ref, oinc_hbm, ores_hbm, odir_hbm,
    oinc_ref, ores_ref, odir_ref, sem,
):
    flat, nx = res_ref.shape
    totals = tot_ref[0:1, :]
    lane = lax.broadcasted_iota(jnp.int32, (1, nx), 1)

    def total(n):
        return totals[:, n : n + 1]

    first = K * K
    rr, ri, ii, di = (total(first + 2 * K + n) for n in range(4))
    step_size = rr / di
    moments = [total(first + k) - step_size * total(first + K + k) for k in range(K)]
    left, right = jnp.zeros((1, nx), f32), jnp.zeros((1, nx), f32)
    for j in range(K):
        left = jnp.where((lane >= j * K) & (lane < (j + 1) * K), moments[j], left)
    single = jnp.zeros((1, nx), f32)
    for k in range(K):
        hit = lane == k
        for j in range(1, K):
            hit = hit | (lane == j * K + k)
        right = jnp.where(hit, moments[k], right)
        single = jnp.where(lane == k, moments[k], single)
    squares = jnp.sum(left * right * totals, axis=1, keepdims=True)
    crossed = jnp.sum(single * single, axis=1, keepdims=True)
    moved_norm = rr + step_size * (step_size * ii - 2.0 * ri)
    norm_new = moved_norm + (squares / total_cells - 2.0 * crossed) / total_cells
    coefficient = [jnp.broadcast_to(x / total_cells, (CHUNK, nx)) for x in moments]
    step_wide = jnp.broadcast_to(step_size, (CHUNK, nx))
    ratio = jnp.broadcast_to(norm_new / rr, (CHUNK, nx))
    oinc_ref[...] = inc_ref[...] + jnp.broadcast_to(step_size, (flat, nx)) * dir_ref[...]
    copies = [pltpu.make_async_copy(oinc_ref, oinc_hbm, sem.at[0, 2])]
    copies[0].start()
    size = flat // parts
    for part in range(parts):

        def advance(s, carry):
            rows = pl.ds(pl.multiple_of(part * size + s * CHUNK, CHUNK), CHUNK)
            new = res_ref[rows, :] - step_wide * img_ref[rows, :]
            for k in range(K):
                new = new - coefficient[k] * lz_ref[k, rows, :].astype(f32)
            ores_ref[rows, :] = new
            odir_ref[rows, :] = new + ratio * dir_ref[rows, :]
            return carry

        lax.fori_loop(0, size // CHUNK, advance, 0, unroll=4)
        rows = pl.ds(part * size, size)
        for n, (src, dst) in enumerate(((ores_ref, ores_hbm), (odir_ref, odir_hbm))):
            copies.append(pltpu.make_async_copy(src.at[rows], dst.at[rows], sem.at[part, n]))
            copies[-1].start()
    for copy in copies:
        copy.wait()


def local(
    R, C,
    increment, residual, direction, lanczos, vertical_modes, amplitude,
    length_east, length_north, observed_cell, observed_weight, observed_count,
):
    V, L, ny, nx = direction.shape
    M = length_east.shape[1]
    K = lanczos.shape[0]
    I = V * M
    N = R * C
    flat = V * L * ny
    slots = observed_cell.shape[0]
    pad = (L + 15) // 16 * 16
    hbm = pl.BlockSpec(memory_space=pltpu.HBM)
    near = pl.BlockSpec(memory_space=pltpu.VMEM)
    field = pltpu.VMEM((flat, nx), f32)
    lead = pltpu.VMEM((I * ny, nx), f32)
    held = pl.pallas_call(
        functools.partial(kernel, R, C, V, L, M, K, ny, nx),
        out_shape=(pltpu.VMEM((8, nx), f32),) + (field,) * 4 + (pltpu.VMEM((K, flat, nx), bf16),),
        in_specs=[hbm] * 11,
        out_specs=(near,) * 6,
        scratch_shapes=[
            pltpu.VMEM((1, 1), jnp.int32),
            pltpu.VMEM((2, V, M), f32), pltpu.VMEM((L, V, L), f32),
            pltpu.VMEM((V, L), f32), pltpu.VMEM((1, slots), jnp.int32), pltpu.VMEM((1, slots), f32),
            lead, lead, pltpu.VMEM((2, I * ny, nx), f32), pltpu.VMEM((2, I * ny, nx), f32),
            pltpu.VMEM((V, 2 * pad, 2 * pad), f32),
            pltpu.VMEM((2 * I, nx), f32), pltpu.VMEM((5, I * ny, nx), f32),
            lead, pltpu.VMEM((2, I * ny, nx), f32),
            pltpu.VMEM((ny * nx, slots), bf16), pltpu.VMEM((2 * nx, slots), bf16),
            pltpu.VMEM((I * ny, slots), f32), pltpu.VMEM((V * (pad - M), slots), f32),
            pltpu.VMEM((2, ny, nx), f32), pltpu.VMEM((2, C, ny, nx), f32),
            pltpu.VMEM((2, 2 * I, nx), f32), pltpu.VMEM((2, R, 2 * I, nx), f32),
            pltpu.VMEM((2, 1, nx), f32), pltpu.VMEM((2, R, C, nx), f32),
            pltpu.VMEM((1, nx), f32), pltpu.VMEM((N, nx), f32),
            pltpu.SemaphoreType.DMA((10 + 2 * V,)),
            pltpu.SemaphoreType.DMA((2, C)), pltpu.SemaphoreType.DMA((2, C)),
            pltpu.SemaphoreType.DMA((2, R)), pltpu.SemaphoreType.DMA((2, R)),
            pltpu.SemaphoreType.DMA((2, R)), pltpu.SemaphoreType.DMA((2, R)),
            pltpu.SemaphoreType.DMA((1,)), pltpu.SemaphoreType.DMA((1,)),
        ],
        compiler_params=pltpu.CompilerParams(
            collective_id=0, has_side_effects=True, vmem_limit_bytes=54 * 2**20
        ),
    )(
        observed_count.reshape(1, 1), direction.reshape(flat, nx), length_east, length_north,
        jnp.transpose(vertical_modes, (1, 0, 2)), amplitude,
        observed_cell.reshape(1, slots), observed_weight.reshape(1, slots),
        residual.reshape(flat, nx), increment.reshape(flat, nx), lanczos.reshape(K, flat, nx),
    )
    done = pl.pallas_call(
        functools.partial(update, K, float(flat * nx * N), PARTS),
        out_shape=(jax.ShapeDtypeStruct((flat, nx), f32),) * 3,
        in_specs=[near] * 6,
        out_specs=(hbm,) * 3,
        scratch_shapes=[
            pltpu.VMEM((flat, nx), f32), pltpu.VMEM((flat, nx), f32), pltpu.VMEM((flat, nx), f32),
            pltpu.SemaphoreType.DMA((PARTS, 3)),
        ],
        compiler_params=pltpu.CompilerParams(vmem_limit_bytes=16 * 2**20),
    )(*held)
    return tuple(x.reshape(V, L, ny, nx) for x in done)


def solution(mesh):
    field = P(None, None, "row", "col")
    tile = P(("row", "col"))
    in_specs = (
        field, field, field, P(None, None, None, "row", "col"),
        P(), P(), P(), P(), tile, tile, tile,
    )
    return jax.shard_map(
        functools.partial(local, mesh.shape["row"], mesh.shape["col"]),
        mesh=mesh, in_specs=in_specs, out_specs=(field,) * 3, check_vma=False,
    )
```
